32 devices in a mesh: dp: 8 (over z, y), mp: 4 (over x, core).
Axes of the slice: x: 2, y: 2, z: 4, core: 2. Of those that a mesh axis runs over, the one named last changes fastest.
Arguments:
- points_in: bfloat16 [8192, 96], P(('dp', 'mp')), may hold values from -1 to 1
- view_enc: bfloat16 [128, 27], P(('dp', 'mp')), may hold values from -1 to 1
- deltas: float32 [128, 64], P(('dp', 'mp')), may hold values from 0.01 to 0.1
- counts: int32 [128], P(('dp', 'mp')), may hold values from 16 to 64, as said below
- w_first: bfloat16 [96, 1024], P(None, 'mp'), may hold values from -1 to 1
- w_col: bfloat16 [2, 1024, 1024], P(None, None, 'mp'), may hold values from -0.25 to 0.25
- w_skip: bfloat16 [1120, 1024], P(None, 'mp'), may hold values from -0.25 to 0.25
- w_row: bfloat16 [4, 1024, 1024], P(None, 'mp'), may hold values from -0.25 to 0.25
- b_col: bfloat16 [4, 1024], P(None, 'mp'), may hold values from -1.5 to 1.5
- b_row: bfloat16 [4, 1024], replicated, may hold values from -1.5 to 1.5
- w_density: bfloat16 [1024], replicated, may hold values from -0.25 to 0.25
- w_bottle: bfloat16 [1024, 256], replicated, may hold values from -0.25 to 0.25
- b_bottle: bfloat16 [256], replicated, may hold values from -1.5 to 1.5
- w_view: bfloat16 [283, 128], replicated, may hold values from -0.5 to 0.5
- b_view: bfloat16 [128], replicated, may hold values from -1.5 to 1.5
- w_rgb: bfloat16 [128, 3], replicated, may hold values from -0.75 to 0.75
- b_rgb: bfloat16 [3], replicated, may hold values from -1.5 to 1.5
- prop_in: bfloat16 [8192, 96], P(('dp', 'mp')), may hold values from -1 to 1
- prop_deltas: float32 [128, 64], P(('dp', 'mp')), may hold values from 0.01 to 0.1
- bin_bounds: int32 [2, 128, 64], P(None, ('dp', 'mp')), may hold values from 0 to 64, as said below
- wp_first: bfloat16 [96, 256], replicated, may hold values from -1 to 1
- wp_rest: bfloat16 [3, 256, 256], replicated, may hold values from -0.5 to 0.5
- b_prop: bfloat16 [4, 256], replicated, may hold values from -1.5 to 1.5
- wp_density: bfloat16 [256], replicated, may hold values from -0.5 to 0.5
- d_colour: float32 [3, 128], P(None, ('dp', 'mp')), may hold values from -6 to 6
Outputs:
- colour: float32 [3, 128], P(None, ('dp', 'mp'))
- grad_points: float32 [8192, 96], P(('dp', 'mp'))
- grad_view: float32 [128, 27], P(('dp', 'mp'))
- grad_prop_in: float32 [8192, 96], P(('dp', 'mp'))
- grad_w_first: float32 [96, 1024], P(None, 'mp')
- grad_w_col: float32 [2, 1024, 1024], P(None, None, 'mp')
- grad_w_skip: float32 [1120, 1024], P(None, 'mp')
- grad_w_row: float32 [4, 1024, 1024], P(None, 'mp')
- grad_b_col: float32 [4, 1024], P(None, 'mp')
- grad_b_row: float32 [4, 1024], replicated
- grad_w_density: float32 [1024], replicated
- grad_w_bottle: float32 [1024, 256], replicated
- grad_b_bottle: float32 [256], replicated
- grad_w_view: float32 [283, 128], replicated
- grad_b_view: float32 [128], replicated
- grad_w_rgb: float32 [128, 3], replicated
- grad_b_rgb: float32 [3], replicated
- grad_wp_first: float32 [96, 256], replicated
- grad_wp_rest: float32 [3, 256, 256], replicated
- grad_b_prop: float32 [4, 256], replicated
- grad_wp_density: float32 [256], replicated
The draws below stay inside these ranges and needn't reach their ends.
Inputs may be any that keep to these rules, and one draw needn't show every extreme that they name: Samples of a ray at index counts or higher are padding; one ray of the batch has all 64 live and one has a quarter of 64. `bin_bounds`: row 0 holds the first proposal interval covered by a sample interval, row 1 one past its last, always above row 0; every ray's first sample interval starts at interval 0 and its last ends at 64.
All inputs are finite; a program needn't handle non-finite values.
Results may differ from the reference program's by a relative error of at most 0.023.
Values may be sent and summed in bfloat16 or wider, within the bound.
No kernel may reach another device: no remote copies, remote signals or barrier semaphores. Data moves between devices by JAX's collectives and lax.ppermute only.
A program may use at most 128 MiB of HBM per device.

```python
import math
import jax
import jax.numpy as jnp
from jax import lax

FEAT = 1024
IPE = 96
BOTTLE = 256
VENC = 27
VIEWW = 128
PWIDTH = 256
SAMPLES = 64
PSAMP = 64
RAYS = 128
POINTS = 8192
PPOINTS = 8192
N_DP = 8


def draw_counts(key, part):
    lengths = jax.random.randint(jax.random.fold_in(key, 101), (RAYS,), SAMPLES // 4, SAMPLES + 1)
    full_ray = jax.random.randint(jax.random.fold_in(key, 102), (), 0, RAYS)
    short_ray = (full_ray + jax.random.randint(jax.random.fold_in(key, 103), (), 1, RAYS)) % RAYS
    places = jnp.arange(RAYS)
    lengths = jnp.where(places == full_ray, SAMPLES, lengths)
    lengths = jnp.where(places == short_ray, SAMPLES // 4, lengths)
    return lengths.astype(jnp.int32)


def draw_bin_bounds(key, part):
    sample = jnp.arange(SAMPLES)[None, :]
    centre = sample * PSAMP // SAMPLES
    jitter = jax.random.randint(jax.random.fold_in(key, 201), (RAYS, SAMPLES), -2, 3)
    lower = jnp.clip(centre + jitter, 0, PSAMP - 1)
    lower = jnp.where(sample == 0, 0, lower)
    extent = jax.random.randint(jax.random.fold_in(key, 202), (RAYS, SAMPLES), 1, 5)
    upper = jnp.minimum(lower + extent, PSAMP)
    upper = jnp.where(sample == SAMPLES - 1, PSAMP, upper)
    return jnp.stack([lower, upper]).astype(jnp.int32)


def block_scale(stream_key, shape, cuts, least, largest):
    loudness = 1.0
    for position, blocks in cuts:
        steps = jax.random.uniform(jax.random.fold_in(jax.random.fold_in(stream_key, 6), position), (blocks,), jnp.float32, least / len(cuts), largest / len(cuts))
        loudness = loudness * jnp.repeat(jnp.exp(steps), shape[position] // blocks).reshape((-1,) + (1,) * (len(shape) - 1 - position))
    return loudness


def normal_values(stream_key, dims, spread, most, cuts=(), held_as=jnp.bfloat16):
    values = jax.random.normal(stream_key, dims, jnp.float32) * spread
    if len(cuts) > 0:
        values = block_scale(stream_key, dims, cuts, -0.22, 0.18) * values
    return jnp.clip(values, min=-most, max=most).astype(held_as)


def setup_inputs(seed: int = 0) -> dict:
    arg_keys = jax.random.split(jax.random.key(seed), 26)
    return {
        "points_in": jnp.clip(jax.random.uniform(arg_keys[0], (POINTS, IPE), jnp.float32, -1.0, 1.0) * block_scale(arg_keys[0], (POINTS, IPE), ((0, 32),), -0.4, 0.0), -1.0, 1.0).astype(jnp.bfloat16),
        "view_enc": jnp.clip(jax.random.uniform(arg_keys[1], (RAYS, VENC), jnp.float32, -1.0, 1.0) * block_scale(arg_keys[1], (RAYS, VENC), ((0, 32),), -0.4, 0.0), -1.0, 1.0).astype(jnp.bfloat16),
        "deltas": jnp.clip(jnp.exp(math.log(0.1) - 2.3025851 * jax.random.uniform(arg_keys[2], (RAYS, SAMPLES), jnp.float32) ** block_scale(arg_keys[2], (RAYS, SAMPLES), ((0, 32),), -0.2, 0.2)), 0.01, 0.1),
        "counts": draw_counts(jax.random.fold_in(arg_keys[25], 71), 0),
        "w_first": normal_values(arg_keys[4], (IPE, FEAT), (IPE // 3) ** -0.5, 1.0, ((1, 4),)),
        "w_col": normal_values(arg_keys[5], (2, FEAT, FEAT), (FEAT // 2) ** -0.5, 0.25, ((2, 4),)),
        "w_skip": normal_values(arg_keys[6], (FEAT + IPE, FEAT), (FEAT // 2) ** -0.5, 0.25, ((1, 4),)),
        "w_row": normal_values(arg_keys[7], (4, FEAT, FEAT), (FEAT // 2) ** -0.5, 0.25, ((1, 4),)),
        "b_col": normal_values(arg_keys[8], (4, FEAT), 0.3, 1.5, ((1, 4),)),
        "b_row": normal_values(arg_keys[9], (4, FEAT), 0.3, 1.5),
        "w_density": normal_values(arg_keys[10], (FEAT,), (FEAT // 2) ** -0.5, 0.25),
        "w_bottle": normal_values(arg_keys[11], (FEAT, BOTTLE), (FEAT // 2) ** -0.5, 0.25),
        "b_bottle": normal_values(arg_keys[12], (BOTTLE,), 0.3, 1.5),
        "w_view": normal_values(arg_keys[13], (BOTTLE + VENC, VIEWW), ((BOTTLE + VENC) // 2) ** -0.5, 0.5),
        "b_view": normal_values(arg_keys[14], (VIEWW,), 0.3, 1.5),
        "w_rgb": normal_values(arg_keys[15], (VIEWW, 3), (VIEWW // 2) ** -0.5, 0.75),
        "b_rgb": normal_values(arg_keys[16], (3,), 0.3, 1.5),
        "prop_in": jnp.clip(jax.random.uniform(arg_keys[17], (PPOINTS, IPE), jnp.float32, -1.0, 1.0) * block_scale(arg_keys[17], (PPOINTS, IPE), ((0, 32),), -0.4, 0.0), -1.0, 1.0).astype(jnp.bfloat16),
        "prop_deltas": jnp.clip(jnp.exp(math.log(0.1) - 2.3025851 * jax.random.uniform(arg_keys[18], (RAYS, PSAMP), jnp.float32) ** block_scale(arg_keys[18], (RAYS, PSAMP), ((0, 32),), -0.2, 0.2)), 0.01, 0.1),
        "bin_bounds": draw_bin_bounds(jax.random.fold_in(arg_keys[25], 71), 0),
        "wp_first": normal_values(arg_keys[20], (IPE, PWIDTH), (IPE // 3) ** -0.5, 1.0),
        "wp_rest": normal_values(arg_keys[21], (3, PWIDTH, PWIDTH), (PWIDTH // 2) ** -0.5, 0.5),
        "b_prop": normal_values(arg_keys[22], (4, PWIDTH), 0.3, 1.5),
        "wp_density": normal_values(arg_keys[23], (PWIDTH,), (PWIDTH // 2) ** -0.5, 0.5),
        "d_colour": normal_values(arg_keys[24], (3, RAYS), 1.0, 6.0, ((1, 32),), jnp.float32),
    }


HIGHEST = lax.Precision.HIGHEST
epsilon = 0.0001

@jax.custom_vjp
def low(v):
    return lax.optimization_barrier(v.astype(jnp.bfloat16)).astype(jnp.float32)

@jax.custom_vjp
def low_back(v):
    return v

def low_keep(v):
    return (low(v), None)

def low_pass(kept, grad):
    return (grad,)

def back_keep(v):
    return (v, None)

def back_low(kept, grad):
    return (low(grad),)
low.defvjp(low_keep, low_pass)
low_back.defvjp(back_keep, back_low)

def affine(left, weight, bias):
    return jnp.dot(left, weight, precision=HIGHEST) + bias

def hidden(pre):
    return low(jax.nn.silu(pre))

def composite(depth):
    before = jnp.cumsum(depth, axis=1) - depth
    return -jnp.expm1(-depth) * jnp.exp(-before)

def nerf_forward(trunk, heads, point_rows, view_rows_in, block_deltas, block_counts):
    w_first, w_col, w_skip, w_row, b_col, b_row = trunk
    col_weights = (w_first, w_col[0], w_skip, w_col[1])
    current = point_rows
    for number in range(4):
        if number == 2:
            current = jnp.concatenate([current, point_rows], 1)
        col_act = hidden(low_back(affine(current, col_weights[number], b_col[number])))
        current = hidden(low_back(affine(col_act, w_row[number], b_row[number])))
    w_density, w_bottle, b_bottle, w_view, b_view, w_rgb, b_rgb = heads
    raw = low_back(jnp.dot(current, w_density, precision=HIGHEST))
    sigma = jax.nn.softplus(raw - 1.0)
    bottle = low(low_back(affine(current, w_bottle, b_bottle)))
    rays_here = block_counts.shape[0]
    venc_width = view_rows_in.shape[1]
    view_rows = jnp.broadcast_to(view_rows_in[:, None, :], (rays_here, SAMPLES, venc_width)).reshape(rays_here * SAMPLES, venc_width)
    view_act = hidden(low_back(affine(jnp.concatenate([bottle, view_rows], 1), w_view, b_view)))
    rgb_pre = low_back(jnp.einsum('kc,qk->cq', w_rgb, view_act, precision=HIGHEST) + b_rgb[:, None])
    rgb = jax.nn.sigmoid(rgb_pre).reshape(3, rays_here, SAMPLES)
    live = lax.broadcasted_iota(jnp.int32, block_deltas.shape, 1) < block_counts[:, None]
    depth = jnp.where(live, sigma.reshape(rays_here, SAMPLES) * block_deltas, 0.0)
    weights = composite(depth)
    colour = jnp.einsum('rs,crs->cr', weights, rgb, precision=HIGHEST)
    return (colour, weights)

def prop_forward(prop, prop_rows, block_prop_deltas, bounds, weights):
    wp_first, wp_rest, b_prop, wp_density = prop
    layers = (wp_first, wp_rest[0], wp_rest[1], wp_rest[2])
    current = prop_rows
    for number in range(4):
        current = hidden(low_back(affine(current, layers[number], b_prop[number])))
    raw = low_back(jnp.dot(current, wp_density, precision=HIGHEST))
    rays_here = block_prop_deltas.shape[0]
    prop_weights = composite(jax.nn.softplus(raw - 1.0).reshape(rays_here, PSAMP) * block_prop_deltas)
    bins = lax.broadcasted_iota(jnp.int32, (1, 1, PSAMP), 2)
    inside = ((bins >= bounds[0][:, :, None]) & (bins < bounds[1][:, :, None])).astype(jnp.float32)
    bound = jnp.einsum('rij,rj->ri', inside, prop_weights, precision=HIGHEST)
    excess = jnp.maximum(weights - bound, 0.0)
    return jnp.sum(excess * excess / (weights + epsilon))

def widen(tree):
    return jax.tree.map(lambda v: v.astype(jnp.float32), tree)

def reference(points_in, view_enc, deltas, counts, w_first, w_col, w_skip, w_row, b_col, b_row, w_density, w_bottle, b_bottle, w_view, b_view, w_rgb, b_rgb, prop_in, prop_deltas, bin_bounds, wp_first, wp_rest, b_prop, wp_density, d_colour):
    trunk = widen((w_first, w_col, w_skip, w_row, b_col, b_row))
    heads = widen((w_density, w_bottle, b_bottle, w_view, b_view, w_rgb, b_rgb))
    prop = widen((wp_first, wp_rest, b_prop, wp_density))
    blocks = N_DP
    block_rays = RAYS // blocks
    inputs = (points_in.astype(jnp.float32).reshape(blocks, block_rays * SAMPLES, IPE), view_enc.astype(jnp.float32).reshape(blocks, block_rays, VENC), deltas.reshape(blocks, block_rays, SAMPLES), counts.reshape(blocks, block_rays), prop_in.astype(jnp.float32).reshape(blocks, block_rays * PSAMP, IPE), prop_deltas.reshape(blocks, block_rays, PSAMP), jnp.moveaxis(bin_bounds.reshape(2, blocks, block_rays, SAMPLES), 1, 0), jnp.moveaxis(d_colour.reshape(3, blocks, block_rays), 1, 0))
    zeros = jax.tree.map(jnp.zeros_like, (trunk, heads, prop))

    def step(carry, block):
        point_rows, view_rows_in, block_deltas, block_counts, prop_rows, block_prop_deltas, bounds, block_cot = block

        def nerf_part(trunk_in, heads_in, points_here, view_here):
            return nerf_forward(trunk_in, heads_in, points_here, view_here, block_deltas, block_counts)
        (colour, weights), pull = jax.vjp(nerf_part, trunk, heads, point_rows, view_rows_in)
        grad_trunk, grad_heads, grad_pts, grad_vw = pull((block_cot, jnp.zeros_like(weights)))

        def prop_part(prop_here, prop_points):
            return prop_forward(prop_here, prop_points, block_prop_deltas, bounds, weights)
        loss, pull_prop = jax.vjp(prop_part, prop, prop_rows)
        grad_prop, grad_prop_rows = pull_prop(jnp.ones_like(loss))
        carry = jax.tree.map(jnp.add, carry, (grad_trunk, grad_heads, grad_prop))
        return (carry, (colour, grad_pts, grad_vw, grad_prop_rows))
    totals, per_block = lax.scan(step, zeros, inputs)
    grad_trunk, grad_heads, grad_prop = totals
    colour = jnp.moveaxis(per_block[0], 0, 1).reshape(3, RAYS)
    grad_points = per_block[1].reshape(POINTS, IPE)
    grad_view = per_block[2].reshape(RAYS, VENC)
    grad_prop_in = per_block[3].reshape(PPOINTS, IPE)
    return (colour, grad_points, grad_view, grad_prop_in, grad_trunk[0], grad_trunk[1], grad_trunk[2], grad_trunk[3], grad_trunk[4], grad_trunk[5], grad_heads[0], grad_heads[1], grad_heads[2], grad_heads[3], grad_heads[4], grad_heads[5], grad_heads[6], grad_prop[0], grad_prop[1], grad_prop[2], grad_prop[3])
```

```python
import functools

import jax
import jax.numpy as jnp
from jax import lax
from jax.experimental import pallas as pl
from jax.experimental.pallas import tpu as pltpu
from jax.sharding import PartitionSpec as P

EPS = 0.0001
BF = jnp.bfloat16
F32 = jnp.float32
HIGH = lax.Precision.HIGHEST
COPIES = 48
EXTRA = 208
SMALL = 16


def dot(a, b):
    return jnp.dot(a, b, preferred_element_type=F32)


def dot_nt(a, b):
    return lax.dot_general(a, b, (((1,), (1,)), ((), ())), preferred_element_type=F32)


def dot_tn(a, b):
    return lax.dot_general(a, b, (((0,), (0,)), ((), ())), preferred_element_type=F32)


def dot_exact(a, b, dims=(((1,), (0,)), ((), ()))):
    return lax.dot_general(a, b, dims, precision=HIGH, preferred_element_type=F32)


def silu_pair(pre):
    gate = 0.5 + 0.5 * jnp.tanh(0.5 * pre)
    return (pre * gate).astype(BF), gate * (1.0 + pre * (1.0 - gate))


def softplus(v):
    tail = jnp.exp(-jnp.abs(v))
    series = tail * (1.0 - tail * (1.0 / 2 - tail * (1.0 / 3 - tail * (1.0 / 4 - tail * (1.0 / 5)))))
    return jnp.maximum(v, 0.0) + jnp.where(tail < 0.03, series, jnp.log(1.0 + tail))


def one_minus_exp(depth):
    nested = 1.0
    for n in (8, 7, 6, 5, 4, 3, 2):
        nested = 1.0 - depth * (1.0 / n) * nested
    return jnp.where(depth < 0.25, depth * nested, 1.0 - jnp.exp(-depth))


class Copies:
    def __init__(self, sems):
        self.sems = sems
        self.count = 0

    def start(self, source, target):
        copy = pltpu.make_async_copy(source, target, self.sems.at[self.count])
        self.count += 1
        copy.start()
        return copy

    def split(self, whole, index, keep, send):
        half = whole.shape[0] // 2
        at = pl.multiple_of(index * half, half)
        other = pl.multiple_of((1 - index) * half, half)
        one = self.start(whole.at[pl.ds(other, half)], send)
        two = self.start(whole.at[pl.ds(at, half)], keep)
        one.wait()
        two.wait()


def size_of(shape, dtype):
    total = jnp.dtype(dtype).itemsize
    for extent in shape:
        total *= extent
    return total


def kernel(body, name, ins, outs, bufs=(), alias=None, spare=10):
    spaces = {"s": pltpu.SMEM, "v": pltpu.VMEM, "w": pltpu.VMEM, "a": pltpu.HBM}
    held = [(a.shape, a.dtype) for kind, a in ins if kind == "v"] + [o[1:] for o in outs if o[0] == "v"] + list(bufs)
    grant = spare * 1024 * 1024 + sum(2 * size_of(*h) if h[0][-1] < 128 else size_of(*h) for h in held)
    shapes = {"v": jax.ShapeDtypeStruct, "w": pltpu.VMEM, "a": pltpu.HBM}

    def placed(kind, array):
        return pltpu.with_memory_space_constraint(array, spaces[kind]) if kind in "aw" else array

    return pl.pallas_call(
        body,
        out_shape=[shapes[kind](shape, dtype) for kind, shape, dtype in outs],
        in_specs=[pl.BlockSpec(memory_space=spaces[kind]) for kind, _ in ins],
        out_specs=[pl.BlockSpec(memory_space=spaces[kind]) for kind, _, _ in outs],
        scratch_shapes=[pltpu.VMEM(shape, dtype) for shape, dtype in bufs] + [pltpu.SemaphoreType.DMA((COPIES,))],
        input_output_aliases=alias or {},
        compiler_params=pltpu.CompilerParams(vmem_limit_bytes=grant),
        cost_estimate=pl.CostEstimate(flops=1, bytes_accessed=1, transcendentals=0),
        name=name,
    )(*[placed(kind, array) for kind, array in ins])


def pack_first_body(y_ref, w_first, w_skip, b_col, w_row, extra, message, whole, sems):
    io = Copies(sems)
    depth, width = w_first.shape
    count = (message.shape[0] - EXTRA) // width
    tail = w_skip.shape[0] - depth
    copies = [
        io.start(w_row.at[0, :, pl.ds(pl.multiple_of((y_ref[0] * count + n) * width, width), width)], whole.at[EXTRA + n * width : EXTRA + (n + 1) * width])
        for n in range(count)
    ]
    copies.append(io.start(w_first, whole.at[0:depth]))
    copies.append(io.start(w_skip.at[tail : tail + depth], whole.at[depth : 2 * depth]))
    whole[2 * depth : EXTRA] = jnp.concatenate([b_col[...].astype(F32), jnp.zeros((EXTRA - 2 * depth - 4, width), F32)], 0).astype(BF)
    for copy in copies:
        copy.wait()
    copies = [io.start(whole, message), io.start(whole.at[0:EXTRA], extra)]
    for copy in copies:
        copy.wait()


def pack_rest_body(y_ref, w_row, w_col, w_skip, h1, h2, h3, b1, b2, b3, sems):
    io = Copies(sems)
    count, width = b1.shape[0], b1.shape[1]
    outs = ((b1, h1), (b2, h2), (b3, h3))

    def move(source):
        io.count = 0
        groups = [[io.start(source(k + 1, n), buf.at[n]) for n in range(count)] for k, (buf, _) in enumerate(outs)]
        last = []
        for group, (buf, out) in zip(groups, outs):
            for copy in group:
                copy.wait()
            last.append(io.start(buf, out))
        for copy in last:
            copy.wait()

    @pl.when(y_ref[0] == 0)
    def rows():
        move(lambda k, n: w_row.at[k, :, n * width : (n + 1) * width])

    @pl.when(y_ref[0] != 0)
    def columns():
        move(lambda k, n: (w_skip if k == 2 else w_col.at[k // 2]).at[n * width : (n + 1) * width])


class Weights:
    def __init__(self, io, k, y, refs, bufs, rows_first=False):
        own_row, sib_row, own_col, sib_col, hx, hy, cx, cy = refs
        row0, row1, col0, col1, far2, far3 = bufs
        self.bufs = bufs
        self.width = row0.shape[0]
        self.blocks = row0.shape[1] // self.width
        half = far2.shape[0] // 2
        at, other = pl.multiple_of(y * half, half), pl.multiple_of((1 - y) * half, half)
        col_of = (lambda ref: ref.at[0 : self.blocks * self.width]) if k == 2 else (lambda ref: ref.at[k // 2])
        pairs = {
            ("col", 0): [(col_of(own_col), col0)],
            ("col", 1): [(col_of(sib_col), col1)],
            ("far", 2): [(hx, far2.at[pl.ds(at, half)]), (hy, far2.at[pl.ds(other, half)])],
            ("far", 3): [(cx, far3.at[pl.ds(at, half)]), (cy, far3.at[pl.ds(other, half)])],
            ("row", 0): [(own_row.at[k], row0)],
            ("row", 1): [(sib_row.at[k], row1)],
        }
        near, late = (("row", "col") if rows_first else ("col", "row"))
        keys = [(near, 1), (near, 0), ("far", 3), ("far", 2), (late, 1), (late, 0)]
        self.waits = {key: [io.start(*pair) for pair in pairs[key]] for key in keys}

    def ready(self, *key):
        for copy in self.waits.pop(key, ()):
            copy.wait()

    def col(self, j):
        self.ready("col" if j < 2 else "far", j)
        if j < 2:
            return self.bufs[2 + j][...]
        return self.bufs[2 + j][self.blocks : 2 * self.blocks].reshape(self.blocks * self.width, self.width)

    def row(self, j, n):
        self.ready("row" if j < 2 else "far", j)
        if j < 2:
            return self.bufs[j][:, n * self.width : (n + 1) * self.width]
        return self.bufs[2 + j][n]


class FirstWeights:
    def __init__(self, io, y, refs, bufs):
        own_row, sib_row, hx, hy, cx, cy = refs
        self.bufs = bufs
        self.width = bufs[0].shape[0]
        half = bufs[2].shape[0] // 2
        at, other = pl.multiple_of(y * half, half), pl.multiple_of((1 - y) * half, half)
        rows = slice(EXTRA, EXTRA + half)
        self.waits = {
            1: [io.start(sib_row.at[0], bufs[1])],
            0: [io.start(own_row.at[0], bufs[0])],
            3: [io.start(cx.at[rows], bufs[3].at[pl.ds(at, half)]), io.start(cy.at[rows], bufs[3].at[pl.ds(other, half)])],
            2: [io.start(hx.at[rows], bufs[2].at[pl.ds(at, half)]), io.start(hy.at[rows], bufs[2].at[pl.ds(other, half)])],
        }

    def row(self, j, n):
        for copy in self.waits.pop(j, ()):
            copy.wait()
        cols = slice(n * self.width, (n + 1) * self.width)
        return self.bufs[j][:, cols] if j < 2 else self.bufs[j][cols]


def put_block(j, value, even, odd):
    (odd if j % 2 else even)[j // 2] = value


def get_block(j, even, odd):
    return (odd if j % 2 else even)[j // 2]


def first_body(pts, e0, e1, m2, m3, act02, act13, slope_ref, bias_ref, extras, acts, acts13, slopes, sems):
    io = Copies(sems)
    loads = [io.start(m2.at[0:EXTRA], extras.at[2]), io.start(m3.at[0:EXTRA], extras.at[3])]
    extras[0] = e0[...]
    extras[1] = e1[...]
    depth, width = pts.shape[0], e0.shape[1]
    for load in loads:
        load.wait()
    for j in range(4):
        bias_ref[:, j * width : (j + 1) * width] = extras[j, 2 * depth : 2 * depth + 4, :].astype(F32)
    outs = []
    for j in (1, 3, 0, 2):
        act, slope = silu_pair(dot_tn(pts[...], extras[j, 0:depth, :]) + bias_ref[0:1, j * width : (j + 1) * width])
        put_block(j, act, acts, acts13)
        slopes[j] = slope
        if j == 3:
            outs.append(io.start(acts13, act13))
    outs += [io.start(acts, act02), io.start(slopes, slope_ref)]
    for copy in outs:
        copy.wait()


def row_forward(weights, k, acts, acts13, b_row, up, slopes):
    width = acts.shape[1]
    for n in range(up.shape[1] // width):
        cols = slice(n * width, (n + 1) * width)
        pre = b_row[k : k + 1, cols].astype(F32)
        for j in (3, 2, 1, 0):
            pre = pre + dot(get_block(j, acts, acts13), weights.row(j, n))
        act, slope = silu_pair(pre)
        up[:, cols] = act
        slopes[:, cols] = slope


def row0_body(y_ref, b_row, act02, act13, own, sib, hx, hy, cx, cy, up_ref, slope_ref, acts, acts13, w0, w1, w2, w3, up, slopes, sems):
    io = Copies(sems)
    loads = [io.start(act02, acts), io.start(act13, acts13)]
    weights = FirstWeights(io, y_ref[0], (own, sib, hx, hy, cx, cy), (w0, w1, w2, w3))
    for load in loads:
        load.wait()
    row_forward(weights, 0, acts, acts13, b_row, up, slopes)
    outs = [io.start(up, up_ref), io.start(slopes, slope_ref)]
    for copy in outs:
        copy.wait()


def col_forward(weights, k, value, bias, pts, extras, acts, acts13, slopes):
    width = acts.shape[1]
    for j in (1, 0, 3, 2):
        pre = dot(value, weights.col(j)) + bias[k : k + 1, j * width : (j + 1) * width]
        if extras is not None:
            depth = pts.shape[0]
            pre = pre + dot_tn(pts[...], extras[j, depth : 2 * depth, :])
        act, slope = silu_pair(pre)
        put_block(j, act, acts, acts13)
        slopes[j] = slope


def pair_body(k, skip, y_ref, bias, b_row, *rest):
    rest = list(rest)
    pts = rest.pop(0) if skip else None
    extras = rest.pop(0) if skip else None
    u, own_row, sib_row, own_col, sib_col, hx, hy, cx, cy, act02, act13, slope_col, up_ref, slope_row, u_buf, w0, w1, w2, w3, w4, w5, acts, acts13, slopes_c, up, slopes_r, sems = rest
    io = Copies(sems)
    load = io.start(u, u_buf)
    weights = Weights(io, k, y_ref[0], (own_row, sib_row, own_col, sib_col, hx, hy, cx, cy), (w0, w1, w2, w3, w4, w5))
    load.wait()
    col_forward(weights, k, u_buf[...], bias, pts, extras, acts, acts13, slopes_c)
    outs = [io.start(acts13, act13), io.start(acts, act02), io.start(slopes_c, slope_col)]
    row_forward(weights, k, acts, acts13, b_row, up, slopes_r)
    outs += [io.start(up, up_ref), io.start(slopes_r, slope_row)]
    for copy in outs:
        copy.wait()


def chain_step(weights, gr, slope_col, slope_row, pts_depth, extras, gcs, gcs13, gru, gp):
    width = gcs.shape[1]
    blocks = gr.shape[1] // width
    for j in (1, 0, 3, 2):
        gca = dot_nt(gr[:, 0:width], weights.row(j, 0))
        for n in range(1, blocks):
            gca += dot_nt(gr[:, n * width : (n + 1) * width], weights.row(j, n))
        put_block(j, (gca * slope_col[j]).astype(BF), gcs, gcs13)
    if gru is not None:
        gu = None
        for j in (1, 0, 3, 2):
            step = dot_nt(get_block(j, gcs, gcs13), weights.col(j))
            gu = step if gu is None else gu + step
        gru[...] = (gu * slope_row[...]).astype(BF)
    if extras is not None:
        at = pts_depth if gru is not None else 0
        for j in (1, 0, 3, 2):
            gp = gp + dot_nt(extras[j, at : at + pts_depth, :], get_block(j, gcs, gcs13))
    return gp


def top_body(k, samples, n_heads, y_ref, counts, bias, b_row, *rest):
    rest = list(rest)
    heads_in = [rest.pop(0) for _ in range(n_heads)]
    u, slope_row, own_row, sib_row, own_col, sib_col, hx, hy, cx, cy, act02, act13, gr_ref, gc02, gc13, gr_low, colour_ref, gview_ref, weights_ref, gwb_ref, gwv_ref, small_ref, u_buf, sr_buf, w0, w1, w2, w3, w4, w5, acts, acts13, slopes_c, up, slopes_r, gr, gcs, gcs13, gru, sems = rest
    io = Copies(sems)
    load = io.start(u, u_buf)
    weights = Weights(io, k, y_ref[0], (own_row, sib_row, own_col, sib_col, hx, hy, cx, cy), (w0, w1, w2, w3, w4, w5))
    late = io.start(slope_row, sr_buf)
    load.wait()
    col_forward(weights, k, u_buf[...], bias, None, None, acts, acts13, slopes_c)
    outs = [io.start(acts13, act13), io.start(acts, act02)]
    row_forward(weights, k, acts, acts13, b_row, up, slopes_r)
    heads_body(samples, up, counts, *heads_in, slopes_r, colour_ref, gview_ref, gr, weights_ref, gwb_ref, gwv_ref, small_ref)
    outs.append(io.start(gr, gr_ref))
    late.wait()
    chain_step(weights, gr, slopes_c, sr_buf, 0, None, gcs, gcs13, gru, None)
    outs += [io.start(gcs13, gc13), io.start(gcs, gc02), io.start(gru, gr_low)]
    for copy in outs:
        copy.wait()


def chain_body(y_ref, extras, *rest):
    rest = list(rest)
    gr2_in = rest.pop(0)
    slopes_c = {k: rest.pop(0) for k in (2, 1, 0)}
    slopes_r = {k: rest.pop(0) for k in (1, 0)}
    refs = {k: [rest.pop(0) for _ in range(8)] for k in (2, 1)}
    refs[0] = [rest.pop(0) for _ in range(6)]
    gc02 = {k: rest.pop(0) for k in (2, 1, 0)}
    gc13 = {k: rest.pop(0) for k in (2, 1, 0)}
    gr_out = {k: rest.pop(0) for k in (1, 0)}
    gp_ref = rest.pop(0)
    gr = {k: rest.pop(0) for k in (2, 1, 0)}
    sc = {k: rest.pop(0) for k in (2, 1, 0)}
    sr = {k: rest.pop(0) for k in (1, 0)}
    bufs = {k: [rest.pop(0) for _ in range(6)] for k in (2, 1)}
    bufs[0] = [rest.pop(0) for _ in range(4)]
    gcs = {k: rest.pop(0) for k in (2, 1, 0)}
    gcs13 = {k: rest.pop(0) for k in (2, 1, 0)}
    (sems,) = rest
    io = Copies(sems)
    y = y_ref[0]
    weights, loads = {}, {}
    for k in (2, 1, 0):
        loads[k] = [io.start(slopes_c[k], sc[k])]
        if k == 2:
            loads[k].append(io.start(gr2_in, gr[2]))
        weights[k] = Weights(io, k, y, refs[k], bufs[k], rows_first=True) if k else FirstWeights(io, y, refs[k], bufs[k])
        if k:
            loads[k].append(io.start(slopes_r[k - 1], sr[k - 1]))
    depth = gp_ref.shape[0]
    gp = jnp.zeros(gp_ref.shape, F32)
    outs = []
    for k in (2, 1, 0):
        for load in loads[k]:
            load.wait()
        gp = chain_step(weights[k], gr[k], sc[k], sr.get(k - 1), depth, extras if k != 1 else None, gcs[k], gcs13[k], gr.get(k - 1), gp)
        outs += [io.start(gcs13[k], gc13[k]), io.start(gcs[k], gc02[k])]
        if k:
            outs.append(io.start(gr[k - 1], gr_out[k - 1]))
    gp_ref[...] = gp
    for copy in outs:
        copy.wait()


def row_sum(value):
    return jnp.sum(value.astype(F32), axis=0, keepdims=True)


def products_body(kind, folded, *rest):
    rest = list(rest)
    pair = kind != "low"
    i_ref = rest.pop(0) if folded else None
    x_ref = rest.pop(0) if kind == "shared" else None
    points = kind != "plain"
    if points:
        pts, pts_s = rest.pop(0), rest.pop(0)
    if kind == "shared":
        keep_h, came_h = rest.pop(0), rest.pop(0)
    if kind == "low":
        bcs = [rest.pop(0) for _ in range(3)]
        dx2 = rest.pop(0)
        brs = [rest.pop(0) for _ in range(3)]
    act, act_s, gr, gr_s, gc, gc_s = [rest.pop(0) for _ in range(6)]
    if pair:
        u, u_s = rest.pop(0), rest.pop(0)
    away, home = rest.pop(0), rest.pop(0)
    if kind != "low":
        bc_ref, brow_ref = rest.pop(0), rest.pop(0)
    if kind == "shared":
        dx_ref = rest.pop(0)
    act_b, act_sb, gr_b, gr_sb, gc_b, gc_sb = [rest.pop(0) for _ in range(6)]
    if pair:
        u_b, u_sb = rest.pop(0), rest.pop(0)
    away_b, home_b, sems = rest
    io = Copies(sems)
    loads = [io.start(a, b) for a, b in ((act, act_b), (act_s, act_sb), (gr, gr_b), (gr_s, gr_sb), (gc, gc_b), (gc_s, gc_sb))]
    more = [io.start(u, u_b), io.start(u_s, u_sb)] if pair else []
    for load in loads:
        load.wait()
    width = act_b.shape[2]
    feat = gr_b.shape[1]
    blocks = feat // width
    outs = []
    dx = {}
    bc = {}
    for slot, out_b, out in ((1, away_b, away), (0, home_b, home)):
        for n in range(blocks):
            cols = slice(n * width, (n + 1) * width)
            out_b[n * width : (n + 1) * width] = (dot_tn(act_b[slot], gr_b[:, cols]) + dot_tn(act_sb[slot], gr_sb[:, cols])).astype(BF)
        for load in more:
            load.wait()
        more = []
        if pair:
            out_b[feat : 2 * feat] = (dot_tn(u_b[...], gc_b[slot]) + dot_tn(u_sb[...], gc_sb[slot])).astype(BF)
        bc[slot] = row_sum(gc_b[slot]) + row_sum(gc_sb[slot])
        if points:
            dx[slot] = dot(pts[...], gc_b[slot]) + dot(pts_s[...], gc_sb[slot])
        if kind == "shared":
            half = keep_h.shape[0] // 2
            index = x_ref[0] if slot == 0 else 1 - x_ref[0]
            at = pl.ds(pl.multiple_of(index * half, half), half)
            out_b[2 * feat : 2 * feat + half] = (keep_h[at, :].astype(F32) + came_h[at, :].astype(F32)).astype(BF)
        if kind == "low":
            depth = pts.shape[0]
            parts = [dx[slot], dx2[slot], bc[slot]] + [b[slot : slot + 1, :] for b in bcs]
            parts.append(jnp.zeros((EXTRA - 2 * depth - 4, width), F32))
            brow = jnp.concatenate([row_sum(gr_b[:, n * width : (n + 1) * width]) + row_sum(gr_sb[:, n * width : (n + 1) * width]) for n in range(blocks)], 0)
            parts += [brow] + [br[...] for br in brs]
            tail = jnp.concatenate(parts, 0)
            pad = out_b.shape[0] - feat - tail.shape[0]
            out_b[feat:] = jnp.concatenate([tail, jnp.zeros((pad, width), F32)], 0).astype(BF)
        if not folded:
            outs.append(io.start(out_b, out))
            continue
        half = out_b.shape[0] // 2
        at = pl.multiple_of(i_ref[0] * half, half)
        other = pl.multiple_of((1 - i_ref[0]) * half, half)
        rows = slice(0, half) if slot else slice(half, 2 * half)
        outs.append(io.start(out_b.at[pl.ds(other, half)], away.at[rows]))
        outs.append(io.start(out_b.at[pl.ds(at, half)], home.at[rows]))
    if kind != "low":
        for slot in range(2):
            bc_ref[slot : slot + 1, :] = bc[slot]
            if kind == "shared":
                dx_ref[slot] = dx[slot]
        for n in range(blocks):
            cols = slice(n * width, (n + 1) * width)
            brow_ref[n : n + 1, :] = row_sum(gr_b[:, cols]) + row_sum(gr_sb[:, cols])
    for copy in outs:
        copy.wait()


def add_body(a, b, out):
    out[...] = (a[...].astype(F32) + b[...].astype(F32)).astype(BF)


def add_split_body(i_ref, a, b, keep, send):
    half = keep.shape[0]
    at = pl.ds(pl.multiple_of(i_ref[0] * half, half), half)
    other = pl.ds(pl.multiple_of((1 - i_ref[0]) * half, half), half)
    send[...] = (a[other, :].astype(F32) + b[other, :].astype(F32)).astype(BF)
    keep[...] = (a[at, :].astype(F32) + b[at, :].astype(F32)).astype(BF)


def merge_body(i_ref, a, b, out):
    half = a.shape[0]
    out[pl.ds(pl.multiple_of(i_ref[0] * half, half), half), :] = a[...]
    out[pl.ds(pl.multiple_of((1 - i_ref[0]) * half, half), half), :] = b[...]


def gather_pieces(y, z, pieces, whole):
    piece = pieces[0].shape[0]
    places = ((y, z), (y, 1 - z), (1 - y, z), (1 - y, 1 - z))
    for p, (a, b) in zip(pieces, places):
        whole[pl.ds(pl.multiple_of((2 * a + b) * piece, piece), piece), :] = p[...]


def write_row(io, whole, row_b, out, k):
    width = whole.shape[1]
    for n in range(row_b.shape[1] // width):
        row_b[:, n * width : (n + 1) * width] = whole[n * width : (n + 1) * width].astype(F32)
    return io.start(row_b, out.at[k])


def final_pair_body(k, n_alias, y_ref, z_ref, p0, p1, p2, p3, *rest):
    row_out, col_out, whole, row_b, col_b, sems = rest[n_alias:]
    io = Copies(sems)
    gather_pieces(y_ref[0], z_ref[0], (p0, p1, p2, p3), whole)
    copies = [write_row(io, whole, row_b, row_out, k)]
    feat = row_b.shape[1]
    col_b[...] = whole[feat : 2 * feat].astype(F32)
    copies.append(io.start(col_b, col_out.at[k // 2]))
    for copy in copies:
        copy.wait()


def final_skip_body(k, n_alias, y_ref, z_ref, p0, p1, p2, p3, *rest):
    row_out, skip_out, share, whole, row_b, col_b, sems = rest[n_alias:]
    io = Copies(sems)
    gather_pieces(y_ref[0], z_ref[0], (p0, p1, p2, p3), whole)
    copies = [write_row(io, whole, row_b, row_out, k)]
    feat = row_b.shape[1]
    col_b[...] = whole[feat : 2 * feat].astype(F32)
    copies.append(io.start(col_b, skip_out.at[0:feat]))
    share[...] = whole[2 * feat :]
    for copy in copies:
        copy.wait()


def final_low_body(n_alias, y_ref, z_ref, p0, p1, p2, p3, *rest):
    row_out, skip_out, first, bcol, brow, whole, row_b, tail_b, sems = rest[n_alias:]
    io = Copies(sems)
    gather_pieces(y_ref[0], z_ref[0], (p0, p1, p2, p3), whole)
    copies = [write_row(io, whole, row_b, row_out, 0)]
    feat = row_b.shape[1]
    width = whole.shape[1]
    depth = first.shape[0]
    tail_b[...] = whole[feat:].astype(F32)
    copies.append(io.start(tail_b.at[depth : 2 * depth], skip_out.at[feat : feat + depth]))
    first[...] = tail_b[0:depth]
    bcol[...] = tail_b[2 * depth : 2 * depth + 4]
    blocks = feat // width
    for j in range(4):
        for n in range(blocks):
            at = EXTRA + j * blocks + n
            brow[j : j + 1, n * width : (n + 1) * width] = tail_b[at : at + 1]
    for copy in copies:
        copy.wait()


def unpack_body(i_ref, a, b, g_density, g_bottle, gb_bottle, g_view, gb_view, g_rgb, gb_rgb, g_first, g_rest, gb_prop, g_wpd, packed, sems):
    merge_body(i_ref, a, b, packed)
    feat, width = g_bottle.shape
    vw = g_view.shape[1]
    g_bottle[...] = packed[0:feat].astype(F32)
    g_rest[...] = packed[feat : feat + 3 * width].reshape(3, width, width).astype(F32)
    first_at = feat + 3 * width
    view_at = first_at + g_first.shape[0]
    g_first[...] = packed[first_at:view_at].astype(F32)
    wide = packed[view_at : view_at + 144].astype(F32)
    g_view[0:144] = wide[:, 0:vw]
    g_view[144 : g_view.shape[0]] = wide[0 : g_view.shape[0] - 144, vw : 2 * vw]
    small = packed[view_at + 144 : view_at + 144 + SMALL].astype(F32)
    for n in range(feat // width):
        g_density[:, n * width : (n + 1) * width] = small[n : n + 1, :]
    gb_bottle[...] = small[4:5, :]
    gb_view[...] = small[5:6, 0:vw]
    gb_rgb[...] = small[5:6, vw : vw + 3]
    g_rgb[...] = small[6:9, 0:vw]
    gb_prop[...] = small[9:13, :]
    g_wpd[...] = small[13:14, :]


def ray_masks(count, samples):
    row = lax.broadcasted_iota(jnp.int32, (count, count), 0)
    col = lax.broadcasted_iota(jnp.int32, (count, count), 1)
    same = (row // samples) == (col // samples)
    return row, col, same


def exclusive_sum(depth, samples):
    row, col, same = ray_masks(depth.shape[1], samples)
    mask = jnp.where(same & (row < col), 1.0, 0.0)
    return dot_exact(depth, mask)


def later_sum(carried, samples):
    row, col, same = ray_masks(carried.shape[1], samples)
    mask = jnp.where(same & (row > col), 1.0, 0.0)
    return dot_exact(carried, mask)


def pad_rows(value, rows):
    return jnp.concatenate([value, jnp.zeros((rows - value.shape[0], value.shape[1]), value.dtype)], 0)


def row(ref):
    return ref[...].astype(F32)[None, :]


def spread(value, count):
    rays, samples = value.shape
    lane = lax.broadcasted_iota(jnp.int32, (samples, count), 1) % samples
    pick = jnp.where(lane == lax.broadcasted_iota(jnp.int32, (samples, count), 0), 1.0, 0.0)
    wide = dot_exact(value, pick)
    ray = lax.broadcasted_iota(jnp.int32, (rays, count), 1) // samples
    return jnp.sum(jnp.where(ray == lax.broadcasted_iota(jnp.int32, (rays, count), 0), wide, 0.0), axis=0, keepdims=True)


def heads_body(samples, top_ref, counts, w_density, w_bottle, b_bottle, w_view, b_view, w_rgb3, b_rgb, view_enc, deltas, d_ref, slope_row, colour_ref, gview_ref, gr_ref, weights_ref, gwb_ref, gwv_ref, small_ref):
    top = top_ref[...]
    count = top.shape[0]
    rays = count // samples
    venc = view_enc.shape[1]
    vw = w_view.shape[1]
    w_view_b = w_view.at[0 : w_bottle.shape[1]]
    w_view_v = w_view.at[w_bottle.shape[1] : w_view.shape[0]]
    w8 = pad_rows(row(w_density), 8).astype(BF)
    w_rgb = pad_rows(w_rgb3[...].astype(F32), 8).astype(BF)
    deltas = spread(deltas[...], count)
    raw = dot_nt(w8, top)[0:1]
    sigma = softplus(raw - 1.0)
    bottle = (dot(top, w_bottle[...]) + row(b_bottle)).astype(BF)
    view_rows = jnp.concatenate([jnp.broadcast_to(view_enc[r : r + 1, :].astype(F32), (samples, venc)) for r in range(rays)], 0).astype(BF)
    view_pre = dot(bottle, w_view_b[...]) + dot(view_rows, w_view_v[...]) + row(b_view)
    view_act, view_slope = silu_pair(view_pre)
    lane3 = lax.broadcasted_iota(jnp.int32, (3, 3), 0) == lax.broadcasted_iota(jnp.int32, (3, 3), 1)
    rgb_bias = jnp.sum(jnp.where(lane3, row(b_rgb), 0.0), axis=1, keepdims=True)
    rgb = jax.nn.sigmoid(dot_nt(w_rgb, view_act)[0:3] + rgb_bias)
    place = lax.broadcasted_iota(jnp.int32, (1, count), 1)
    limit = jnp.zeros((1, count), jnp.int32)
    for r in range(rays):
        limit = jnp.where(place // samples == r, counts[r], limit)
    live = place % samples < limit
    depth = jnp.where(live, sigma * deltas, 0.0)
    before = exclusive_sum(depth, samples)
    trans = jnp.exp(-before)
    weights = one_minus_exp(depth) * trans
    weights_ref[...] = weights
    pick = jnp.where(
        lax.broadcasted_iota(jnp.int32, (count, rays), 0) // samples == lax.broadcasted_iota(jnp.int32, (count, rays), 1), 1.0, 0.0
    )
    colour_ref[...] = dot_exact(weights * rgb, pick)
    d = dot_exact(d_ref[...], pick, (((1,), (1,)), ((), ())))
    grad_weights = jnp.sum(d * rgb, axis=0, keepdims=True)
    grad_rgb = (d * weights * rgb * (1.0 - rgb)).astype(BF)
    later = later_sum(grad_weights * weights, samples)
    grad_depth = grad_weights * jnp.exp(-depth) * trans - later
    grad_raw = (jnp.where(live, grad_depth * deltas, 0.0) * jax.nn.sigmoid(raw - 1.0)).astype(BF)
    grad_rgb8 = pad_rows(grad_rgb.astype(F32), 8).astype(BF)
    grad_raw8 = pad_rows(grad_raw.astype(F32), 8).astype(BF)
    grad_view_act = dot_tn(grad_rgb8, w_rgb)
    gvp = (grad_view_act * view_slope).astype(BF)
    g_bias_view = jnp.sum(gvp.astype(F32), axis=0, keepdims=True)
    grad_input = dot_nt(gvp, w_view_b[...])
    grad_bottle = grad_input.astype(BF)
    gview = dot_nt(gvp, w_view_v[...])
    gview_ref[...] = jnp.concatenate(
        [jnp.sum(gview[r * samples : (r + 1) * samples], axis=0, keepdims=True) for r in range(rays)], 0
    )
    gr_ref[...] = ((dot_nt(grad_bottle, w_bottle[...]) + dot_tn(grad_raw8, w8)) * slope_row[...]).astype(BF)
    gwb_ref[...] = dot_tn(top, grad_bottle).astype(BF)
    gwv = jnp.concatenate([dot_tn(bottle, gvp), pad_rows(dot_tn(view_rows, gvp), 32)], 0)
    half = gwv.shape[0] // 2
    gwv_ref[:, 0:vw] = gwv[0:half].astype(BF)
    gwv_ref[:, vw : 2 * vw] = gwv[half : 2 * half].astype(BF)
    width = small_ref.shape[1]
    small_ref[...] = jnp.zeros_like(small_ref)
    gwd = dot(grad_raw8, top)[0:1]
    for n in range(top.shape[1] // width):
        small_ref[n : n + 1, :] = gwd[:, n * width : (n + 1) * width]
    small_ref[4:5, :] = jnp.sum(grad_bottle.astype(F32), axis=0, keepdims=True)
    small_ref[5:6, 0:vw] = g_bias_view
    small_ref[6:9, 0:vw] = dot(grad_rgb8, view_act)[0:3]
    small_ref[5:6, vw : vw + 8] = dot_nt(jnp.ones((8, count), BF), grad_rgb8)[0:1]


def prop_forward_body(prop_in, wp_first, wp_rest, b_prop, wp_density, acts_ref, slopes_ref, raw_ref):
    current = prop_in[...]
    for j in range(4):
        weight = wp_first[...] if j == 0 else wp_rest[j - 1]
        pre = dot(current, weight) if j else dot_tn(current, weight)
        act, slope = silu_pair(pre + b_prop[j : j + 1, :].astype(F32))
        acts_ref[j] = act
        slopes_ref[j] = slope
        current = act
    raw_ref[...] = dot_nt(pad_rows(row(wp_density), 8).astype(BF), current)[0:1]


def prop_backward_body(samples, prop_in, acts, slopes, raw_ref, deltas, bounds, weights_ref, wp_first, wp_rest, wp_density, small_a, c_ref, g_bottle, g_view, gin_ref, keep, send, packed, small_ref, sems):
    io = Copies(sems)
    feat = g_bottle.shape[0]
    width = packed.shape[1]
    rest_at, first_at = feat, feat + 3 * width
    view_at = first_at + prop_in.shape[0]
    small_at = view_at + g_view.shape[0]
    loads = [io.start(g_bottle, packed.at[0:feat]), io.start(g_view, packed.at[view_at:small_at])]
    count = prop_in.shape[1]
    raw = raw_ref[...]
    deltas = spread(deltas[...], count)
    bounds = [spread(bounds[n].astype(F32), count) for n in range(2)]
    weights = weights_ref[...]
    depth = softplus(raw - 1.0) * deltas
    before = exclusive_sum(depth, samples)
    trans = jnp.exp(-before)
    pweights = one_minus_exp(depth) * trans
    at_row, _, same = ray_masks(count, samples)
    place = (at_row % samples).astype(F32)
    inside = jnp.where(same & (place >= bounds[0]) & (place < bounds[1]), 1.0, 0.0)
    bound = dot_exact(pweights, inside)
    excess = jnp.maximum(weights - bound, 0.0)
    grad_bound = -2.0 * excess / (weights + EPS)
    grad_pw = dot_exact(grad_bound, inside, (((1,), (1,)), ((), ())))
    later = later_sum(grad_pw * pweights, samples)
    grad_depth = grad_pw * jnp.exp(-depth) * trans - later
    grad_raw = (grad_depth * deltas * jax.nn.sigmoid(raw - 1.0)).astype(BF)
    raw8 = pad_rows(grad_raw.astype(F32), 8).astype(BF)
    wd8 = pad_rows(row(wp_density), 8).astype(BF)
    small_ref[...] = small_a[...]
    small_ref[13:14, :] = dot(raw8, acts[3])[0:1]
    grad = dot_tn(raw8, wd8)
    for j in (3, 2, 1, 0):
        gpre = (grad * slopes[j]).astype(BF)
        small_ref[9 + j : 10 + j, :] = jnp.sum(gpre.astype(F32), axis=0, keepdims=True)
        if j:
            packed[rest_at + (j - 1) * width : rest_at + j * width] = dot_tn(acts[j - 1], gpre).astype(BF)
            grad = dot_nt(gpre, wp_rest[j - 1])
        else:
            packed[first_at:view_at] = dot(prop_in[...], gpre).astype(BF)
            gin_ref[...] = dot_nt(wp_first[...], gpre)
    packed[small_at : small_at + SMALL] = small_ref[...].astype(BF)
    for load in loads:
        load.wait()
    io.split(packed, c_ref[0], keep, send)


def swap(value, axis, bit):
    size = lax.axis_size(axis)
    return lax.ppermute(value, axis, [(i, i ^ bit) for i in range(size)])


class Order:
    def __init__(self):
        self.token = None

    def enter(self, *values):
        if self.token is None:
            return values
        return lax.optimization_barrier((*values, self.token))[:-1]

    def leave(self, value):
        self.token = value
        return value


def late_bits(start):
    bit = start
    while bit < lax.axis_size("dp"):
        yield bit
        bit *= 2


def add_here(order, mine, came, name):
    mine, came = order.enter(mine, came)
    [out] = kernel(lambda a, b, o, sems: add_body(a, b, o), name, [("w", mine), ("v", came)], [("w", mine.shape, BF)], spare=1)
    return order.leave(out)


def split_here(order, index, mine, came, name):
    mine, came = order.enter(mine, came)
    half = (mine.shape[0] // 2, *mine.shape[1:])
    keep, send = kernel(
        lambda i, a, b, k, s, sems: add_split_body(i, a, b, k, s),
        name,
        [("s", index), ("w", mine), ("v", came)],
        [("w", half, BF), ("v", half, BF)],
        spare=1,
    )
    order.leave(send)
    return keep, send


DIMS = {3: "xyz", 2: "xyz", 1: "xyz", 0: "xyz"}
PLAN = "333232312312012021s01s00"
WIRES = {"x": ("mp", 2), "y": ("dp", 1), "z": ("dp", 2)}


def reduce_steps(order, name, dims, send, keep, index, finish):
    outer, inner = [d for d in dims if d != "x"]
    came = swap(send, *WIRES[dims[0]])
    yield
    if dims[0] == "x":
        keep, send = split_here(order, index[outer], keep, came, name + "_a")
        came = swap(send, *WIRES[outer])
    else:
        keep, send = split_here(order, index["second"], keep, came, name + "_a")
        came = swap(send, *WIRES["x"])
    yield
    keep, send = split_here(order, index[inner], keep, came, name + "_b")
    came = swap(send, *WIRES[inner])
    yield
    mine = add_here(order, keep, came, name + "_c")
    for bit in late_bits(4):
        came = swap(mine, "dp", bit)
        yield
        mine = add_here(order, mine, came, name + "_far")
    beside = swap(mine, *WIRES[inner])
    across = swap(mine, *WIRES[outer])
    yield
    (beside,) = order.enter(beside)
    corner = swap(beside, *WIRES[outer])
    yield
    finish((outer, inner), (mine, beside, across, corner))


def shared_steps(order, mine, x1, finish):
    came = swap(mine, "mp", 2)
    yield
    mine, came = order.enter(mine, came)
    [mine] = kernel(
        lambda i, a, b, o, sems: merge_body(i, a, b, o),
        "shared_merge",
        [("s", x1), ("v", mine), ("v", came)],
        [("v", (2 * mine.shape[0], mine.shape[1]), BF)],
        spare=1,
    )
    order.leave(mine)
    came = swap(mine, "mp", 1)
    yield
    finish(mine, came)


class Chain:
    def __init__(self, steps):
        self.steps = steps
        self.step()

    def step(self):
        next(self.steps, None)


def on_device(points_in, view_enc, deltas, counts, w_first, w_col, w_skip, w_row, b_col, b_row, w_density, w_bottle, b_bottle, w_view, b_view, w_rgb, b_rgb, prop_in, prop_deltas, bin_bounds, wp_first, wp_rest, b_prop, wp_density, d_colour):
    rows, ipe = points_in.shape
    rays, samples = deltas.shape
    feat = w_row.shape[2]
    width = w_row.shape[1]
    blocks = feat // width
    bottle = w_bottle.shape[1]
    vw = w_view.shape[1]
    venc = view_enc.shape[1]
    dp = lax.axis_index("dp")
    mp = lax.axis_index("mp")

    def scalar(value):
        return jnp.reshape(value, (1,)).astype(jnp.int32)

    one1 = jnp.ones((1,), jnp.int32)
    y1, z1, c1, x1 = scalar(dp % 2), scalar((dp // 2) % 2), scalar(mp % 2), scalar((mp // 2) % 2)
    order = Order()
    mat = (width, feat)
    tall = (feat, width)
    flat = (rows, feat)
    two = (2, rows, width)
    four = (4, rows, width)
    some = (blocks, width, width)
    many = (2 * blocks, width, width)

    message = (EXTRA + feat // 2, width)
    extra, first_half = kernel(
        pack_first_body,
        "pack_first",
        [("s", y1), ("a", w_first), ("a", w_skip), ("v", b_col), ("a", w_row)],
        [("a", (EXTRA, width), BF), ("a", message, BF)],
        [(message, BF)],
        spare=2,
    )
    order.leave(extra)
    hx = {0: swap(first_half, "mp", 2)}
    e1 = swap(extra, "mp", 1)
    pts = points_in.T
    (y1_k,) = order.enter(y1)
    hs = kernel(pack_rest_body, "pack_rest", [("s", y1_k), ("a", w_row), ("a", w_col), ("a", w_skip)], [("a", some, BF)] * 3, [(some, BF)] * 3, spare=2)
    order.leave(hs[0])
    for k in (1, 2, 3):
        hx[k] = swap(hs[k - 1], "mp", 2)
    row_s = swap(w_row, "mp", 1)
    col_s = swap(w_col, "mp", 1)
    skip_s = swap(w_skip, "mp", 1)
    pts_s = swap(pts, "mp", 1)
    own_cols = {1: w_col, 2: w_skip, 3: w_col}
    sib_cols = {1: col_s, 2: skip_s, 3: col_s}

    act02, act13, act_s, slope_col, slope_row, inputs, inputs_s, gathered = {}, {}, {}, {}, {}, {}, {}, {}

    def arrive(k):
        (hx[k],) = order.enter(hx[k])
        order.leave(hx[k])
        hy = swap(hx[k], "dp", 1)
        cx = swap(hx[k], "mp", 1)
        gathered[k] = (hx[k], hy, cx, swap(hy, "mp", 1))

    arrive(0)
    args = order.enter(pts, extra, e1, gathered[0][0], gathered[0][2])
    act02[0], act13[0], slope_col[0], bias, extras = kernel(
        first_body,
        "first_forward",
        [("v", a) for a in args[:3]] + [("a", a) for a in args[3:]],
        [("a", two, BF), ("a", two, BF), ("a", four, F32), ("v", (4, feat), F32), ("v", (4, EXTRA, width), BF)],
        [(two, BF), (two, BF), (four, F32)],
        spare=4,
    )
    order.leave(bias)
    act_s[0] = swap(act13[0], "mp", 1)
    arrive(1)

    prop_t, wp_first_k = order.enter(prop_in.T, wp_first)
    acts, slopes, prop_raw = kernel(
        lambda *refs: prop_forward_body(*refs[:-1]),
        "prop_forward",
        [("v", prop_t), ("v", wp_first_k), ("v", wp_rest), ("v", b_prop), ("v", wp_density)],
        [("v", (4, rows, bottle), BF), ("v", (4, rows, bottle), F32), ("v", (1, rows), F32)],
        spare=4,
    )
    order.leave(prop_raw)
    arrive(2)
    b_row_k, a02, a13 = order.enter(b_row, act02[0], act13[0])
    up, slope_row[0] = kernel(
        row0_body,
        "row0_forward",
        [("s", y1), ("v", b_row_k), ("a", a02), ("a", a13), ("a", w_row), ("a", row_s)] + [("a", a) for a in gathered[0]],
        [("a", flat, BF), ("a", flat, F32)],
        [(two, BF), (two, BF), (mat, BF), (mat, BF), (tall, BF), (tall, BF), (flat, BF), (flat, F32)],
        spare=6,
    )
    order.leave(up)
    arrive(3)
    weight_bufs = [(mat, BF), (mat, BF), (tall, BF), (tall, BF), (many, BF), (many, BF)]

    def weights_of(k):
        return [("a", a) for a in (w_row, row_s, own_cols[k], sib_cols[k], *gathered[k])]

    for k in (1, 2):
        inputs[k] = up
        inputs_s[k] = swap(up, "mp", 1)
        (b_row_k,) = order.enter(b_row)
        more = [("v", pts), ("v", extras)] if k == 2 else []
        act02[k], act13[k], slope_col[k], up, slope_row[k] = kernel(
            functools.partial(pair_body, k, k == 2),
            f"pair{k}_forward",
            [("s", y1), ("v", bias), ("v", b_row_k)] + more + [("a", inputs[k])] + weights_of(k),
            [("a", two, BF), ("a", two, BF), ("a", four, F32), ("a", flat, BF), ("a", flat, F32)],
            [(flat, BF), *weight_bufs, (two, BF), (two, BF), (four, F32), (flat, BF), (flat, F32)],
            spare=6,
        )
        order.leave(up)
        act_s[k] = swap(act13[k], "mp", 1)

    inputs[3] = up
    inputs_s[3] = swap(up, "mp", 1)
    grs, gr_s, gc02, gc13, gc_s, bc, dx, brow = {}, {}, {}, {}, {}, {}, {}, {}
    heads_in = (w_density, w_bottle, b_bottle, w_view, b_view, w_rgb.T, b_rgb, view_enc, deltas, d_colour)
    (b_row_k,) = order.enter(b_row)
    got = kernel(
        functools.partial(top_body, 3, samples, len(heads_in)),
        "top",
        [("s", y1), ("s", counts), ("v", bias), ("v", b_row_k)] + [("v", a) for a in heads_in] + [("a", up), ("a", slope_row[2])] + weights_of(3),
        [("a", two, BF), ("a", two, BF), ("a", flat, BF), ("a", two, BF), ("a", two, BF), ("a", flat, BF)]
        + [("v", (3, rays), F32), ("v", (rays, venc), F32), ("v", (1, rows), F32), ("v", (feat, bottle), BF), ("v", (144, 2 * vw), BF), ("v", (SMALL, width), F32)],
        [(flat, BF), (flat, F32), *weight_bufs, (two, BF), (two, BF), (four, F32), (flat, BF), (flat, F32), (flat, BF), (two, BF), (two, BF), (flat, BF)],
    )
    act02[3], act13[3], grs[3], gc02[3], gc13[3], grs[2], colour, grad_view, ray_weights, g_bottle, g_view, small_a = got
    order.leave(grs[2])
    act_s[3] = swap(act13[3], "mp", 1)
    gr_s[3] = swap(grs[3], "mp", 1)
    gc_s[3] = swap(gc13[3], "mp", 1)

    results, chains = {}, {}

    index = {"x": x1, "y": y1, "z": z1, "second": one1}

    def finish(k, halved, pieces):
        pieces = order.enter(*pieces)
        size = (4 * pieces[0].shape[0], width)
        ins = [("s", index[halved[0]]), ("s", index[halved[1]])] + [("v", p) for p in pieces]
        outs = [("a", (4, width, feat), F32)]
        bufs = [(size, BF), (mat, F32)]
        alias = {}

        def in_place(name, index):
            if name in results:
                alias[len(ins)] = index
                ins.append(("a", results[name]))

        in_place("row", 0)
        if k == 2:
            outs += [("a", (feat + ipe, width), F32), ("v", (size[0] - 2 * feat, width), BF)]
            bufs.append((tall, F32))
            in_place("skip", 1)
            got = kernel(functools.partial(final_skip_body, k, len(alias)), f"final{k}", ins, outs, bufs, alias, spare=4)
            results["skip"] = got[1]
            chains["s"] = Chain(shared_steps(order, got[2], x1, finish_shared))
        elif k:
            outs.append(("a", (2, feat, width), F32))
            bufs.append((tall, F32))
            in_place("col", 1)
            got = kernel(functools.partial(final_pair_body, k, len(alias)), f"final{k}", ins, outs, bufs, alias, spare=4)
            results["col"] = got[1]
        else:
            outs += [("a", (feat + ipe, width), F32), ("v", (ipe, width), F32), ("v", (4, width), F32), ("v", (4, feat), F32)]
            bufs.append(((size[0] - feat, width), F32))
            in_place("skip", 1)
            got = kernel(functools.partial(final_low_body, len(alias)), f"final{k}", ins, outs, bufs, alias, spare=4)
            results["skip"] = got[1]
            results["tail"] = got[2:]
        results["row"] = got[0]
        order.leave(got[0])

    def finish_shared(mine, came):
        mine, came = order.enter(mine, came)
        results["shared"] = kernel(
            unpack_body,
            "unpack",
            [("s", c1), ("v", mine), ("v", came)],
            [
                ("v", (1, feat), F32),
                ("v", (feat, bottle), F32),
                ("v", (1, bottle), F32),
                ("v", (bottle + venc, vw), F32),
                ("v", (1, vw), F32),
                ("v", (3, vw), F32),
                ("v", (1, 3), F32),
                ("v", (ipe, bottle), F32),
                ("v", (3, bottle, bottle), F32),
                ("v", (4, bottle), F32),
                ("v", (1, bottle), F32),
            ],
            [((2048, bottle), BF)],
            spare=4,
        )
        order.leave(results["shared"][0])

    def send_away(k):
        dims = DIMS[k]
        folded = dims[0] != "x"
        kind = {3: "plain", 2: "shared", 1: "plain", 0: "low"}[k]
        args = [act02[k], act_s[k], grs[k], gr_s[k], gc02[k], gc_s[k]] + ([inputs[k], inputs_s[k]] if k else [])
        args = order.enter(*args)
        height = {"plain": 2 * feat, "shared": 2 * feat + 512, "low": feat + 256}[kind]
        small = [("s", index[dims[0]])] if folded else []
        if kind == "shared":
            small += [("s", x1)]
        if kind != "plain":
            small += [("v", pts), ("v", pts_s)]
        if kind == "shared":
            small += [("v", keep_h), ("v", came_h)]
        if kind == "low":
            small += [("v", bc[1]), ("v", bc[2]), ("v", bc[3]), ("v", dx[2]), ("v", brow[1]), ("v", brow[2]), ("v", brow[3])]
        outs = [("a", (height, width), BF), ("w", (height, width), BF)]
        if kind != "low":
            outs += [("v", (2, width), F32), ("v", (blocks, width), F32)]
        if kind == "shared":
            outs.append(("v", (2, ipe, width), F32))
        bufs = [(two, BF), (two, BF), (flat, BF), (flat, BF), (two, BF), (two, BF)] + ([(flat, BF), (flat, BF)] if k else [])
        out, home, *rest = kernel(
            functools.partial(products_body, kind, folded), f"products{k}", small + [("a", a) for a in args], outs, bufs + [((height, width), BF)] * 2, spare=6
        )
        if rest:
            bc[k], brow[k] = rest[:2]
        if kind == "shared":
            dx[k] = rest[2]
        order.leave(out)
        chains[str(k)] = Chain(reduce_steps(order, f"sum{k}", dims, out, home, index, functools.partial(finish, k)))

    send_away(3)

    prop_args = order.enter(prop_t, acts, slopes, prop_raw, prop_deltas, bin_bounds, ray_weights, wp_first, wp_rest, wp_density, small_a, c1, g_bottle, g_view)
    grad_prop_in, keep_h, send_h = kernel(
        functools.partial(prop_backward_body, samples),
        "prop_backward",
        [("s" if n == 11 else "a" if n > 11 else "v", a) for n, a in enumerate(prop_args)],
        [("v", (ipe, rows), F32), ("a", (1024, bottle), BF), ("a", (1024, bottle), BF)],
        [((2048, bottle), BF), ((SMALL, width), F32)],
        spare=6,
    )
    order.leave(send_h)
    came_h = swap(send_h, "mp", 1)

    args = order.enter(grs[2], slope_col[2], slope_col[1], slope_col[0], slope_row[1], slope_row[0])
    got = kernel(
        chain_body,
        "chain",
        [("s", y1), ("v", extras)]
        + [("a", a) for a in args]
        + weights_of(2)
        + weights_of(1)
        + [("a", a) for a in (w_row, row_s, *gathered[0])],
        [("a", two, BF)] * 6 + [("a", flat, BF)] * 2 + [("v", (ipe, rows), F32)],
        [(flat, BF)] * 3 + [(four, F32)] * 3 + [(flat, F32)] * 2 + weight_bufs + weight_bufs + [(mat, BF)] * 2 + [(tall, BF)] * 2 + [(two, BF)] * 6,
        spare=6,
    )
    gc02[2], gc02[1], gc02[0], gc13[2], gc13[1], gc13[0], grs[1], grs[0], grad_points = got
    order.leave(grad_points)
    for k in (2, 1, 0):
        gr_s[k] = swap(grs[k], "mp", 1)
        gc_s[k] = swap(gc13[k], "mp", 1)
    send_away(2)
    send_away(1)
    send_away(0)
    for item in PLAN:
        if item in chains:
            chains[item].step()
    for item in ("3", "2", "1", "0", "s"):
        for _ in range(16):
            chains[item].step()

    g_density, g_bottle, gb_bottle, g_view, gb_view, g_rgb, gb_rgb, g_first, g_rest, gb_prop, g_wpd = results["shared"]
    first, bcol, brow_out = results["tail"]
    return (
        colour,
        grad_points.T,
        grad_view,
        grad_prop_in.T,
        first,
        results["col"],
        results["skip"],
        results["row"],
        bcol,
        brow_out,
        g_density.reshape(feat),
        g_bottle,
        gb_bottle.reshape(bottle),
        g_view,
        gb_view.reshape(vw),
        g_rgb.T,
        gb_rgb.reshape(3),
        g_first,
        g_rest,
        gb_prop,
        g_wpd.reshape(bottle),
    )


def solution(mesh):
    both = ("dp", "mp")
    placed = (
        P(both, None),
        P(both, None),
        P(both, None),
        P(both),
        P(None, "mp"),
        P(None, None, "mp"),
        P(None, "mp"),
        P(None, "mp", None),
        P(None, "mp"),
        *([P()] * 8),
        P(both, None),
        P(both, None),
        P(None, both, None),
        P(),
        P(),
        P(),
        P(),
        P(None, both),
    )
    return jax.shard_map(
        on_device,
        mesh=mesh,
        in_specs=placed,
        out_specs=(
            P(None, both),
            P(both, None),
            P(both, None),
            P(both, None),
            P(None, "mp"),
            P(None, None, "mp"),
            P(None, "mp"),
            P(None, "mp", None),
            P(None, "mp"),
            *([P()] * 12),
        ),
        check_vma=False,
    )
```

```python
import functools

import jax
import jax.numpy as jnp
from jax import lax
from jax.experimental import pallas as pl
from jax.experimental.pallas import tpu as pltpu
from jax.sharding import PartitionSpec as P

EPS = 0.0001
BF = jnp.bfloat16
F32 = jnp.float32
HIGH = lax.Precision.HIGHEST
COPIES = 48
EXTRA = 208
SMALL = 16


def dot(a, b):
    return jnp.dot(a, b, preferred_element_type=F32)


def dot_nt(a, b):
    return lax.dot_general(a, b, (((1,), (1,)), ((), ())), preferred_element_type=F32)


def dot_tn(a, b):
    return lax.dot_general(a, b, (((0,), (0,)), ((), ())), preferred_element_type=F32)


def dot_exact(a, b, dims=(((1,), (0,)), ((), ()))):
    return lax.dot_general(a, b, dims, precision=HIGH, preferred_element_type=F32)


def silu_pair(pre):
    gate = 0.5 + 0.5 * jnp.tanh(0.5 * pre)
    return (pre * gate).astype(BF), gate * (1.0 + pre * (1.0 - gate))


def softplus(v):
    tail = jnp.exp(-jnp.abs(v))
    series = tail * (1.0 - tail * (1.0 / 2 - tail * (1.0 / 3 - tail * (1.0 / 4 - tail * (1.0 / 5)))))
    return jnp.maximum(v, 0.0) + jnp.where(tail < 0.03, series, jnp.log(1.0 + tail))


def one_minus_exp(depth):
    nested = 1.0
    for n in (8, 7, 6, 5, 4, 3, 2):
        nested = 1.0 - depth * (1.0 / n) * nested
    return jnp.where(depth < 0.25, depth * nested, 1.0 - jnp.exp(-depth))


class Copies:
    def __init__(self, sems):
        self.sems = sems
        self.count = 0

    def start(self, source, target):
        copy = pltpu.make_async_copy(source, target, self.sems.at[self.count])
        self.count += 1
        copy.start()
        return copy

    def split(self, whole, index, keep, send):
        half = whole.shape[0] // 2
        at = pl.multiple_of(index * half, half)
        other = pl.multiple_of((1 - index) * half, half)
        one = self.start(whole.at[pl.ds(other, half)], send)
        two = self.start(whole.at[pl.ds(at, half)], keep)
        one.wait()
        two.wait()


def size_of(shape, dtype):
    total = jnp.dtype(dtype).itemsize
    for extent in shape:
        total *= extent
    return total


def kernel(body, name, ins, outs, bufs=(), alias=None, spare=10):
    spaces = {"s": pltpu.SMEM, "v": pltpu.VMEM, "w": pltpu.VMEM, "a": pltpu.HBM}
    held = [(a.shape, a.dtype) for kind, a in ins if kind == "v"] + [o[1:] for o in outs if o[0] == "v"] + list(bufs)
    grant = spare * 1024 * 1024 + sum(2 * size_of(*h) if h[0][-1] < 128 else size_of(*h) for h in held)
    shapes = {"v": jax.ShapeDtypeStruct, "w": pltpu.VMEM, "a": pltpu.HBM}

    def placed(kind, array):
        return pltpu.with_memory_space_constraint(array, spaces[kind]) if kind in "aw" else array

    return pl.pallas_call(
        body,
        out_shape=[shapes[kind](shape, dtype) for kind, shape, dtype in outs],
        in_specs=[pl.BlockSpec(memory_space=spaces[kind]) for kind, _ in ins],
        out_specs=[pl.BlockSpec(memory_space=spaces[kind]) for kind, _, _ in outs],
        scratch_shapes=[pltpu.VMEM(shape, dtype) for shape, dtype in bufs] + [pltpu.SemaphoreType.DMA((COPIES,))],
        input_output_aliases=alias or {},
        compiler_params=pltpu.CompilerParams(vmem_limit_bytes=grant),
        cost_estimate=pl.CostEstimate(flops=1, bytes_accessed=1, transcendentals=0),
        name=name,
    )(*[placed(kind, array) for kind, array in ins])


def pack_first_body(y_ref, w_first, w_skip, b_col, w_row, extra, message, whole, sems):
    io = Copies(sems)
    depth, width = w_first.shape
    count = (message.shape[0] - EXTRA) // width
    tail = w_skip.shape[0] - depth
    copies = [
        io.start(w_row.at[0, :, pl.ds(pl.multiple_of((y_ref[0] * count + n) * width, width), width)], whole.at[EXTRA + n * width : EXTRA + (n + 1) * width])
        for n in range(count)
    ]
    copies.append(io.start(w_first, whole.at[0:depth]))
    copies.append(io.start(w_skip.at[tail : tail + depth], whole.at[depth : 2 * depth]))
    whole[2 * depth : EXTRA] = jnp.concatenate([b_col[...].astype(F32), jnp.zeros((EXTRA - 2 * depth - 4, width), F32)], 0).astype(BF)
    for copy in copies:
        copy.wait()
    copies = [io.start(whole, message), io.start(whole.at[0:EXTRA], extra)]
    for copy in copies:
        copy.wait()


def pack_rest_body(y_ref, w_row, w_col, w_skip, h1, h2, h3, b1, b2, b3, sems):
    io = Copies(sems)
    count, width = b1.shape[0], b1.shape[1]
    outs = ((b1, h1), (b2, h2), (b3, h3))

    def move(source):
        io.count = 0
        groups = [[io.start(source(k + 1, n), buf.at[n]) for n in range(count)] for k, (buf, _) in enumerate(outs)]
        last = []
        for group, (buf, out) in zip(groups, outs):
            for copy in group:
                copy.wait()
            last.append(io.start(buf, out))
        for copy in last:
            copy.wait()

    @pl.when(y_ref[0] == 0)
    def rows():
        move(lambda k, n: w_row.at[k, :, n * width : (n + 1) * width])

    @pl.when(y_ref[0] != 0)
    def columns():
        move(lambda k, n: (w_skip if k == 2 else w_col.at[k // 2]).at[n * width : (n + 1) * width])


class Weights:
    def __init__(self, io, k, y, refs, bufs, rows_first=False):
        own_row, sib_row, own_col, sib_col, hx, hy, cx, cy = refs
        row0, row1, col0, col1, far2, far3 = bufs
        self.bufs = bufs
        self.width = row0.shape[0]
        self.blocks = row0.shape[1] // self.width
        half = far2.shape[0] // 2
        at, other = pl.multiple_of(y * half, half), pl.multiple_of((1 - y) * half, half)
        col_of = (lambda ref: ref.at[0 : self.blocks * self.width]) if k == 2 else (lambda ref: ref.at[k // 2])
        pairs = {
            ("col", 0): [(col_of(own_col), col0)],
            ("col", 1): [(col_of(sib_col), col1)],
            ("far", 2): [(hx, far2.at[pl.ds(at, half)]), (hy, far2.at[pl.ds(other, half)])],
            ("far", 3): [(cx, far3.at[pl.ds(at, half)]), (cy, far3.at[pl.ds(other, half)])],
            ("row", 0): [(own_row.at[k], row0)],
            ("row", 1): [(sib_row.at[k], row1)],
        }
        near, late = (("row", "col") if rows_first else ("col", "row"))
        keys = [(near, 1), (near, 0), ("far", 3), ("far", 2), (late, 1), (late, 0)]
        self.waits = {key: [io.start(*pair) for pair in pairs[key]] for key in keys}

    def ready(self, *key):
        for copy in self.waits.pop(key, ()):
            copy.wait()

    def col(self, j):
        self.ready("col" if j < 2 else "far", j)
        if j < 2:
            return self.bufs[2 + j][...]
        return self.bufs[2 + j][self.blocks : 2 * self.blocks].reshape(self.blocks * self.width, self.width)

    def row(self, j, n):
        self.ready("row" if j < 2 else "far", j)
        if j < 2:
            return self.bufs[j][:, n * self.width : (n + 1) * self.width]
        return self.bufs[2 + j][n]


class FirstWeights:
    def __init__(self, io, y, refs, bufs):
        own_row, sib_row, hx, hy, cx, cy = refs
        self.bufs = bufs
        self.width = bufs[0].shape[0]
        half = bufs[2].shape[0] // 2
        at, other = pl.multiple_of(y * half, half), pl.multiple_of((1 - y) * half, half)
        rows = slice(EXTRA, EXTRA + half)
        self.waits = {
            1: [io.start(sib_row.at[0], bufs[1])],
            0: [io.start(own_row.at[0], bufs[0])],
            3: [io.start(cx.at[rows], bufs[3].at[pl.ds(at, half)]), io.start(cy.at[rows], bufs[3].at[pl.ds(other, half)])],
            2: [io.start(hx.at[rows], bufs[2].at[pl.ds(at, half)]), io.start(hy.at[rows], bufs[2].at[pl.ds(other, half)])],
        }

    def row(self, j, n):
        for copy in self.waits.pop(j, ()):
            copy.wait()
        cols = slice(n * self.width, (n + 1) * self.width)
        return self.bufs[j][:, cols] if j < 2 else self.bufs[j][cols]


def put_block(j, value, even, odd):
    (odd if j % 2 else even)[j // 2] = value


def get_block(j, even, odd):
    return (odd if j % 2 else even)[j // 2]


def first_body(pts, e0, e1, m2, m3, act02, act13, slope_ref, bias_ref, extras, acts, acts13, slopes, sems):
    io = Copies(sems)
    loads = [io.start(m2.at[0:EXTRA], extras.at[2]), io.start(m3.at[0:EXTRA], extras.at[3])]
    extras[0] = e0[...]
    extras[1] = e1[...]
    depth, width = pts.shape[0], e0.shape[1]
    for load in loads:
        load.wait()
    for j in range(4):
        bias_ref[:, j * width : (j + 1) * width] = extras[j, 2 * depth : 2 * depth + 4, :].astype(F32)
    outs = []
    for j in (1, 3, 0, 2):
        act, slope = silu_pair(dot_tn(pts[...], extras[j, 0:depth, :]) + bias_ref[0:1, j * width : (j + 1) * width])
        put_block(j, act, acts, acts13)
        slopes[j] = slope
        if j == 3:
            outs.append(io.start(acts13, act13))
    outs += [io.start(acts, act02), io.start(slopes, slope_ref)]
    for copy in outs:
        copy.wait()


def row_forward(weights, k, acts, acts13, b_row, up, slopes):
    width = acts.shape[1]
    for n in range(up.shape[1] // width):
        cols = slice(n * width, (n + 1) * width)
        pre = b_row[k : k + 1, cols].astype(F32)
        for j in (3, 2, 1, 0):
            pre = pre + dot(get_block(j, acts, acts13), weights.row(j, n))
        act, slope = silu_pair(pre)
        up[:, cols] = act
        slopes[:, cols] = slope


def row0_body(y_ref, b_row, act02, act13, own, sib, hx, hy, cx, cy, up_ref, slope_ref, acts, acts13, w0, w1, w2, w3, up, slopes, sems):
    io = Copies(sems)
    loads = [io.start(act02, acts), io.start(act13, acts13)]
    weights = FirstWeights(io, y_ref[0], (own, sib, hx, hy, cx, cy), (w0, w1, w2, w3))
    for load in loads:
        load.wait()
    row_forward(weights, 0, acts, acts13, b_row, up, slopes)
    outs = [io.start(up, up_ref), io.start(slopes, slope_ref)]
    for copy in outs:
        copy.wait()


def col_forward(weights, k, value, bias, pts, extras, acts, acts13, slopes):
    width = acts.shape[1]
    for j in (1, 0, 3, 2):
        pre = dot(value, weights.col(j)) + bias[k : k + 1, j * width : (j + 1) * width]
        if extras is not None:
            depth = pts.shape[0]
            pre = pre + dot_tn(pts[...], extras[j, depth : 2 * depth, :])
        act, slope = silu_pair(pre)
        put_block(j, act, acts, acts13)
        slopes[j] = slope


def pair_body(k, skip, y_ref, bias, b_row, *rest):
    rest = list(rest)
    pts = rest.pop(0) if skip else None
    extras = rest.pop(0) if skip else None
    u, own_row, sib_row, own_col, sib_col, hx, hy, cx, cy, act02, act13, slope_col, up_ref, slope_row, u_buf, w0, w1, w2, w3, w4, w5, acts, acts13, slopes_c, up, slopes_r, sems = rest
    io = Copies(sems)
    load = io.start(u, u_buf)
    weights = Weights(io, k, y_ref[0], (own_row, sib_row, own_col, sib_col, hx, hy, cx, cy), (w0, w1, w2, w3, w4, w5))
    load.wait()
    col_forward(weights, k, u_buf[...], bias, pts, extras, acts, acts13, slopes_c)
    outs = [io.start(acts13, act13), io.start(acts, act02), io.start(slopes_c, slope_col)]
    row_forward(weights, k, acts, acts13, b_row, up, slopes_r)
    outs += [io.start(up, up_ref), io.start(slopes_r, slope_row)]
    for copy in outs:
        copy.wait()


def chain_step(weights, gr, slope_col, slope_row, pts_depth, extras, gcs, gcs13, gru, gp):
    width = gcs.shape[1]
    blocks = gr.shape[1] // width
    for j in (1, 0, 3, 2):
        gca = dot_nt(gr[:, 0:width], weights.row(j, 0))
        for n in range(1, blocks):
            gca += dot_nt(gr[:, n * width : (n + 1) * width], weights.row(j, n))
        put_block(j, (gca * slope_col[j]).astype(BF), gcs, gcs13)
    if gru is not None:
        gu = None
        for j in (1, 0, 3, 2):
            step = dot_nt(get_block(j, gcs, gcs13), weights.col(j))
            gu = step if gu is None else gu + step
        gru[...] = (gu * slope_row[...]).astype(BF)
    if extras is not None:
        at = pts_depth if gru is not None else 0
        for j in (1, 0, 3, 2):
            gp = gp + dot_nt(extras[j, at : at + pts_depth, :], get_block(j, gcs, gcs13))
    return gp


def top_body(k, samples, n_heads, y_ref, counts, bias, b_row, *rest):
    rest = list(rest)
    heads_in = [rest.pop(0) for _ in range(n_heads)]
    u, slope_row, own_row, sib_row, own_col, sib_col, hx, hy, cx, cy, act02, act13, gr_ref, gc02, gc13, gr_low, colour_ref, gview_ref, weights_ref, gwb_ref, gwv_ref, small_ref, u_buf, sr_buf, w0, w1, w2, w3, w4, w5, acts, acts13, slopes_c, up, slopes_r, gr, gcs, gcs13, gru, sems = rest
    io = Copies(sems)
    load = io.start(u, u_buf)
    weights = Weights(io, k, y_ref[0], (own_row, sib_row, own_col, sib_col, hx, hy, cx, cy), (w0, w1, w2, w3, w4, w5))
    late = io.start(slope_row, sr_buf)
    load.wait()
    col_forward(weights, k, u_buf[...], bias, None, None, acts, acts13, slopes_c)
    outs = [io.start(acts13, act13), io.start(acts, act02)]
    row_forward(weights, k, acts, acts13, b_row, up, slopes_r)
    heads_body(samples, up, counts, *heads_in, slopes_r, colour_ref, gview_ref, gr, weights_ref, gwb_ref, gwv_ref, small_ref)
    outs.append(io.start(gr, gr_ref))
    late.wait()
    chain_step(weights, gr, slopes_c, sr_buf, 0, None, gcs, gcs13, gru, None)
    outs += [io.start(gcs13, gc13), io.start(gcs, gc02), io.start(gru, gr_low)]
    for copy in outs:
        copy.wait()


def chain_body(y_ref, extras, *rest):
    rest = list(rest)
    gr2_in = rest.pop(0)
    slopes_c = {k: rest.pop(0) for k in (2, 1, 0)}
    slopes_r = {k: rest.pop(0) for k in (1, 0)}
    refs = {k: [rest.pop(0) for _ in range(8)] for k in (2, 1)}
    refs[0] = [rest.pop(0) for _ in range(6)]
    gc02 = {k: rest.pop(0) for k in (2, 1, 0)}
    gc13 = {k: rest.pop(0) for k in (2, 1, 0)}
    gr_out = {k: rest.pop(0) for k in (1, 0)}
    gp_ref = rest.pop(0)
    gr = {k: rest.pop(0) for k in (2, 1, 0)}
    sc = {k: rest.pop(0) for k in (2, 1, 0)}
    sr = {k: rest.pop(0) for k in (1, 0)}
    bufs = {k: [rest.pop(0) for _ in range(6)] for k in (2, 1)}
    bufs[0] = [rest.pop(0) for _ in range(4)]
    gcs = {k: rest.pop(0) for k in (2, 1, 0)}
    gcs13 = {k: rest.pop(0) for k in (2, 1, 0)}
    (sems,) = rest
    io = Copies(sems)
    y = y_ref[0]
    weights, loads = {}, {}
    for k in (2, 1, 0):
        loads[k] = [io.start(slopes_c[k], sc[k])]
        if k == 2:
            loads[k].append(io.start(gr2_in, gr[2]))
        weights[k] = Weights(io, k, y, refs[k], bufs[k], rows_first=True) if k else FirstWeights(io, y, refs[k], bufs[k])
        if k:
            loads[k].append(io.start(slopes_r[k - 1], sr[k - 1]))
    depth = gp_ref.shape[0]
    gp = jnp.zeros(gp_ref.shape, F32)
    outs = []
    for k in (2, 1, 0):
        for load in loads[k]:
            load.wait()
        gp = chain_step(weights[k], gr[k], sc[k], sr.get(k - 1), depth, extras if k != 1 else None, gcs[k], gcs13[k], gr.get(k - 1), gp)
        outs += [io.start(gcs13[k], gc13[k]), io.start(gcs[k], gc02[k])]
        if k:
            outs.append(io.start(gr[k - 1], gr_out[k - 1]))
    gp_ref[...] = gp
    for copy in outs:
        copy.wait()


def row_sum(value):
    return jnp.sum(value.astype(F32), axis=0, keepdims=True)


def products_body(kind, folded, *rest):
    rest = list(rest)
    pair = kind != "low"
    i_ref = rest.pop(0) if folded else None
    x_ref = rest.pop(0) if kind == "low" else None
    points = kind != "plain"
    if points:
        pts, pts_s = rest.pop(0), rest.pop(0)
    if kind == "low":
        keep_h, came_h = rest.pop(0), rest.pop(0)
        bcs = [rest.pop(0) for _ in range(3)]
        dx2 = rest.pop(0)
        brs = [rest.pop(0) for _ in range(3)]
    act, act_s, gr, gr_s, gc, gc_s = [rest.pop(0) for _ in range(6)]
    if pair:
        u, u_s = rest.pop(0), rest.pop(0)
    away, home = rest.pop(0), rest.pop(0)
    if kind != "low":
        bc_ref, brow_ref = rest.pop(0), rest.pop(0)
    if kind == "points":
        dx_ref = rest.pop(0)
    act_b, act_sb, gr_b, gr_sb, gc_b, gc_sb = [rest.pop(0) for _ in range(6)]
    if pair:
        u_b, u_sb = rest.pop(0), rest.pop(0)
    away_b, home_b, sems = rest
    io = Copies(sems)
    loads = [io.start(a, b) for a, b in ((act, act_b), (act_s, act_sb), (gr, gr_b), (gr_s, gr_sb), (gc, gc_b), (gc_s, gc_sb))]
    more = [io.start(u, u_b), io.start(u_s, u_sb)] if pair else []
    for load in loads:
        load.wait()
    width = act_b.shape[2]
    feat = gr_b.shape[1]
    blocks = feat // width
    outs = []
    dx = {}
    bc = {}
    for slot, out_b, out in ((1, away_b, away), (0, home_b, home)):
        for n in range(blocks):
            cols = slice(n * width, (n + 1) * width)
            out_b[n * width : (n + 1) * width] = (dot_tn(act_b[slot], gr_b[:, cols]) + dot_tn(act_sb[slot], gr_sb[:, cols])).astype(BF)
        for load in more:
            load.wait()
        more = []
        if pair:
            out_b[feat : 2 * feat] = (dot_tn(u_b[...], gc_b[slot]) + dot_tn(u_sb[...], gc_sb[slot])).astype(BF)
        bc[slot] = row_sum(gc_b[slot]) + row_sum(gc_sb[slot])
        if points:
            dx[slot] = dot(pts[...], gc_b[slot]) + dot(pts_s[...], gc_sb[slot])
        if kind == "low":
            half = keep_h.shape[0] // 2
            index = x_ref[0] if slot == 0 else 1 - x_ref[0]
            at = pl.ds(pl.multiple_of(index * half, half), half)
            out_b[feat : feat + half] = (keep_h[at, :].astype(F32) + came_h[at, :].astype(F32)).astype(BF)
            depth = pts.shape[0]
            parts = [dx[slot], dx2[slot], bc[slot]] + [b[slot : slot + 1, :] for b in bcs]
            parts.append(jnp.zeros((EXTRA - 2 * depth - 4, width), F32))
            brow = jnp.concatenate([row_sum(gr_b[:, n * width : (n + 1) * width]) + row_sum(gr_sb[:, n * width : (n + 1) * width]) for n in range(blocks)], 0)
            parts += [brow] + [br[...] for br in brs]
            tail = jnp.concatenate(parts, 0)
            pad = out_b.shape[0] - feat - half - tail.shape[0]
            out_b[feat + half :] = jnp.concatenate([tail, jnp.zeros((pad, width), F32)], 0).astype(BF)
        if not folded:
            outs.append(io.start(out_b, out))
            continue
        half = out_b.shape[0] // 2
        at = pl.multiple_of(i_ref[0] * half, half)
        other = pl.multiple_of((1 - i_ref[0]) * half, half)
        rows = slice(0, half) if slot else slice(half, 2 * half)
        outs.append(io.start(out_b.at[pl.ds(other, half)], away.at[rows]))
        outs.append(io.start(out_b.at[pl.ds(at, half)], home.at[rows]))
    if kind != "low":
        for slot in range(2):
            bc_ref[slot : slot + 1, :] = bc[slot]
            if kind == "points":
                dx_ref[slot] = dx[slot]
        for n in range(blocks):
            cols = slice(n * width, (n + 1) * width)
            brow_ref[n : n + 1, :] = row_sum(gr_b[:, cols]) + row_sum(gr_sb[:, cols])
    for copy in outs:
        copy.wait()


def add_body(a, b, out):
    out[...] = (a[...].astype(F32) + b[...].astype(F32)).astype(BF)


def add_split_body(i_ref, a, b, keep, send):
    half = keep.shape[0]
    at = pl.ds(pl.multiple_of(i_ref[0] * half, half), half)
    other = pl.ds(pl.multiple_of((1 - i_ref[0]) * half, half), half)
    send[...] = (a[other, :].astype(F32) + b[other, :].astype(F32)).astype(BF)
    keep[...] = (a[at, :].astype(F32) + b[at, :].astype(F32)).astype(BF)


def merge_body(i_ref, a, b, out):
    half = a.shape[0]
    out[pl.ds(pl.multiple_of(i_ref[0] * half, half), half), :] = a[...]
    out[pl.ds(pl.multiple_of((1 - i_ref[0]) * half, half), half), :] = b[...]


def gather_pieces(y, z, pieces, whole):
    piece = pieces[0].shape[0]
    places = ((y, z), (y, 1 - z), (1 - y, z), (1 - y, 1 - z))
    for p, (a, b) in zip(pieces, places):
        whole[pl.ds(pl.multiple_of((2 * a + b) * piece, piece), piece), :] = p[...]


def write_row(io, whole, row_b, out, k):
    width = whole.shape[1]
    for n in range(row_b.shape[1] // width):
        row_b[:, n * width : (n + 1) * width] = whole[n * width : (n + 1) * width].astype(F32)
    return io.start(row_b, out.at[k])


def final_pair_body(k, n_alias, y_ref, z_ref, p0, p1, p2, p3, *rest):
    row_out, col_out, whole, row_b, col_b, sems = rest[n_alias:]
    io = Copies(sems)
    gather_pieces(y_ref[0], z_ref[0], (p0, p1, p2, p3), whole)
    copies = [write_row(io, whole, row_b, row_out, k)]
    feat = row_b.shape[1]
    col_b[...] = whole[feat : 2 * feat].astype(F32)
    copies.append(io.start(col_b, col_out.at[k // 2]))
    for copy in copies:
        copy.wait()


def final_skip_body(k, n_alias, y_ref, z_ref, p0, p1, p2, p3, *rest):
    row_out, skip_out, whole, row_b, col_b, sems = rest[n_alias:]
    io = Copies(sems)
    gather_pieces(y_ref[0], z_ref[0], (p0, p1, p2, p3), whole)
    copies = [write_row(io, whole, row_b, row_out, k)]
    feat = row_b.shape[1]
    col_b[...] = whole[feat : 2 * feat].astype(F32)
    copies.append(io.start(col_b, skip_out.at[0:feat]))
    for copy in copies:
        copy.wait()


def final_low_body(n_alias, y_ref, z_ref, p0, p1, p2, p3, *rest):
    row_out, skip_out, first, bcol, brow, share, whole, row_b, tail_b, sems = rest[n_alias:]
    io = Copies(sems)
    gather_pieces(y_ref[0], z_ref[0], (p0, p1, p2, p3), whole)
    copies = [write_row(io, whole, row_b, row_out, 0)]
    feat = row_b.shape[1]
    width = whole.shape[1]
    depth = first.shape[0]
    half = share.shape[0]
    share[...] = whole[feat : feat + half]
    tail_b[...] = whole[feat + half :].astype(F32)
    copies.append(io.start(tail_b.at[depth : 2 * depth], skip_out.at[feat : feat + depth]))
    first[...] = tail_b[0:depth]
    bcol[...] = tail_b[2 * depth : 2 * depth + 4]
    blocks = feat // width
    for j in range(4):
        for n in range(blocks):
            at = EXTRA + j * blocks + n
            brow[j : j + 1, n * width : (n + 1) * width] = tail_b[at : at + 1]
    for copy in copies:
        copy.wait()


def unpack_body(i_ref, a, b, g_density, g_bottle, gb_bottle, g_view, gb_view, g_rgb, gb_rgb, g_first, g_rest, gb_prop, g_wpd, packed, sems):
    merge_body(i_ref, a, b, packed)
    feat, width = g_bottle.shape
    vw = g_view.shape[1]
    g_bottle[...] = packed[0:feat].astype(F32)
    g_rest[...] = packed[feat : feat + 3 * width].reshape(3, width, width).astype(F32)
    first_at = feat + 3 * width
    view_at = first_at + g_first.shape[0]
    g_first[...] = packed[first_at:view_at].astype(F32)
    wide = packed[view_at : view_at + 144].astype(F32)
    g_view[0:144] = wide[:, 0:vw]
    g_view[144 : g_view.shape[0]] = wide[0 : g_view.shape[0] - 144, vw : 2 * vw]
    small = packed[view_at + 144 : view_at + 144 + SMALL].astype(F32)
    for n in range(feat // width):
        g_density[:, n * width : (n + 1) * width] = small[n : n + 1, :]
    gb_bottle[...] = small[4:5, :]
    gb_view[...] = small[5:6, 0:vw]
    gb_rgb[...] = small[5:6, vw : vw + 3]
    g_rgb[...] = small[6:9, 0:vw]
    gb_prop[...] = small[9:13, :]
    g_wpd[...] = small[13:14, :]


def ray_masks(count, samples):
    row = lax.broadcasted_iota(jnp.int32, (count, count), 0)
    col = lax.broadcasted_iota(jnp.int32, (count, count), 1)
    same = (row // samples) == (col // samples)
    return row, col, same


def exclusive_sum(depth, samples):
    row, col, same = ray_masks(depth.shape[1], samples)
    mask = jnp.where(same & (row < col), 1.0, 0.0)
    return dot_exact(depth, mask)


def later_sum(carried, samples):
    row, col, same = ray_masks(carried.shape[1], samples)
    mask = jnp.where(same & (row > col), 1.0, 0.0)
    return dot_exact(carried, mask)


def pad_rows(value, rows):
    return jnp.concatenate([value, jnp.zeros((rows - value.shape[0], value.shape[1]), value.dtype)], 0)


def row(ref):
    return ref[...].astype(F32)[None, :]


def spread(value, count):
    rays, samples = value.shape
    lane = lax.broadcasted_iota(jnp.int32, (samples, count), 1) % samples
    pick = jnp.where(lane == lax.broadcasted_iota(jnp.int32, (samples, count), 0), 1.0, 0.0)
    wide = dot_exact(value, pick)
    ray = lax.broadcasted_iota(jnp.int32, (rays, count), 1) // samples
    return jnp.sum(jnp.where(ray == lax.broadcasted_iota(jnp.int32, (rays, count), 0), wide, 0.0), axis=0, keepdims=True)


def heads_body(samples, top_ref, counts, w_density, w_bottle, b_bottle, w_view, b_view, w_rgb3, b_rgb, view_enc, deltas, d_ref, slope_row, colour_ref, gview_ref, gr_ref, weights_ref, gwb_ref, gwv_ref, small_ref):
    top = top_ref[...]
    count = top.shape[0]
    rays = count // samples
    venc = view_enc.shape[1]
    vw = w_view.shape[1]
    w_view_b = w_view.at[0 : w_bottle.shape[1]]
    w_view_v = w_view.at[w_bottle.shape[1] : w_view.shape[0]]
    w8 = pad_rows(row(w_density), 8).astype(BF)
    w_rgb = pad_rows(w_rgb3[...].astype(F32), 8).astype(BF)
    deltas = spread(deltas[...], count)
    raw = dot_nt(w8, top)[0:1]
    sigma = softplus(raw - 1.0)
    bottle = (dot(top, w_bottle[...]) + row(b_bottle)).astype(BF)
    view_rows = jnp.concatenate([jnp.broadcast_to(view_enc[r : r + 1, :].astype(F32), (samples, venc)) for r in range(rays)], 0).astype(BF)
    view_pre = dot(bottle, w_view_b[...]) + dot(view_rows, w_view_v[...]) + row(b_view)
    view_act, view_slope = silu_pair(view_pre)
    lane3 = lax.broadcasted_iota(jnp.int32, (3, 3), 0) == lax.broadcasted_iota(jnp.int32, (3, 3), 1)
    rgb_bias = jnp.sum(jnp.where(lane3, row(b_rgb), 0.0), axis=1, keepdims=True)
    rgb = jax.nn.sigmoid(dot_nt(w_rgb, view_act)[0:3] + rgb_bias)
    place = lax.broadcasted_iota(jnp.int32, (1, count), 1)
    limit = jnp.zeros((1, count), jnp.int32)
    for r in range(rays):
        limit = jnp.where(place // samples == r, counts[r], limit)
    live = place % samples < limit
    depth = jnp.where(live, sigma * deltas, 0.0)
    before = exclusive_sum(depth, samples)
    trans = jnp.exp(-before)
    weights = one_minus_exp(depth) * trans
    weights_ref[...] = weights
    pick = jnp.where(
        lax.broadcasted_iota(jnp.int32, (count, rays), 0) // samples == lax.broadcasted_iota(jnp.int32, (count, rays), 1), 1.0, 0.0
    )
    colour_ref[...] = dot_exact(weights * rgb, pick)
    d = dot_exact(d_ref[...], pick, (((1,), (1,)), ((), ())))
    grad_weights = jnp.sum(d * rgb, axis=0, keepdims=True)
    grad_rgb = (d * weights * rgb * (1.0 - rgb)).astype(BF)
    later = later_sum(grad_weights * weights, samples)
    grad_depth = grad_weights * jnp.exp(-depth) * trans - later
    grad_raw = (jnp.where(live, grad_depth * deltas, 0.0) * jax.nn.sigmoid(raw - 1.0)).astype(BF)
    grad_rgb8 = pad_rows(grad_rgb.astype(F32), 8).astype(BF)
    grad_raw8 = pad_rows(grad_raw.astype(F32), 8).astype(BF)
    grad_view_act = dot_tn(grad_rgb8, w_rgb)
    gvp = (grad_view_act * view_slope).astype(BF)
    g_bias_view = jnp.sum(gvp.astype(F32), axis=0, keepdims=True)
    grad_input = dot_nt(gvp, w_view_b[...])
    grad_bottle = grad_input.astype(BF)
    gview = dot_nt(gvp, w_view_v[...])
    gview_ref[...] = jnp.concatenate(
        [jnp.sum(gview[r * samples : (r + 1) * samples], axis=0, keepdims=True) for r in range(rays)], 0
    )
    gr_ref[...] = ((dot_nt(grad_bottle, w_bottle[...]) + dot_tn(grad_raw8, w8)) * slope_row[...]).astype(BF)
    gwb_ref[...] = dot_tn(top, grad_bottle).astype(BF)
    gwv = jnp.concatenate([dot_tn(bottle, gvp), pad_rows(dot_tn(view_rows, gvp), 32)], 0)
    half = gwv.shape[0] // 2
    gwv_ref[:, 0:vw] = gwv[0:half].astype(BF)
    gwv_ref[:, vw : 2 * vw] = gwv[half : 2 * half].astype(BF)
    width = small_ref.shape[1]
    small_ref[...] = jnp.zeros_like(small_ref)
    gwd = dot(grad_raw8, top)[0:1]
    for n in range(top.shape[1] // width):
        small_ref[n : n + 1, :] = gwd[:, n * width : (n + 1) * width]
    small_ref[4:5, :] = jnp.sum(grad_bottle.astype(F32), axis=0, keepdims=True)
    small_ref[5:6, 0:vw] = g_bias_view
    small_ref[6:9, 0:vw] = dot(grad_rgb8, view_act)[0:3]
    small_ref[5:6, vw : vw + 8] = dot_nt(jnp.ones((8, count), BF), grad_rgb8)[0:1]


def prop_forward_body(prop_in, wp_first, wp_rest, b_prop, wp_density, acts_ref, slopes_ref, raw_ref):
    current = prop_in[...]
    for j in range(4):
        weight = wp_first[...] if j == 0 else wp_rest[j - 1]
        pre = dot(current, weight) if j else dot_tn(current, weight)
        act, slope = silu_pair(pre + b_prop[j : j + 1, :].astype(F32))
        acts_ref[j] = act
        slopes_ref[j] = slope
        current = act
    raw_ref[...] = dot_nt(pad_rows(row(wp_density), 8).astype(BF), current)[0:1]


def prop_backward_body(samples, prop_in, acts, slopes, raw_ref, deltas, bounds, weights_ref, wp_first, wp_rest, wp_density, small_a, c_ref, g_bottle, g_view, gin_ref, keep, send, packed, small_ref, sems):
    io = Copies(sems)
    feat = g_bottle.shape[0]
    width = packed.shape[1]
    rest_at, first_at = feat, feat + 3 * width
    view_at = first_at + prop_in.shape[0]
    small_at = view_at + g_view.shape[0]
    loads = [io.start(g_bottle, packed.at[0:feat]), io.start(g_view, packed.at[view_at:small_at])]
    count = prop_in.shape[1]
    raw = raw_ref[...]
    deltas = spread(deltas[...], count)
    bounds = [spread(bounds[n].astype(F32), count) for n in range(2)]
    weights = weights_ref[...]
    depth = softplus(raw - 1.0) * deltas
    before = exclusive_sum(depth, samples)
    trans = jnp.exp(-before)
    pweights = one_minus_exp(depth) * trans
    at_row, _, same = ray_masks(count, samples)
    place = (at_row % samples).astype(F32)
    inside = jnp.where(same & (place >= bounds[0]) & (place < bounds[1]), 1.0, 0.0)
    bound = dot_exact(pweights, inside)
    excess = jnp.maximum(weights - bound, 0.0)
    grad_bound = -2.0 * excess / (weights + EPS)
    grad_pw = dot_exact(grad_bound, inside, (((1,), (1,)), ((), ())))
    later = later_sum(grad_pw * pweights, samples)
    grad_depth = grad_pw * jnp.exp(-depth) * trans - later
    grad_raw = (grad_depth * deltas * jax.nn.sigmoid(raw - 1.0)).astype(BF)
    raw8 = pad_rows(grad_raw.astype(F32), 8).astype(BF)
    wd8 = pad_rows(row(wp_density), 8).astype(BF)
    small_ref[...] = small_a[...]
    small_ref[13:14, :] = dot(raw8, acts[3])[0:1]
    grad = dot_tn(raw8, wd8)
    for j in (3, 2, 1, 0):
        gpre = (grad * slopes[j]).astype(BF)
        small_ref[9 + j : 10 + j, :] = jnp.sum(gpre.astype(F32), axis=0, keepdims=True)
        if j:
            packed[rest_at + (j - 1) * width : rest_at + j * width] = dot_tn(acts[j - 1], gpre).astype(BF)
            grad = dot_nt(gpre, wp_rest[j - 1])
        else:
            packed[first_at:view_at] = dot(prop_in[...], gpre).astype(BF)
            gin_ref[...] = dot_nt(wp_first[...], gpre)
    packed[small_at : small_at + SMALL] = small_ref[...].astype(BF)
    for load in loads:
        load.wait()
    io.split(packed, c_ref[0], keep, send)


def swap(value, axis, bit):
    size = lax.axis_size(axis)
    return lax.ppermute(value, axis, [(i, i ^ bit) for i in range(size)])


class Order:
    def __init__(self):
        self.token = None

    def enter(self, *values):
        if self.token is None:
            return values
        return lax.optimization_barrier((*values, self.token))[:-1]

    def leave(self, value):
        self.token = value
        return value


def late_bits(start):
    bit = start
    while bit < lax.axis_size("dp"):
        yield bit
        bit *= 2


def add_here(order, mine, came, name):
    mine, came = order.enter(mine, came)
    [out] = kernel(lambda a, b, o, sems: add_body(a, b, o), name, [("w", mine), ("v", came)], [("w", mine.shape, BF)], spare=1)
    return order.leave(out)


def split_here(order, index, mine, came, name):
    mine, came = order.enter(mine, came)
    half = (mine.shape[0] // 2, *mine.shape[1:])
    keep, send = kernel(
        lambda i, a, b, k, s, sems: add_split_body(i, a, b, k, s),
        name,
        [("s", index), ("w", mine), ("v", came)],
        [("w", half, BF), ("v", half, BF)],
        spare=1,
    )
    order.leave(send)
    return keep, send


DIMS = {3: "xyz", 2: "yxz", 1: "xyz", 0: "zxy"}
PLAN = "Q P3 K P2 3 P1 P0 2 1 3 0 2 3 1 2 3 1 0 2 0 3 1 3 2 0 2 1 0 0 1 s s"
WIRES = {"x": ("mp", 2), "y": ("dp", 1), "z": ("dp", 2)}


def reduce_steps(order, name, dims, send, keep, index, finish):
    outer, inner = [d for d in dims if d != "x"]
    came = swap(send, *WIRES[dims[0]])
    yield
    if dims[0] == "x":
        keep, send = split_here(order, index[outer], keep, came, name + "_a")
        came = swap(send, *WIRES[outer])
    else:
        keep, send = split_here(order, index["second"], keep, came, name + "_a")
        came = swap(send, *WIRES["x"])
    yield
    keep, send = split_here(order, index[inner], keep, came, name + "_b")
    came = swap(send, *WIRES[inner])
    yield
    mine = add_here(order, keep, came, name + "_c")
    for bit in late_bits(4):
        came = swap(mine, "dp", bit)
        yield
        mine = add_here(order, mine, came, name + "_far")
    beside = swap(mine, *WIRES[inner])
    across = swap(mine, *WIRES[outer])
    yield
    (beside,) = order.enter(beside)
    corner = swap(beside, *WIRES[outer])
    yield
    finish((outer, inner), (mine, beside, across, corner))


def shared_steps(order, mine, x1, finish):
    came = swap(mine, "mp", 2)
    yield
    mine, came = order.enter(mine, came)
    [mine] = kernel(
        lambda i, a, b, o, sems: merge_body(i, a, b, o),
        "shared_merge",
        [("s", x1), ("v", mine), ("v", came)],
        [("v", (2 * mine.shape[0], mine.shape[1]), BF)],
        spare=1,
    )
    order.leave(mine)
    came = swap(mine, "mp", 1)
    yield
    finish(mine, came)


class Chain:
    def __init__(self, steps):
        self.steps = steps
        self.step()

    def step(self):
        next(self.steps, None)


def on_device(points_in, view_enc, deltas, counts, w_first, w_col, w_skip, w_row, b_col, b_row, w_density, w_bottle, b_bottle, w_view, b_view, w_rgb, b_rgb, prop_in, prop_deltas, bin_bounds, wp_first, wp_rest, b_prop, wp_density, d_colour):
    rows, ipe = points_in.shape
    rays, samples = deltas.shape
    feat = w_row.shape[2]
    width = w_row.shape[1]
    blocks = feat // width
    bottle = w_bottle.shape[1]
    vw = w_view.shape[1]
    venc = view_enc.shape[1]
    dp = lax.axis_index("dp")
    mp = lax.axis_index("mp")

    def scalar(value):
        return jnp.reshape(value, (1,)).astype(jnp.int32)

    one1 = jnp.ones((1,), jnp.int32)
    y1, z1, c1, x1 = scalar(dp % 2), scalar((dp // 2) % 2), scalar(mp % 2), scalar((mp // 2) % 2)
    order = Order()
    mat = (width, feat)
    tall = (feat, width)
    flat = (rows, feat)
    two = (2, rows, width)
    four = (4, rows, width)
    some = (blocks, width, width)
    many = (2 * blocks, width, width)

    message = (EXTRA + feat // 2, width)
    extra, first_half = kernel(
        pack_first_body,
        "pack_first",
        [("s", y1), ("a", w_first), ("a", w_skip), ("v", b_col), ("a", w_row)],
        [("a", (EXTRA, width), BF), ("a", message, BF)],
        [(message, BF)],
        spare=2,
    )
    order.leave(extra)
    hx = {0: swap(first_half, "mp", 2)}
    e1 = swap(extra, "mp", 1)
    pts = points_in.T
    (y1_k,) = order.enter(y1)
    hs = kernel(pack_rest_body, "pack_rest", [("s", y1_k), ("a", w_row), ("a", w_col), ("a", w_skip)], [("a", some, BF)] * 3, [(some, BF)] * 3, spare=2)
    order.leave(hs[0])
    for k in (1, 2, 3):
        hx[k] = swap(hs[k - 1], "mp", 2)
    row_s = swap(w_row, "mp", 1)
    col_s = swap(w_col, "mp", 1)
    skip_s = swap(w_skip, "mp", 1)
    pts_s = swap(pts, "mp", 1)
    own_cols = {1: w_col, 2: w_skip, 3: w_col}
    sib_cols = {1: col_s, 2: skip_s, 3: col_s}

    act02, act13, act_s, slope_col, slope_row, inputs, inputs_s, gathered = {}, {}, {}, {}, {}, {}, {}, {}

    crossed = {}

    def arrive(k):
        (hx[k],) = order.enter(hx[k])
        order.leave(hx[k])
        crossed[k] = swap(hx[k], "dp", 1), swap(hx[k], "mp", 1)

    def complete(k):
        hy, cx = crossed[k]
        (hy,) = order.enter(hy)
        order.leave(hy)
        gathered[k] = (hx[k], hy, cx, swap(hy, "mp", 1))

    arrive(0)
    args = order.enter(pts, extra, e1, hx[0], crossed[0][1])
    act02[0], act13[0], slope_col[0], bias, extras = kernel(
        first_body,
        "first_forward",
        [("v", a) for a in args[:3]] + [("a", a) for a in args[3:]],
        [("a", two, BF), ("a", two, BF), ("a", four, F32), ("v", (4, feat), F32), ("v", (4, EXTRA, width), BF)],
        [(two, BF), (two, BF), (four, F32)],
        spare=4,
    )
    order.leave(bias)
    act_s[0] = swap(act13[0], "mp", 1)
    arrive(1)

    prop_t, wp_first_k = order.enter(prop_in.T, wp_first)
    acts, slopes, prop_raw = kernel(
        lambda *refs: prop_forward_body(*refs[:-1]),
        "prop_forward",
        [("v", prop_t), ("v", wp_first_k), ("v", wp_rest), ("v", b_prop), ("v", wp_density)],
        [("v", (4, rows, bottle), BF), ("v", (4, rows, bottle), F32), ("v", (1, rows), F32)],
        spare=4,
    )
    order.leave(prop_raw)
    complete(0)
    arrive(2)
    b_row_k, a02, a13 = order.enter(b_row, act02[0], act13[0])
    up, slope_row[0] = kernel(
        row0_body,
        "row0_forward",
        [("s", y1), ("v", b_row_k), ("a", a02), ("a", a13), ("a", w_row), ("a", row_s)] + [("a", a) for a in gathered[0]],
        [("a", flat, BF), ("a", flat, F32)],
        [(two, BF), (two, BF), (mat, BF), (mat, BF), (tall, BF), (tall, BF), (flat, BF), (flat, F32)],
        spare=6,
    )
    order.leave(up)
    complete(1)
    arrive(3)
    complete(2)
    weight_bufs = [(mat, BF), (mat, BF), (tall, BF), (tall, BF), (many, BF), (many, BF)]

    def weights_of(k):
        return [("a", a) for a in (w_row, row_s, own_cols[k], sib_cols[k], *gathered[k])]

    for k in (1, 2):
        inputs[k] = up
        inputs_s[k] = swap(up, "mp", 1)
        (b_row_k,) = order.enter(b_row)
        more = [("v", pts), ("v", extras)] if k == 2 else []
        act02[k], act13[k], slope_col[k], up, slope_row[k] = kernel(
            functools.partial(pair_body, k, k == 2),
            f"pair{k}_forward",
            [("s", y1), ("v", bias), ("v", b_row_k)] + more + [("a", inputs[k])] + weights_of(k),
            [("a", two, BF), ("a", two, BF), ("a", four, F32), ("a", flat, BF), ("a", flat, F32)],
            [(flat, BF), *weight_bufs, (two, BF), (two, BF), (four, F32), (flat, BF), (flat, F32)],
            spare=6,
        )
        order.leave(up)
        act_s[k] = swap(act13[k], "mp", 1)

    complete(3)
    inputs[3] = up
    inputs_s[3] = swap(up, "mp", 1)
    grs, gr_s, gc02, gc13, gc_s, bc, dx, brow = {}, {}, {}, {}, {}, {}, {}, {}
    heads_in = (w_density, w_bottle, b_bottle, w_view, b_view, w_rgb.T, b_rgb, view_enc, deltas, d_colour)
    (b_row_k,) = order.enter(b_row)
    got = kernel(
        functools.partial(top_body, 3, samples, len(heads_in)),
        "top",
        [("s", y1), ("s", counts), ("v", bias), ("v", b_row_k)] + [("v", a) for a in heads_in] + [("a", up), ("a", slope_row[2])] + weights_of(3),
        [("a", two, BF), ("a", two, BF), ("a", flat, BF), ("a", two, BF), ("a", two, BF), ("a", flat, BF)]
        + [("v", (3, rays), F32), ("v", (rays, venc), F32), ("v", (1, rows), F32), ("v", (feat, bottle), BF), ("v", (144, 2 * vw), BF), ("v", (SMALL, width), F32)],
        [(flat, BF), (flat, F32), *weight_bufs, (two, BF), (two, BF), (four, F32), (flat, BF), (flat, F32), (flat, BF), (two, BF), (two, BF), (flat, BF)],
    )
    act02[3], act13[3], grs[3], gc02[3], gc13[3], grs[2], colour, grad_view, ray_weights, g_bottle, g_view, small_a = got
    order.leave(grs[2])
    act_s[3] = swap(act13[3], "mp", 1)
    gr_s[3] = swap(grs[3], "mp", 1)
    gc_s[3] = swap(gc13[3], "mp", 1)

    results, chains = {}, {}

    index = {"x": x1, "y": y1, "z": z1, "second": one1}

    def finish(k, halved, pieces):
        pieces = order.enter(*pieces)
        size = (4 * pieces[0].shape[0], width)
        ins = [("s", index[halved[0]]), ("s", index[halved[1]])] + [("v", p) for p in pieces]
        outs = [("a", (4, width, feat), F32)]
        bufs = [(size, BF), (mat, F32)]
        alias = {}

        def in_place(name, index):
            if name in results:
                alias[len(ins)] = index
                ins.append(("a", results[name]))

        in_place("row", 0)
        if k == 2:
            outs.append(("a", (feat + ipe, width), F32))
            bufs.append((tall, F32))
            in_place("skip", 1)
            got = kernel(functools.partial(final_skip_body, k, len(alias)), f"final{k}", ins, outs, bufs, alias, spare=4)
            results["skip"] = got[1]
        elif k:
            outs.append(("a", (2, feat, width), F32))
            bufs.append((tall, F32))
            in_place("col", 1)
            got = kernel(functools.partial(final_pair_body, k, len(alias)), f"final{k}", ins, outs, bufs, alias, spare=4)
            results["col"] = got[1]
        else:
            outs += [("a", (feat + ipe, width), F32), ("v", (ipe, width), F32), ("v", (4, width), F32), ("v", (4, feat), F32), ("v", (512, width), BF)]
            bufs.append(((size[0] - feat - 512, width), F32))
            in_place("skip", 1)
            got = kernel(functools.partial(final_low_body, len(alias)), f"final{k}", ins, outs, bufs, alias, spare=4)
            results["skip"] = got[1]
            results["tail"] = got[2:5]
            chains["s"] = Chain(shared_steps(order, got[5], x1, finish_shared))
        results["row"] = got[0]
        order.leave(got[0])

    def finish_shared(mine, came):
        mine, came = order.enter(mine, came)
        results["shared"] = kernel(
            unpack_body,
            "unpack",
            [("s", c1), ("v", mine), ("v", came)],
            [
                ("v", (1, feat), F32),
                ("v", (feat, bottle), F32),
                ("v", (1, bottle), F32),
                ("v", (bottle + venc, vw), F32),
                ("v", (1, vw), F32),
                ("v", (3, vw), F32),
                ("v", (1, 3), F32),
                ("v", (ipe, bottle), F32),
                ("v", (3, bottle, bottle), F32),
                ("v", (4, bottle), F32),
                ("v", (1, bottle), F32),
            ],
            [((2048, bottle), BF)],
            spare=4,
        )
        order.leave(results["shared"][0])

    def send_away(k):
        dims = DIMS[k]
        folded = dims[0] != "x"
        kind = {3: "plain", 2: "points", 1: "plain", 0: "low"}[k]
        args = [act02[k], act_s[k], grs[k], gr_s[k], gc02[k], gc_s[k]] + ([inputs[k], inputs_s[k]] if k else [])
        args = order.enter(*args)
        height = feat + 512 + 256 if kind == "low" else 2 * feat
        small = [("s", index[dims[0]])] if folded else []
        if kind == "low":
            small += [("s", x1)]
        if kind != "plain":
            small += [("v", pts), ("v", pts_s)]
        if kind == "low":
            small += [("v", keep_h), ("v", came_h)]
            small += [("v", bc[1]), ("v", bc[2]), ("v", bc[3]), ("v", dx[2]), ("v", brow[1]), ("v", brow[2]), ("v", brow[3])]
        outs = [("a", (height, width), BF), ("w", (height, width), BF)]
        if kind != "low":
            outs += [("v", (2, width), F32), ("v", (blocks, width), F32)]
        if kind == "points":
            outs.append(("v", (2, ipe, width), F32))
        bufs = [(two, BF), (two, BF), (flat, BF), (flat, BF), (two, BF), (two, BF)] + ([(flat, BF), (flat, BF)] if k else [])
        out, home, *rest = kernel(
            functools.partial(products_body, kind, folded), f"products{k}", small + [("a", a) for a in args], outs, bufs + [((height, width), BF)] * 2, spare=6
        )
        if rest:
            bc[k], brow[k] = rest[:2]
        if kind == "points":
            dx[k] = rest[2]
        order.leave(out)
        chains[str(k)] = Chain(reduce_steps(order, f"sum{k}", dims, out, home, index, functools.partial(finish, k)))

    def prop_backward():
        nonlocal grad_prop_in, keep_h, came_h
        prop_args = order.enter(prop_t, acts, slopes, prop_raw, prop_deltas, bin_bounds, ray_weights, wp_first, wp_rest, wp_density, small_a, c1, g_bottle, g_view)
        grad_prop_in, keep_h, send_h = kernel(
            functools.partial(prop_backward_body, samples),
            "prop_backward",
            [("s" if n == 11 else "a" if n > 11 else "v", a) for n, a in enumerate(prop_args)],
            [("v", (ipe, rows), F32), ("a", (1024, bottle), BF), ("a", (1024, bottle), BF)],
            [((2048, bottle), BF), ((SMALL, width), F32)],
            spare=6,
        )
        order.leave(send_h)
        came_h = swap(send_h, "mp", 1)

    def chain_backward():
        nonlocal grad_points
        args = order.enter(grs[2], slope_col[2], slope_col[1], slope_col[0], slope_row[1], slope_row[0])
        got = kernel(
            chain_body,
            "chain",
            [("s", y1), ("v", extras)]
            + [("a", a) for a in args]
            + weights_of(2)
            + weights_of(1)
            + [("a", a) for a in (w_row, row_s, *gathered[0])],
            [("a", two, BF)] * 6 + [("a", flat, BF)] * 2 + [("v", (ipe, rows), F32)],
            [(flat, BF)] * 3 + [(four, F32)] * 3 + [(flat, F32)] * 2 + weight_bufs + weight_bufs + [(mat, BF)] * 2 + [(tall, BF)] * 2 + [(two, BF)] * 6,
            spare=6,
        )
        gc02[2], gc02[1], gc02[0], gc13[2], gc13[1], gc13[0], grs[1], grs[0], grad_points = got
        order.leave(grad_points)
        for k in (2, 1, 0):
            gr_s[k] = swap(grs[k], "mp", 1)
            gc_s[k] = swap(gc13[k], "mp", 1)

    grad_prop_in = keep_h = came_h = grad_points = None
    for item in PLAN.split():
        if item == "Q":
            prop_backward()
        elif item == "K":
            chain_backward()
        elif item[0] == "P":
            send_away(int(item[1]))
        elif item in chains:
            chains[item].step()
    for item in ("3", "2", "1", "0", "s"):
        for _ in range(16):
            chains[item].step()

    g_density, g_bottle, gb_bottle, g_view, gb_view, g_rgb, gb_rgb, g_first, g_rest, gb_prop, g_wpd = results["shared"]
    first, bcol, brow_out = results["tail"]
    return (
        colour,
        grad_points.T,
        grad_view,
        grad_prop_in.T,
        first,
        results["col"],
        results["skip"],
        results["row"],
        bcol,
        brow_out,
        g_density.reshape(feat),
        g_bottle,
        gb_bottle.reshape(bottle),
        g_view,
        gb_view.reshape(vw),
        g_rgb.T,
        gb_rgb.reshape(3),
        g_first,
        g_rest,
        gb_prop,
        g_wpd.reshape(bottle),
    )


def solution(mesh):
    both = ("dp", "mp")
    placed = (
        P(both, None),
        P(both, None),
        P(both, None),
        P(both),
        P(None, "mp"),
        P(None, None, "mp"),
        P(None, "mp"),
        P(None, "mp", None),
        P(None, "mp"),
        *([P()] * 8),
        P(both, None),
        P(both, None),
        P(None, both, None),
        P(),
        P(),
        P(),
        P(),
        P(None, both),
    )
    return jax.shard_map(
        on_device,
        mesh=mesh,
        in_specs=placed,
        out_specs=(
            P(None, both),
            P(both, None),
            P(both, None),
            P(both, None),
            P(None, "mp"),
            P(None, None, "mp"),
            P(None, "mp"),
            P(None, "mp", None),
            P(None, "mp"),
            *([P()] * 12),
        ),
        check_vma=False,
    )
```

```python
import functools

import jax
import jax.numpy as jnp
from jax import lax
from jax.experimental import pallas as pl
from jax.experimental.pallas import tpu as pltpu
from jax.sharding import PartitionSpec as P

EPS = 0.0001
BF = jnp.bfloat16
F32 = jnp.float32
HIGH = lax.Precision.HIGHEST
COPIES = 48
EXTRA = 208
SMALL = 16


def dot(a, b):
    return jnp.dot(a, b, preferred_element_type=F32)


def dot_nt(a, b):
    return lax.dot_general(a, b, (((1,), (1,)), ((), ())), preferred_element_type=F32)


def dot_tn(a, b):
    return lax.dot_general(a, b, (((0,), (0,)), ((), ())), preferred_element_type=F32)


def dot_exact(a, b, dims=(((1,), (0,)), ((), ()))):
    return lax.dot_general(a, b, dims, precision=HIGH, preferred_element_type=F32)


def silu_pair(pre):
    gate = 0.5 + 0.5 * jnp.tanh(0.5 * pre)
    return (pre * gate).astype(BF), gate * (1.0 + pre * (1.0 - gate))


def softplus(v):
    tail = jnp.exp(-jnp.abs(v))
    series = tail * (1.0 - tail * (1.0 / 2 - tail * (1.0 / 3 - tail * (1.0 / 4 - tail * (1.0 / 5)))))
    return jnp.maximum(v, 0.0) + jnp.where(tail < 0.03, series, jnp.log(1.0 + tail))


def one_minus_exp(depth):
    nested = 1.0
    for n in (8, 7, 6, 5, 4, 3, 2):
        nested = 1.0 - depth * (1.0 / n) * nested
    return jnp.where(depth < 0.25, depth * nested, 1.0 - jnp.exp(-depth))


class Copies:
    def __init__(self, sems):
        self.sems = sems
        self.count = 0

    def start(self, source, target):
        copy = pltpu.make_async_copy(source, target, self.sems.at[self.count])
        self.count += 1
        copy.start()
        return copy

    def split(self, whole, index, keep, send):
        half = whole.shape[0] // 2
        at = pl.multiple_of(index * half, half)
        other = pl.multiple_of((1 - index) * half, half)
        one = self.start(whole.at[pl.ds(other, half)], send)
        two = self.start(whole.at[pl.ds(at, half)], keep)
        one.wait()
        two.wait()


def size_of(shape, dtype):
    total = jnp.dtype(dtype).itemsize
    for extent in shape:
        total *= extent
    return total


def kernel(body, name, ins, outs, bufs=(), alias=None, spare=10):
    spaces = {"s": pltpu.SMEM, "v": pltpu.VMEM, "w": pltpu.VMEM, "a": pltpu.HBM, "n": pl.ANY}
    held = [(a.shape, a.dtype) for kind, a in ins if kind == "v"] + [o[1:] for o in outs if o[0] == "v"] + list(bufs)
    grant = spare * 1024 * 1024 + sum(2 * size_of(*h) if h[0][-1] < 128 else size_of(*h) for h in held)
    shapes = {"v": jax.ShapeDtypeStruct, "w": pltpu.VMEM, "a": pltpu.HBM}

    def placed(kind, array):
        return pltpu.with_memory_space_constraint(array, spaces[kind]) if kind in "aw" else array

    return pl.pallas_call(
        body,
        out_shape=[shapes[kind](shape, dtype) for kind, shape, dtype in outs],
        in_specs=[pl.BlockSpec(memory_space=spaces[kind]) for kind, _ in ins],
        out_specs=[pl.BlockSpec(memory_space=spaces[kind]) for kind, _, _ in outs],
        scratch_shapes=[pltpu.VMEM(shape, dtype) for shape, dtype in bufs] + [pltpu.SemaphoreType.DMA((COPIES,))],
        input_output_aliases=alias or {},
        compiler_params=pltpu.CompilerParams(vmem_limit_bytes=grant),
        cost_estimate=pl.CostEstimate(flops=1, bytes_accessed=1, transcendentals=0),
        name=name,
    )(*[placed(kind, array) for kind, array in ins])


def pack_first_body(y_ref, w_first, w_skip, b_col, w_row, extra, message, whole, sems):
    io = Copies(sems)
    depth, width = w_first.shape
    count = (message.shape[0] - EXTRA) // width
    tail = w_skip.shape[0] - depth
    copies = [
        io.start(w_row.at[0, :, pl.ds(pl.multiple_of((y_ref[0] * count + n) * width, width), width)], whole.at[EXTRA + n * width : EXTRA + (n + 1) * width])
        for n in range(count)
    ]
    copies.append(io.start(w_first, whole.at[0:depth]))
    copies.append(io.start(w_skip.at[tail : tail + depth], whole.at[depth : 2 * depth]))
    whole[2 * depth : EXTRA] = jnp.concatenate([b_col[...].astype(F32), jnp.zeros((EXTRA - 2 * depth - 4, width), F32)], 0).astype(BF)
    for copy in copies:
        copy.wait()
    copies = [io.start(whole, message), io.start(whole.at[0:EXTRA], extra)]
    for copy in copies:
        copy.wait()


def pack_rest_body(y_ref, w_row, w_col, w_skip, h1, h2, h3, b1, b2, b3, sems):
    io = Copies(sems)
    count, width = b1.shape[0], b1.shape[1]
    outs = ((b1, h1), (b2, h2), (b3, h3))

    def move(source):
        io.count = 0
        groups = [[io.start(source(k + 1, n), buf.at[n]) for n in range(count)] for k, (buf, _) in enumerate(outs)]
        last = []
        for group, (buf, out) in zip(groups, outs):
            for copy in group:
                copy.wait()
            last.append(io.start(buf, out))
        for copy in last:
            copy.wait()

    @pl.when(y_ref[0] == 0)
    def rows():
        move(lambda k, n: w_row.at[k, :, n * width : (n + 1) * width])

    @pl.when(y_ref[0] != 0)
    def columns():
        move(lambda k, n: (w_skip if k == 2 else w_col.at[k // 2]).at[n * width : (n + 1) * width])


class Weights:
    def __init__(self, io, k, y, refs, bufs, rows_first=False):
        own_row, sib_row, own_col, sib_col, hx, hy, cx, cy = refs
        row0, row1, col0, col1, far2, far3 = bufs
        self.bufs = bufs
        self.width = row0.shape[0]
        self.blocks = row0.shape[1] // self.width
        half = far2.shape[0] // 2
        at, other = pl.multiple_of(y * half, half), pl.multiple_of((1 - y) * half, half)
        col_of = (lambda ref: ref.at[0 : self.blocks * self.width]) if k == 2 else (lambda ref: ref.at[k // 2])
        pairs = {
            ("col", 0): [(col_of(own_col), col0)],
            ("col", 1): [(col_of(sib_col), col1)],
            ("far", 2): [(hx, far2.at[pl.ds(at, half)]), (hy, far2.at[pl.ds(other, half)])],
            ("far", 3): [(cx, far3.at[pl.ds(at, half)]), (cy, far3.at[pl.ds(other, half)])],
            ("row", 0): [(own_row.at[k], row0)],
            ("row", 1): [(sib_row.at[k], row1)],
        }
        near, late = (("row", "col") if rows_first else ("col", "row"))
        keys = [(near, 1), (near, 0), ("far", 3), ("far", 2), (late, 1), (late, 0)]
        self.waits = {key: [io.start(*pair) for pair in pairs[key]] for key in keys}

    def ready(self, *key):
        for copy in self.waits.pop(key, ()):
            copy.wait()

    def col(self, j):
        self.ready("col" if j < 2 else "far", j)
        if j < 2:
            return self.bufs[2 + j][...]
        return self.bufs[2 + j][self.blocks : 2 * self.blocks].reshape(self.blocks * self.width, self.width)

    def row(self, j, n):
        self.ready("row" if j < 2 else "far", j)
        if j < 2:
            return self.bufs[j][:, n * self.width : (n + 1) * self.width]
        return self.bufs[2 + j][n]


class FirstWeights:
    def __init__(self, io, y, refs, bufs):
        own_row, sib_row, hx, hy, cx, cy = refs
        self.bufs = bufs
        self.width = bufs[0].shape[0]
        half = bufs[2].shape[0] // 2
        at, other = pl.multiple_of(y * half, half), pl.multiple_of((1 - y) * half, half)
        rows = slice(EXTRA, EXTRA + half)
        self.waits = {
            1: [io.start(sib_row.at[0], bufs[1])],
            0: [io.start(own_row.at[0], bufs[0])],
            3: [io.start(cx.at[rows], bufs[3].at[pl.ds(at, half)]), io.start(cy.at[rows], bufs[3].at[pl.ds(other, half)])],
            2: [io.start(hx.at[rows], bufs[2].at[pl.ds(at, half)]), io.start(hy.at[rows], bufs[2].at[pl.ds(other, half)])],
        }

    def row(self, j, n):
        for copy in self.waits.pop(j, ()):
            copy.wait()
        cols = slice(n * self.width, (n + 1) * self.width)
        return self.bufs[j][:, cols] if j < 2 else self.bufs[j][cols]


def put_block(j, value, even, odd):
    (odd if j % 2 else even)[j // 2] = value


def get_block(j, even, odd):
    return (odd if j % 2 else even)[j // 2]


def first_body(pts, e0, e1, m2, m3, act02, act13, slope_ref, bias_ref, extras, acts, acts13, slopes, sems):
    io = Copies(sems)
    loads = [io.start(m2.at[0:EXTRA], extras.at[2]), io.start(m3.at[0:EXTRA], extras.at[3])]
    extras[0] = e0[...]
    extras[1] = e1[...]
    depth, width = pts.shape[0], e0.shape[1]
    for load in loads:
        load.wait()
    for j in range(4):
        bias_ref[:, j * width : (j + 1) * width] = extras[j, 2 * depth : 2 * depth + 4, :].astype(F32)
    outs = []
    for j in (1, 3, 0, 2):
        act, slope = silu_pair(dot_tn(pts[...], extras[j, 0:depth, :]) + bias_ref[0:1, j * width : (j + 1) * width])
        put_block(j, act, acts, acts13)
        slopes[j] = slope
        if j == 3:
            outs.append(io.start(acts13, act13))
    outs += [io.start(acts, act02), io.start(slopes, slope_ref)]
    for copy in outs:
        copy.wait()


def row_forward(weights, k, acts, acts13, b_row, up, slopes):
    width = acts.shape[1]
    for n in range(up.shape[1] // width):
        cols = slice(n * width, (n + 1) * width)
        pre = b_row[k : k + 1, cols].astype(F32)
        for j in (3, 2, 1, 0):
            pre = pre + dot(get_block(j, acts, acts13), weights.row(j, n))
        act, slope = silu_pair(pre)
        up[:, cols] = act
        slopes[:, cols] = slope


def row0_body(y_ref, b_row, act02, act13, own, sib, hx, hy, cx, cy, up_ref, slope_ref, acts, acts13, w0, w1, w2, w3, up, slopes, sems):
    io = Copies(sems)
    loads = [io.start(act02, acts), io.start(act13, acts13)]
    weights = FirstWeights(io, y_ref[0], (own, sib, hx, hy, cx, cy), (w0, w1, w2, w3))
    for load in loads:
        load.wait()
    row_forward(weights, 0, acts, acts13, b_row, up, slopes)
    outs = [io.start(up, up_ref), io.start(slopes, slope_ref)]
    for copy in outs:
        copy.wait()


def col_forward(weights, k, value, bias, pts, extras, acts, acts13, slopes):
    width = acts.shape[1]
    for j in (1, 0, 3, 2):
        pre = dot(value, weights.col(j)) + bias[k : k + 1, j * width : (j + 1) * width]
        if extras is not None:
            depth = pts.shape[0]
            pre = pre + dot_tn(pts[...], extras[j, depth : 2 * depth, :])
        act, slope = silu_pair(pre)
        put_block(j, act, acts, acts13)
        slopes[j] = slope


def pair_body(k, skip, y_ref, bias, b_row, *rest):
    rest = list(rest)
    pts = rest.pop(0) if skip else None
    extras = rest.pop(0) if skip else None
    u, own_row, sib_row, own_col, sib_col, hx, hy, cx, cy, act02, act13, slope_col, up_ref, slope_row, u_buf, w0, w1, w2, w3, w4, w5, acts, acts13, slopes_c, up, slopes_r, sems = rest
    io = Copies(sems)
    load = io.start(u, u_buf)
    weights = Weights(io, k, y_ref[0], (own_row, sib_row, own_col, sib_col, hx, hy, cx, cy), (w0, w1, w2, w3, w4, w5))
    load.wait()
    col_forward(weights, k, u_buf[...], bias, pts, extras, acts, acts13, slopes_c)
    outs = [io.start(acts13, act13), io.start(acts, act02), io.start(slopes_c, slope_col)]
    row_forward(weights, k, acts, acts13, b_row, up, slopes_r)
    outs += [io.start(up, up_ref), io.start(slopes_r, slope_row)]
    for copy in outs:
        copy.wait()


def chain_step(weights, gr, slope_col, slope_row, pts_depth, extras, gcs, gcs13, gru, gp):
    width = gcs.shape[1]
    blocks = gr.shape[1] // width
    for j in (1, 0, 3, 2):
        gca = dot_nt(gr[:, 0:width], weights.row(j, 0))
        for n in range(1, blocks):
            gca += dot_nt(gr[:, n * width : (n + 1) * width], weights.row(j, n))
        put_block(j, (gca * slope_col[j]).astype(BF), gcs, gcs13)
    if gru is not None:
        gu = None
        for j in (1, 0, 3, 2):
            step = dot_nt(get_block(j, gcs, gcs13), weights.col(j))
            gu = step if gu is None else gu + step
        gru[...] = (gu * slope_row[...]).astype(BF)
    if extras is not None:
        at = pts_depth if gru is not None else 0
        for j in (1, 0, 3, 2):
            gp = gp + dot_nt(extras[j, at : at + pts_depth, :], get_block(j, gcs, gcs13))
    return gp


def top_body(k, samples, n_heads, y_ref, counts, bias, b_row, *rest):
    rest = list(rest)
    heads_in = [rest.pop(0) for _ in range(n_heads)]
    u, slope_row, own_row, sib_row, own_col, sib_col, hx, hy, cx, cy, act02, act13, gr_ref, gc02, gc13, gr_low, colour_ref, gview_ref, weights_ref, gwb_ref, gwv_ref, small_ref, u_buf, sr_buf, w0, w1, w2, w3, w4, w5, acts, acts13, slopes_c, up, slopes_r, gr, gcs, gcs13, gru, sems = rest
    io = Copies(sems)
    load = io.start(u, u_buf)
    weights = Weights(io, k, y_ref[0], (own_row, sib_row, own_col, sib_col, hx, hy, cx, cy), (w0, w1, w2, w3, w4, w5))
    late = io.start(slope_row, sr_buf)
    load.wait()
    col_forward(weights, k, u_buf[...], bias, None, None, acts, acts13, slopes_c)
    outs = [io.start(acts13, act13), io.start(acts, act02)]
    row_forward(weights, k, acts, acts13, b_row, up, slopes_r)
    heads_body(samples, up, counts, *heads_in, slopes_r, colour_ref, gview_ref, gr, weights_ref, gwb_ref, gwv_ref, small_ref)
    outs.append(io.start(gr, gr_ref))
    late.wait()
    chain_step(weights, gr, slopes_c, sr_buf, 0, None, gcs, gcs13, gru, None)
    outs += [io.start(gcs13, gc13), io.start(gcs, gc02), io.start(gru, gr_low)]
    for copy in outs:
        copy.wait()


def chain_body(y_ref, extras, *rest):
    rest = list(rest)
    gr2_in = rest.pop(0)
    slopes_c = {k: rest.pop(0) for k in (2, 1, 0)}
    slopes_r = {k: rest.pop(0) for k in (1, 0)}
    refs = {k: [rest.pop(0) for _ in range(8)] for k in (2, 1)}
    refs[0] = [rest.pop(0) for _ in range(6)]
    gc02 = {k: rest.pop(0) for k in (2, 1, 0)}
    gc13 = {k: rest.pop(0) for k in (2, 1, 0)}
    gr_out = {k: rest.pop(0) for k in (1, 0)}
    gp_ref = rest.pop(0)
    gr = {k: rest.pop(0) for k in (2, 1, 0)}
    sc = {k: rest.pop(0) for k in (2, 1, 0)}
    sr = {k: rest.pop(0) for k in (1, 0)}
    bufs = {k: [rest.pop(0) for _ in range(6)] for k in (2, 1)}
    bufs[0] = [rest.pop(0) for _ in range(4)]
    gcs = {k: rest.pop(0) for k in (2, 1, 0)}
    gcs13 = {k: rest.pop(0) for k in (2, 1, 0)}
    (sems,) = rest
    io = Copies(sems)
    y = y_ref[0]
    weights, loads = {}, {}
    for k in (2, 1, 0):
        loads[k] = [io.start(slopes_c[k], sc[k])]
        if k == 2:
            loads[k].append(io.start(gr2_in, gr[2]))
        weights[k] = Weights(io, k, y, refs[k], bufs[k], rows_first=True) if k else FirstWeights(io, y, refs[k], bufs[k])
        if k:
            loads[k].append(io.start(slopes_r[k - 1], sr[k - 1]))
    depth = gp_ref.shape[0]
    gp = jnp.zeros(gp_ref.shape, F32)
    outs = []
    for k in (2, 1, 0):
        for load in loads[k]:
            load.wait()
        gp = chain_step(weights[k], gr[k], sc[k], sr.get(k - 1), depth, extras if k != 1 else None, gcs[k], gcs13[k], gr.get(k - 1), gp)
        outs += [io.start(gcs13[k], gc13[k]), io.start(gcs[k], gc02[k])]
        if k:
            outs.append(io.start(gr[k - 1], gr_out[k - 1]))
    gp_ref[...] = gp
    for copy in outs:
        copy.wait()


def row_sum(value):
    return jnp.sum(value.astype(F32), axis=0, keepdims=True)


def products_body(kind, folded, *rest):
    rest = list(rest)
    pair = kind != "low"
    i_ref = rest.pop(0) if folded else None
    x_ref = rest.pop(0) if kind == "low" else None
    points = kind != "plain"
    if points:
        pts, pts_s = rest.pop(0), rest.pop(0)
    if kind == "low":
        keep_h, came_h = rest.pop(0), rest.pop(0)
        bcs = [rest.pop(0) for _ in range(3)]
        dx2 = rest.pop(0)
        brs = [rest.pop(0) for _ in range(3)]
    act, act_s, gr, gr_s, gc, gc_s = [rest.pop(0) for _ in range(6)]
    if pair:
        u, u_s = rest.pop(0), rest.pop(0)
    away, home = rest.pop(0), rest.pop(0)
    if kind != "low":
        bc_ref, brow_ref = rest.pop(0), rest.pop(0)
    if kind == "points":
        dx_ref = rest.pop(0)
    act_b, act_sb, gr_b, gr_sb, gc_b, gc_sb = [rest.pop(0) for _ in range(6)]
    if pair:
        u_b, u_sb = rest.pop(0), rest.pop(0)
    if folded:
        away_b, home_b = rest.pop(0), rest.pop(0)
    (sems,) = rest
    io = Copies(sems)
    loads = [io.start(a, b) for a, b in ((act, act_b), (act_s, act_sb), (gr, gr_b), (gr_s, gr_sb), (gc, gc_b), (gc_s, gc_sb))]
    more = [io.start(u, u_b), io.start(u_s, u_sb)] if pair else []
    for load in loads:
        load.wait()
    width = act_b.shape[2]
    feat = gr_b.shape[1]
    blocks = feat // width
    outs = []
    dx = {}
    bc = {}
    if not folded:
        away_b, home_b = away, home
    for slot, out_b, out in ((1, away_b, away), (0, home_b, home)):
        for n in range(blocks):
            cols = slice(n * width, (n + 1) * width)
            out_b[n * width : (n + 1) * width] = (dot_tn(act_b[slot], gr_b[:, cols]) + dot_tn(act_sb[slot], gr_sb[:, cols])).astype(BF)
        for load in more:
            load.wait()
        more = []
        if pair:
            out_b[feat : 2 * feat] = (dot_tn(u_b[...], gc_b[slot]) + dot_tn(u_sb[...], gc_sb[slot])).astype(BF)
        bc[slot] = row_sum(gc_b[slot]) + row_sum(gc_sb[slot])
        if points:
            dx[slot] = dot(pts[...], gc_b[slot]) + dot(pts_s[...], gc_sb[slot])
        if kind == "low":
            half = keep_h.shape[0] // 2
            index = x_ref[0] if slot == 0 else 1 - x_ref[0]
            at = pl.ds(pl.multiple_of(index * half, half), half)
            out_b[feat : feat + half] = (keep_h[at, :].astype(F32) + came_h[at, :].astype(F32)).astype(BF)
            depth = pts.shape[0]
            parts = [dx[slot], dx2[slot], bc[slot]] + [b[slot : slot + 1, :] for b in bcs]
            parts.append(jnp.zeros((EXTRA - 2 * depth - 4, width), F32))
            brow = jnp.concatenate([row_sum(gr_b[:, n * width : (n + 1) * width]) + row_sum(gr_sb[:, n * width : (n + 1) * width]) for n in range(blocks)], 0)
            parts += [brow] + [br[...] for br in brs]
            tail = jnp.concatenate(parts, 0)
            pad = out_b.shape[0] - feat - half - tail.shape[0]
            out_b[feat + half :] = jnp.concatenate([tail, jnp.zeros((pad, width), F32)], 0).astype(BF)
        if not folded:
            continue
        half = out_b.shape[0] // 2
        at = pl.multiple_of(i_ref[0] * half, half)
        other = pl.multiple_of((1 - i_ref[0]) * half, half)
        rows = slice(0, half) if slot else slice(half, 2 * half)
        outs.append(io.start(out_b.at[pl.ds(other, half)], away.at[rows]))
        outs.append(io.start(out_b.at[pl.ds(at, half)], home.at[rows]))
    if kind != "low":
        for slot in range(2):
            bc_ref[slot : slot + 1, :] = bc[slot]
            if kind == "points":
                dx_ref[slot] = dx[slot]
        for n in range(blocks):
            cols = slice(n * width, (n + 1) * width)
            brow_ref[n : n + 1, :] = row_sum(gr_b[:, cols]) + row_sum(gr_sb[:, cols])
    for copy in outs:
        copy.wait()


def add_body(a, b, out):
    out[...] = (a[...].astype(F32) + b[...].astype(F32)).astype(BF)


def add_split_body(i_ref, a, b, keep, send):
    half = keep.shape[0]
    at = pl.ds(pl.multiple_of(i_ref[0] * half, half), half)
    other = pl.ds(pl.multiple_of((1 - i_ref[0]) * half, half), half)
    send[...] = (a[other, :].astype(F32) + b[other, :].astype(F32)).astype(BF)
    keep[...] = (a[at, :].astype(F32) + b[at, :].astype(F32)).astype(BF)


def merge_body(i_ref, a, b, out):
    half = a.shape[0]
    out[pl.ds(pl.multiple_of(i_ref[0] * half, half), half), :] = a[...]
    out[pl.ds(pl.multiple_of((1 - i_ref[0]) * half, half), half), :] = b[...]


def gather_pieces(y, z, pieces, whole):
    piece = pieces[0].shape[0]
    places = ((y, z), (y, 1 - z), (1 - y, z), (1 - y, 1 - z))
    for p, (a, b) in zip(pieces, places):
        whole[pl.ds(pl.multiple_of((2 * a + b) * piece, piece), piece), :] = p[...]


def write_row(io, whole, row_b, out, k):
    width = whole.shape[1]
    for n in range(row_b.shape[1] // width):
        row_b[:, n * width : (n + 1) * width] = whole[n * width : (n + 1) * width].astype(F32)
    return io.start(row_b, out.at[k])


def final_pair_body(k, n_alias, y_ref, z_ref, p0, p1, p2, p3, *rest):
    row_out, col_out, whole, row_b, col_b, sems = rest[n_alias:]
    io = Copies(sems)
    gather_pieces(y_ref[0], z_ref[0], (p0, p1, p2, p3), whole)
    copies = [write_row(io, whole, row_b, row_out, k)]
    feat = row_b.shape[1]
    col_b[...] = whole[feat : 2 * feat].astype(F32)
    copies.append(io.start(col_b, col_out.at[k // 2]))
    for copy in copies:
        copy.wait()


def final_skip_body(k, n_alias, y_ref, z_ref, p0, p1, p2, p3, *rest):
    row_out, skip_out, whole, row_b, col_b, sems = rest[n_alias:]
    io = Copies(sems)
    gather_pieces(y_ref[0], z_ref[0], (p0, p1, p2, p3), whole)
    copies = [write_row(io, whole, row_b, row_out, k)]
    feat = row_b.shape[1]
    col_b[...] = whole[feat : 2 * feat].astype(F32)
    copies.append(io.start(col_b, skip_out.at[0:feat]))
    for copy in copies:
        copy.wait()


def final_low_body(n_alias, y_ref, z_ref, p0, p1, p2, p3, *rest):
    row_out, skip_out, first, bcol, brow, share, whole, row_b, tail_b, sems = rest[n_alias:]
    io = Copies(sems)
    gather_pieces(y_ref[0], z_ref[0], (p0, p1, p2, p3), whole)
    copies = [write_row(io, whole, row_b, row_out, 0)]
    feat = row_b.shape[1]
    width = whole.shape[1]
    depth = first.shape[0]
    half = share.shape[0]
    share[...] = whole[feat : feat + half]
    tail_b[...] = whole[feat + half :].astype(F32)
    copies.append(io.start(tail_b.at[depth : 2 * depth], skip_out.at[feat : feat + depth]))
    first[...] = tail_b[0:depth]
    bcol[...] = tail_b[2 * depth : 2 * depth + 4]
    blocks = feat // width
    for j in range(4):
        for n in range(blocks):
            at = EXTRA + j * blocks + n
            brow[j : j + 1, n * width : (n + 1) * width] = tail_b[at : at + 1]
    for copy in copies:
        copy.wait()


def unpack_body(i_ref, a, b, g_density, g_bottle, gb_bottle, g_view, gb_view, g_rgb, gb_rgb, g_first, g_rest, gb_prop, g_wpd, packed, sems):
    merge_body(i_ref, a, b, packed)
    feat, width = g_bottle.shape
    vw = g_view.shape[1]
    g_bottle[...] = packed[0:feat].astype(F32)
    g_rest[...] = packed[feat : feat + 3 * width].reshape(3, width, width).astype(F32)
    first_at = feat + 3 * width
    view_at = first_at + g_first.shape[0]
    g_first[...] = packed[first_at:view_at].astype(F32)
    wide = packed[view_at : view_at + 144].astype(F32)
    g_view[0:144] = wide[:, 0:vw]
    g_view[144 : g_view.shape[0]] = wide[0 : g_view.shape[0] - 144, vw : 2 * vw]
    small = packed[view_at + 144 : view_at + 144 + SMALL].astype(F32)
    for n in range(feat // width):
        g_density[:, n * width : (n + 1) * width] = small[n : n + 1, :]
    gb_bottle[...] = small[4:5, :]
    gb_view[...] = small[5:6, 0:vw]
    gb_rgb[...] = small[5:6, vw : vw + 3]
    g_rgb[...] = small[6:9, 0:vw]
    gb_prop[...] = small[9:13, :]
    g_wpd[...] = small[13:14, :]


def ray_masks(count, samples):
    row = lax.broadcasted_iota(jnp.int32, (count, count), 0)
    col = lax.broadcasted_iota(jnp.int32, (count, count), 1)
    same = (row // samples) == (col // samples)
    return row, col, same


def exclusive_sum(depth, samples):
    row, col, same = ray_masks(depth.shape[1], samples)
    mask = jnp.where(same & (row < col), 1.0, 0.0)
    return dot_exact(depth, mask)


def later_sum(carried, samples):
    row, col, same = ray_masks(carried.shape[1], samples)
    mask = jnp.where(same & (row > col), 1.0, 0.0)
    return dot_exact(carried, mask)


def pad_rows(value, rows):
    return jnp.concatenate([value, jnp.zeros((rows - value.shape[0], value.shape[1]), value.dtype)], 0)


def row(ref):
    return ref[...].astype(F32)[None, :]


def spread(value, count):
    rays, samples = value.shape
    lane = lax.broadcasted_iota(jnp.int32, (samples, count), 1) % samples
    pick = jnp.where(lane == lax.broadcasted_iota(jnp.int32, (samples, count), 0), 1.0, 0.0)
    wide = dot_exact(value, pick)
    ray = lax.broadcasted_iota(jnp.int32, (rays, count), 1) // samples
    return jnp.sum(jnp.where(ray == lax.broadcasted_iota(jnp.int32, (rays, count), 0), wide, 0.0), axis=0, keepdims=True)


def heads_body(samples, top_ref, counts, w_density, w_bottle, b_bottle, w_view, b_view, w_rgb3, b_rgb, view_enc, deltas, d_ref, slope_row, colour_ref, gview_ref, gr_ref, weights_ref, gwb_ref, gwv_ref, small_ref):
    top = top_ref[...]
    count = top.shape[0]
    rays = count // samples
    venc = view_enc.shape[1]
    vw = w_view.shape[1]
    w_view_b = w_view.at[0 : w_bottle.shape[1]]
    w_view_v = w_view.at[w_bottle.shape[1] : w_view.shape[0]]
    w8 = pad_rows(row(w_density), 8).astype(BF)
    w_rgb = pad_rows(w_rgb3[...].astype(F32), 8).astype(BF)
    deltas = spread(deltas[...], count)
    raw = dot_nt(w8, top)[0:1]
    sigma = softplus(raw - 1.0)
    bottle = (dot(top, w_bottle[...]) + row(b_bottle)).astype(BF)
    view_rows = jnp.concatenate([jnp.broadcast_to(view_enc[r : r + 1, :].astype(F32), (samples, venc)) for r in range(rays)], 0).astype(BF)
    view_pre = dot(bottle, w_view_b[...]) + dot(view_rows, w_view_v[...]) + row(b_view)
    view_act, view_slope = silu_pair(view_pre)
    lane3 = lax.broadcasted_iota(jnp.int32, (3, 3), 0) == lax.broadcasted_iota(jnp.int32, (3, 3), 1)
    rgb_bias = jnp.sum(jnp.where(lane3, row(b_rgb), 0.0), axis=1, keepdims=True)
    rgb = jax.nn.sigmoid(dot_nt(w_rgb, view_act)[0:3] + rgb_bias)
    place = lax.broadcasted_iota(jnp.int32, (1, count), 1)
    limit = jnp.zeros((1, count), jnp.int32)
    for r in range(rays):
        limit = jnp.where(place // samples == r, counts[r], limit)
    live = place % samples < limit
    depth = jnp.where(live, sigma * deltas, 0.0)
    before = exclusive_sum(depth, samples)
    trans = jnp.exp(-before)
    weights = one_minus_exp(depth) * trans
    weights_ref[...] = weights
    pick = jnp.where(
        lax.broadcasted_iota(jnp.int32, (count, rays), 0) // samples == lax.broadcasted_iota(jnp.int32, (count, rays), 1), 1.0, 0.0
    )
    colour_ref[...] = dot_exact(weights * rgb, pick)
    d = dot_exact(d_ref[...], pick, (((1,), (1,)), ((), ())))
    grad_weights = jnp.sum(d * rgb, axis=0, keepdims=True)
    grad_rgb = (d * weights * rgb * (1.0 - rgb)).astype(BF)
    later = later_sum(grad_weights * weights, samples)
    grad_depth = grad_weights * jnp.exp(-depth) * trans - later
    grad_raw = (jnp.where(live, grad_depth * deltas, 0.0) * jax.nn.sigmoid(raw - 1.0)).astype(BF)
    grad_rgb8 = pad_rows(grad_rgb.astype(F32), 8).astype(BF)
    grad_raw8 = pad_rows(grad_raw.astype(F32), 8).astype(BF)
    grad_view_act = dot_tn(grad_rgb8, w_rgb)
    gvp = (grad_view_act * view_slope).astype(BF)
    g_bias_view = jnp.sum(gvp.astype(F32), axis=0, keepdims=True)
    grad_input = dot_nt(gvp, w_view_b[...])
    grad_bottle = grad_input.astype(BF)
    gview = dot_nt(gvp, w_view_v[...])
    gview_ref[...] = jnp.concatenate(
        [jnp.sum(gview[r * samples : (r + 1) * samples], axis=0, keepdims=True) for r in range(rays)], 0
    )
    gr_ref[...] = ((dot_nt(grad_bottle, w_bottle[...]) + dot_tn(grad_raw8, w8)) * slope_row[...]).astype(BF)
    gwb_ref[...] = dot_tn(top, grad_bottle).astype(BF)
    gwv = jnp.concatenate([dot_tn(bottle, gvp), pad_rows(dot_tn(view_rows, gvp), 32)], 0)
    half = gwv.shape[0] // 2
    gwv_ref[:, 0:vw] = gwv[0:half].astype(BF)
    gwv_ref[:, vw : 2 * vw] = gwv[half : 2 * half].astype(BF)
    width = small_ref.shape[1]
    small_ref[...] = jnp.zeros_like(small_ref)
    gwd = dot(grad_raw8, top)[0:1]
    for n in range(top.shape[1] // width):
        small_ref[n : n + 1, :] = gwd[:, n * width : (n + 1) * width]
    small_ref[4:5, :] = jnp.sum(grad_bottle.astype(F32), axis=0, keepdims=True)
    small_ref[5:6, 0:vw] = g_bias_view
    small_ref[6:9, 0:vw] = dot(grad_rgb8, view_act)[0:3]
    small_ref[5:6, vw : vw + 8] = dot_nt(jnp.ones((8, count), BF), grad_rgb8)[0:1]


def prop_forward_body(prop_in, wp_first, wp_rest, b_prop, wp_density, acts_ref, slopes_ref, raw_ref):
    current = prop_in[...]
    for j in range(4):
        weight = wp_first[...] if j == 0 else wp_rest[j - 1]
        pre = dot(current, weight) if j else dot_tn(current, weight)
        act, slope = silu_pair(pre + b_prop[j : j + 1, :].astype(F32))
        acts_ref[j] = act
        slopes_ref[j] = slope
        current = act
    raw_ref[...] = dot_nt(pad_rows(row(wp_density), 8).astype(BF), current)[0:1]


def prop_backward_body(samples, prop_in, acts, slopes, raw_ref, deltas, bounds, weights_ref, wp_first, wp_rest, wp_density, small_a, c_ref, g_bottle, g_view, gin_ref, keep, send, packed, small_ref, sems):
    io = Copies(sems)
    feat = g_bottle.shape[0]
    width = packed.shape[1]
    rest_at, first_at = feat, feat + 3 * width
    view_at = first_at + prop_in.shape[0]
    small_at = view_at + g_view.shape[0]
    packed[0:feat] = g_bottle[...]
    packed[view_at:small_at] = g_view[...]
    count = prop_in.shape[1]
    raw = raw_ref[...]
    deltas = spread(deltas[...], count)
    bounds = [spread(bounds[n].astype(F32), count) for n in range(2)]
    weights = weights_ref[...]
    depth = softplus(raw - 1.0) * deltas
    before = exclusive_sum(depth, samples)
    trans = jnp.exp(-before)
    pweights = one_minus_exp(depth) * trans
    at_row, _, same = ray_masks(count, samples)
    place = (at_row % samples).astype(F32)
    inside = jnp.where(same & (place >= bounds[0]) & (place < bounds[1]), 1.0, 0.0)
    bound = dot_exact(pweights, inside)
    excess = jnp.maximum(weights - bound, 0.0)
    grad_bound = -2.0 * excess / (weights + EPS)
    grad_pw = dot_exact(grad_bound, inside, (((1,), (1,)), ((), ())))
    later = later_sum(grad_pw * pweights, samples)
    grad_depth = grad_pw * jnp.exp(-depth) * trans - later
    grad_raw = (grad_depth * deltas * jax.nn.sigmoid(raw - 1.0)).astype(BF)
    raw8 = pad_rows(grad_raw.astype(F32), 8).astype(BF)
    wd8 = pad_rows(row(wp_density), 8).astype(BF)
    small_ref[...] = small_a[...]
    small_ref[13:14, :] = dot(raw8, acts[3])[0:1]
    grad = dot_tn(raw8, wd8)
    for j in (3, 2, 1, 0):
        gpre = (grad * slopes[j]).astype(BF)
        small_ref[9 + j : 10 + j, :] = jnp.sum(gpre.astype(F32), axis=0, keepdims=True)
        if j:
            packed[rest_at + (j - 1) * width : rest_at + j * width] = dot_tn(acts[j - 1], gpre).astype(BF)
            grad = dot_nt(gpre, wp_rest[j - 1])
        else:
            packed[first_at:view_at] = dot(prop_in[...], gpre).astype(BF)
            gin_ref[...] = dot_nt(wp_first[...], gpre)
    packed[small_at : small_at + SMALL] = small_ref[...].astype(BF)
    io.split(packed, c_ref[0], keep, send)


def swap(value, axis, bit):
    size = lax.axis_size(axis)
    return lax.ppermute(value, axis, [(i, i ^ bit) for i in range(size)])


class Order:
    def __init__(self):
        self.token = None

    def enter(self, *values):
        if self.token is None:
            return values
        return lax.optimization_barrier((*values, self.token))[:-1]

    def leave(self, value):
        self.token = value
        return value


def late_bits(start):
    bit = start
    while bit < lax.axis_size("dp"):
        yield bit
        bit *= 2


def add_here(order, mine, came, name):
    mine, came = order.enter(mine, came)
    [out] = kernel(lambda a, b, o, sems: add_body(a, b, o), name, [("w", mine), ("v", came)], [("w", mine.shape, BF)], spare=1)
    return order.leave(out)


def split_here(order, index, mine, came, name):
    mine, came = order.enter(mine, came)
    half = (mine.shape[0] // 2, *mine.shape[1:])
    keep, send = kernel(
        lambda i, a, b, k, s, sems: add_split_body(i, a, b, k, s),
        name,
        [("s", index), ("w", mine), ("v", came)],
        [("w", half, BF), ("v", half, BF)],
        spare=1,
    )
    order.leave(send)
    return keep, send


DIMS = {3: "xyz", 2: "yxz", 1: "xyz", 0: "zxy"}
PLAN = "Q P3 K P2 P1 3 P0 2 1 3 0 2 3 2 1 3 0 1 2 3 0 1 2 3 0 2 1 0 0 1 s s"
WIRES = {"x": ("mp", 2), "y": ("dp", 1), "z": ("dp", 2)}


def reduce_steps(order, name, dims, send, keep, index, finish):
    outer, inner = [d for d in dims if d != "x"]
    came = swap(send, *WIRES[dims[0]])
    yield
    if dims[0] == "x":
        keep, send = split_here(order, index[outer], keep, came, name + "_a")
        came = swap(send, *WIRES[outer])
    else:
        keep, send = split_here(order, index["second"], keep, came, name + "_a")
        came = swap(send, *WIRES["x"])
    yield
    keep, send = split_here(order, index[inner], keep, came, name + "_b")
    came = swap(send, *WIRES[inner])
    yield
    mine = add_here(order, keep, came, name + "_c")
    for bit in late_bits(4):
        came = swap(mine, "dp", bit)
        yield
        mine = add_here(order, mine, came, name + "_far")
    beside = swap(mine, *WIRES[inner])
    across = swap(mine, *WIRES[outer])
    yield
    (beside,) = order.enter(beside)
    corner = swap(beside, *WIRES[outer])
    yield
    finish((outer, inner), (mine, beside, across, corner))


def shared_steps(order, mine, x1, finish):
    came = swap(mine, "mp", 2)
    yield
    mine, came = order.enter(mine, came)
    [mine] = kernel(
        lambda i, a, b, o, sems: merge_body(i, a, b, o),
        "shared_merge",
        [("s", x1), ("v", mine), ("v", came)],
        [("v", (2 * mine.shape[0], mine.shape[1]), BF)],
        spare=1,
    )
    order.leave(mine)
    came = swap(mine, "mp", 1)
    yield
    finish(mine, came)


class Chain:
    def __init__(self, steps):
        self.steps = steps
        self.step()

    def step(self):
        next(self.steps, None)


def on_device(points_in, view_enc, deltas, counts, w_first, w_col, w_skip, w_row, b_col, b_row, w_density, w_bottle, b_bottle, w_view, b_view, w_rgb, b_rgb, prop_in, prop_deltas, bin_bounds, wp_first, wp_rest, b_prop, wp_density, d_colour):
    rows, ipe = points_in.shape
    rays, samples = deltas.shape
    feat = w_row.shape[2]
    width = w_row.shape[1]
    blocks = feat // width
    bottle = w_bottle.shape[1]
    vw = w_view.shape[1]
    venc = view_enc.shape[1]
    dp = lax.axis_index("dp")
    mp = lax.axis_index("mp")

    def scalar(value):
        return jnp.reshape(value, (1,)).astype(jnp.int32)

    one1 = jnp.ones((1,), jnp.int32)
    y1, z1, c1, x1 = scalar(dp % 2), scalar((dp // 2) % 2), scalar(mp % 2), scalar((mp // 2) % 2)
    order = Order()
    mat = (width, feat)
    tall = (feat, width)
    flat = (rows, feat)
    two = (2, rows, width)
    four = (4, rows, width)
    some = (blocks, width, width)
    many = (2 * blocks, width, width)

    message = (EXTRA + feat // 2, width)
    extra, first_half = kernel(
        pack_first_body,
        "pack_first",
        [("s", y1), ("a", w_first), ("a", w_skip), ("v", b_col), ("a", w_row)],
        [("a", (EXTRA, width), BF), ("a", message, BF)],
        [(message, BF)],
        spare=2,
    )
    order.leave(extra)
    hx = {0: swap(first_half, "mp", 2)}
    e1 = swap(extra, "mp", 1)
    pts = points_in.T
    (y1_k,) = order.enter(y1)
    hs = kernel(pack_rest_body, "pack_rest", [("s", y1_k), ("a", w_row), ("a", w_col), ("a", w_skip)], [("a", some, BF)] * 3, [(some, BF)] * 3, spare=2)
    order.leave(hs[0])
    for k in (1, 2, 3):
        hx[k] = swap(hs[k - 1], "mp", 2)
    row_s = swap(w_row, "mp", 1)
    col_s = swap(w_col, "mp", 1)
    skip_s = swap(w_skip, "mp", 1)
    pts_s = swap(pts, "mp", 1)
    own_cols = {1: w_col, 2: w_skip, 3: w_col}
    sib_cols = {1: col_s, 2: skip_s, 3: col_s}

    act02, act13, act_s, slope_col, slope_row, inputs, inputs_s, gathered = {}, {}, {}, {}, {}, {}, {}, {}

    crossed = {}

    def arrive(k):
        (hx[k],) = order.enter(hx[k])
        order.leave(hx[k])
        crossed[k] = swap(hx[k], "dp", 1), swap(hx[k], "mp", 1)

    def complete(k):
        hy, cx = crossed[k]
        (hy,) = order.enter(hy)
        order.leave(hy)
        gathered[k] = (hx[k], hy, cx, swap(hy, "mp", 1))

    arrive(0)
    args = order.enter(pts, extra, e1, hx[0], crossed[0][1])
    act02[0], act13[0], slope_col[0], bias, extras = kernel(
        first_body,
        "first_forward",
        [("v", a) for a in args[:3]] + [("a", a) for a in args[3:]],
        [("a", two, BF), ("a", two, BF), ("a", four, F32), ("v", (4, feat), F32), ("v", (4, EXTRA, width), BF)],
        [(two, BF), (two, BF), (four, F32)],
        spare=4,
    )
    order.leave(bias)
    act_s[0] = swap(act13[0], "mp", 1)
    arrive(1)

    prop_t, wp_first_k = order.enter(prop_in.T, wp_first)
    acts, slopes, prop_raw = kernel(
        lambda *refs: prop_forward_body(*refs[:-1]),
        "prop_forward",
        [("v", prop_t), ("v", wp_first_k), ("v", wp_rest), ("v", b_prop), ("v", wp_density)],
        [("v", (4, rows, bottle), BF), ("v", (4, rows, bottle), F32), ("v", (1, rows), F32)],
        spare=4,
    )
    order.leave(prop_raw)
    complete(0)
    arrive(2)
    b_row_k, a02, a13 = order.enter(b_row, act02[0], act13[0])
    up, slope_row[0] = kernel(
        row0_body,
        "row0_forward",
        [("s", y1), ("v", b_row_k), ("a", a02), ("a", a13), ("a", w_row), ("a", row_s)] + [("a", a) for a in gathered[0]],
        [("a", flat, BF), ("a", flat, F32)],
        [(two, BF), (two, BF), (mat, BF), (mat, BF), (tall, BF), (tall, BF), (flat, BF), (flat, F32)],
        spare=6,
    )
    order.leave(up)
    complete(1)
    arrive(3)
    complete(2)
    weight_bufs = [(mat, BF), (mat, BF), (tall, BF), (tall, BF), (many, BF), (many, BF)]

    def weights_of(k):
        return [("a", a) for a in (w_row, row_s, own_cols[k], sib_cols[k], *gathered[k])]

    for k in (1, 2):
        inputs[k] = up
        inputs_s[k] = swap(up, "mp", 1)
        (b_row_k,) = order.enter(b_row)
        more = [("v", pts), ("v", extras)] if k == 2 else []
        act02[k], act13[k], slope_col[k], up, slope_row[k] = kernel(
            functools.partial(pair_body, k, k == 2),
            f"pair{k}_forward",
            [("s", y1), ("v", bias), ("v", b_row_k)] + more + [("a", inputs[k])] + weights_of(k),
            [("a", two, BF), ("a", two, BF), ("a", four, F32), ("a", flat, BF), ("a", flat, F32)],
            [(flat, BF), *weight_bufs, (two, BF), (two, BF), (four, F32), (flat, BF), (flat, F32)],
            spare=6,
        )
        order.leave(up)
        act_s[k] = swap(act13[k], "mp", 1)

    complete(3)
    inputs[3] = up
    inputs_s[3] = swap(up, "mp", 1)
    grs, gr_s, gc02, gc13, gc_s, bc, dx, brow = {}, {}, {}, {}, {}, {}, {}, {}
    heads_in = (w_density, w_bottle, b_bottle, w_view, b_view, w_rgb.T, b_rgb, view_enc, deltas, d_colour)
    (b_row_k,) = order.enter(b_row)
    got = kernel(
        functools.partial(top_body, 3, samples, len(heads_in)),
        "top",
        [("s", y1), ("s", counts), ("v", bias), ("v", b_row_k)] + [("v", a) for a in heads_in] + [("a", up), ("a", slope_row[2])] + weights_of(3)[:4] + [("n", a) for a in gathered[3]],
        [("a", two, BF), ("a", two, BF), ("a", flat, BF), ("a", two, BF), ("a", two, BF), ("a", flat, BF)]
        + [("v", (3, rays), F32), ("v", (rays, venc), F32), ("v", (1, rows), F32), ("v", (feat, bottle), BF), ("v", (144, 2 * vw), BF), ("v", (SMALL, width), F32)],
        [(flat, BF), (flat, F32), *weight_bufs, (two, BF), (two, BF), (four, F32), (flat, BF), (flat, F32), (flat, BF), (two, BF), (two, BF), (flat, BF)],
    )
    act02[3], act13[3], grs[3], gc02[3], gc13[3], grs[2], colour, grad_view, ray_weights, g_bottle, g_view, small_a = got
    order.leave(grs[2])
    act_s[3] = swap(act13[3], "mp", 1)
    gr_s[3] = swap(grs[3], "mp", 1)
    gc_s[3] = swap(gc13[3], "mp", 1)

    results, chains = {}, {}

    index = {"x": x1, "y": y1, "z": z1, "second": one1}

    def finish(k, halved, pieces):
        pieces = order.enter(*pieces)
        size = (4 * pieces[0].shape[0], width)
        ins = [("s", index[halved[0]]), ("s", index[halved[1]])] + [("v", p) for p in pieces]
        outs = [("a", (4, width, feat), F32)]
        bufs = [(size, BF), (mat, F32)]
        alias = {}

        def in_place(name, index):
            if name in results:
                alias[len(ins)] = index
                ins.append(("a", results[name]))

        in_place("row", 0)
        if k == 2:
            outs.append(("a", (feat + ipe, width), F32))
            bufs.append((tall, F32))
            in_place("skip", 1)
            got = kernel(functools.partial(final_skip_body, k, len(alias)), f"final{k}", ins, outs, bufs, alias, spare=4)
            results["skip"] = got[1]
        elif k:
            outs.append(("a", (2, feat, width), F32))
            bufs.append((tall, F32))
            in_place("col", 1)
            got = kernel(functools.partial(final_pair_body, k, len(alias)), f"final{k}", ins, outs, bufs, alias, spare=4)
            results["col"] = got[1]
        else:
            outs += [("a", (feat + ipe, width), F32), ("v", (ipe, width), F32), ("v", (4, width), F32), ("v", (4, feat), F32), ("v", (512, width), BF)]
            bufs.append(((size[0] - feat - 512, width), F32))
            in_place("skip", 1)
            got = kernel(functools.partial(final_low_body, len(alias)), f"final{k}", ins, outs, bufs, alias, spare=4)
            results["skip"] = got[1]
            results["tail"] = got[2:5]
            chains["s"] = Chain(shared_steps(order, got[5], x1, finish_shared))
        results["row"] = got[0]
        order.leave(got[0])

    def finish_shared(mine, came):
        mine, came = order.enter(mine, came)
        results["shared"] = kernel(
            unpack_body,
            "unpack",
            [("s", c1), ("v", mine), ("v", came)],
            [
                ("v", (1, feat), F32),
                ("v", (feat, bottle), F32),
                ("v", (1, bottle), F32),
                ("v", (bottle + venc, vw), F32),
                ("v", (1, vw), F32),
                ("v", (3, vw), F32),
                ("v", (1, 3), F32),
                ("v", (ipe, bottle), F32),
                ("v", (3, bottle, bottle), F32),
                ("v", (4, bottle), F32),
                ("v", (1, bottle), F32),
            ],
            [((2048, bottle), BF)],
            spare=4,
        )
        order.leave(results["shared"][0])

    def send_away(k):
        dims = DIMS[k]
        folded = dims[0] != "x"
        kind = {3: "plain", 2: "points", 1: "plain", 0: "low"}[k]
        args = [act02[k], act_s[k], grs[k], gr_s[k], gc02[k], gc_s[k]] + ([inputs[k], inputs_s[k]] if k else [])
        args = order.enter(*args)
        height = feat + 512 + 256 if kind == "low" else 2 * feat
        small = [("s", index[dims[0]])] if folded else []
        if kind == "low":
            small += [("s", x1)]
        if kind != "plain":
            small += [("v", pts), ("v", pts_s)]
        if kind == "low":
            small += [("v", keep_h), ("v", came_h)]
            small += [("v", bc[1]), ("v", bc[2]), ("v", bc[3]), ("v", dx[2]), ("v", brow[1]), ("v", brow[2]), ("v", brow[3])]
        outs = [("a" if folded else "v", (height, width), BF), ("w", (height, width), BF)]
        if kind != "low":
            outs += [("v", (2, width), F32), ("v", (blocks, width), F32)]
        if kind == "points":
            outs.append(("v", (2, ipe, width), F32))
        bufs = [(two, BF), (two, BF), (flat, BF), (flat, BF), (two, BF), (two, BF)] + ([(flat, BF), (flat, BF)] if k else [])
        out, home, *rest = kernel(
            functools.partial(products_body, kind, folded), f"products{k}", small + [("a", a) for a in args], outs, bufs + ([((height, width), BF)] * 2 if folded else []), spare=6
        )
        if rest:
            bc[k], brow[k] = rest[:2]
        if kind == "points":
            dx[k] = rest[2]
        order.leave(out)
        chains[str(k)] = Chain(reduce_steps(order, f"sum{k}", dims, out, home, index, functools.partial(finish, k)))

    def prop_backward():
        nonlocal grad_prop_in, keep_h, came_h
        prop_args = order.enter(prop_t, acts, slopes, prop_raw, prop_deltas, bin_bounds, ray_weights, wp_first, wp_rest, wp_density, small_a, c1, g_bottle, g_view)
        grad_prop_in, keep_h, send_h = kernel(
            functools.partial(prop_backward_body, samples),
            "prop_backward",
            [("s" if n == 11 else "v", a) for n, a in enumerate(prop_args)],
            [("v", (ipe, rows), F32), ("a", (1024, bottle), BF), ("a", (1024, bottle), BF)],
            [((2048, bottle), BF), ((SMALL, width), F32)],
            spare=6,
        )
        order.leave(send_h)
        came_h = swap(send_h, "mp", 1)

    def chain_backward():
        nonlocal grad_points
        args = order.enter(grs[2], slope_col[2], slope_col[1], slope_col[0], slope_row[1], slope_row[0])
        got = kernel(
            chain_body,
            "chain",
            [("s", y1), ("v", extras)]
            + [("a", a) for a in args]
            + weights_of(2)
            + weights_of(1)
            + [("a", a) for a in (w_row, row_s, *gathered[0])],
            [("a", two, BF)] * 6 + [("a", flat, BF)] * 2 + [("v", (ipe, rows), F32)],
            [(flat, BF)] * 3 + [(four, F32)] * 3 + [(flat, F32)] * 2 + weight_bufs + weight_bufs + [(mat, BF)] * 2 + [(tall, BF)] * 2 + [(two, BF)] * 6,
            spare=6,
        )
        gc02[2], gc02[1], gc02[0], gc13[2], gc13[1], gc13[0], grs[1], grs[0], grad_points = got
        order.leave(grad_points)
        for k in (2, 1, 0):
            gr_s[k] = swap(grs[k], "mp", 1)
            gc_s[k] = swap(gc13[k], "mp", 1)

    grad_prop_in = keep_h = came_h = grad_points = None
    for item in PLAN.split():
        if item == "Q":
            prop_backward()
        elif item == "K":
            chain_backward()
        elif item[0] == "P":
            send_away(int(item[1]))
        elif item in chains:
            chains[item].step()
    for item in ("3", "2", "1", "0", "s"):
        for _ in range(16):
            chains[item].step()

    g_density, g_bottle, gb_bottle, g_view, gb_view, g_rgb, gb_rgb, g_first, g_rest, gb_prop, g_wpd = results["shared"]
    first, bcol, brow_out = results["tail"]
    return (
        colour,
        grad_points.T,
        grad_view,
        grad_prop_in.T,
        first,
        results["col"],
        results["skip"],
        results["row"],
        bcol,
        brow_out,
        g_density.reshape(feat),
        g_bottle,
        gb_bottle.reshape(bottle),
        g_view,
        gb_view.reshape(vw),
        g_rgb.T,
        gb_rgb.reshape(3),
        g_first,
        g_rest,
        gb_prop,
        g_wpd.reshape(bottle),
    )


def solution(mesh):
    both = ("dp", "mp")
    placed = (
        P(both, None),
        P(both, None),
        P(both, None),
        P(both),
        P(None, "mp"),
        P(None, None, "mp"),
        P(None, "mp"),
        P(None, "mp", None),
        P(None, "mp"),
        *([P()] * 8),
        P(both, None),
        P(both, None),
        P(None, both, None),
        P(),
        P(),
        P(),
        P(),
        P(None, both),
    )
    return jax.shard_map(
        on_device,
        mesh=mesh,
        in_specs=placed,
        out_specs=(
            P(None, both),
            P(both, None),
            P(both, None),
            P(both, None),
            P(None, "mp"),
            P(None, None, "mp"),
            P(None, "mp"),
            P(None, "mp", None),
            P(None, "mp"),
            *([P()] * 12),
        ),
        check_vma=False,
    )
```

```python
import functools

import jax
import jax.numpy as jnp
from jax import lax
from jax.experimental import pallas as pl
from jax.experimental.pallas import tpu as pltpu
from jax.sharding import PartitionSpec as P

EPS = 0.0001
BF = jnp.bfloat16
F32 = jnp.float32
HIGH = lax.Precision.HIGHEST
COPIES = 48
EXTRA = 208
SMALL = 16


def dot(a, b):
    return jnp.dot(a, b, preferred_element_type=F32)


def dot_nt(a, b):
    return lax.dot_general(a, b, (((1,), (1,)), ((), ())), preferred_element_type=F32)


def dot_tn(a, b):
    return lax.dot_general(a, b, (((0,), (0,)), ((), ())), preferred_element_type=F32)


def dot_exact(a, b, dims=(((1,), (0,)), ((), ()))):
    return lax.dot_general(a, b, dims, precision=HIGH, preferred_element_type=F32)


def silu_pair(pre):
    gate = 0.5 + 0.5 * jnp.tanh(0.5 * pre)
    return (pre * gate).astype(BF), gate * (1.0 + pre * (1.0 - gate))


def softplus(v):
    tail = jnp.exp(-jnp.abs(v))
    series = tail * (1.0 - tail * (1.0 / 2 - tail * (1.0 / 3 - tail * (1.0 / 4 - tail * (1.0 / 5)))))
    return jnp.maximum(v, 0.0) + jnp.where(tail < 0.03, series, jnp.log(1.0 + tail))


def one_minus_exp(depth):
    nested = 1.0
    for n in (8, 7, 6, 5, 4, 3, 2):
        nested = 1.0 - depth * (1.0 / n) * nested
    return jnp.where(depth < 0.25, depth * nested, 1.0 - jnp.exp(-depth))


class Copies:
    def __init__(self, sems):
        self.sems = sems
        self.count = 0

    def start(self, source, target):
        copy = pltpu.make_async_copy(source, target, self.sems.at[self.count])
        self.count += 1
        copy.start()
        return copy

    def split(self, whole, index, keep, send):
        half = whole.shape[0] // 2
        at = pl.multiple_of(index * half, half)
        other = pl.multiple_of((1 - index) * half, half)
        one = self.start(whole.at[pl.ds(other, half)], send)
        two = self.start(whole.at[pl.ds(at, half)], keep)
        one.wait()
        two.wait()


def size_of(shape, dtype):
    total = jnp.dtype(dtype).itemsize
    for extent in shape:
        total *= extent
    return total


def kernel(body, name, ins, outs, bufs=(), alias=None, spare=10):
    spaces = {"s": pltpu.SMEM, "v": pltpu.VMEM, "w": pltpu.VMEM, "a": pltpu.HBM, "n": pl.ANY}
    held = [(a.shape, a.dtype) for kind, a in ins if kind == "v"] + [o[1:] for o in outs if o[0] == "v"] + list(bufs)
    grant = spare * 1024 * 1024 + sum(2 * size_of(*h) if h[0][-1] < 128 else size_of(*h) for h in held)
    shapes = {"v": jax.ShapeDtypeStruct, "w": pltpu.VMEM, "a": pltpu.HBM}

    def placed(kind, array):
        return pltpu.with_memory_space_constraint(array, spaces[kind]) if kind in "aw" else array

    return pl.pallas_call(
        body,
        out_shape=[shapes[kind](shape, dtype) for kind, shape, dtype in outs],
        in_specs=[pl.BlockSpec(memory_space=spaces[kind]) for kind, _ in ins],
        out_specs=[pl.BlockSpec(memory_space=spaces[kind]) for kind, _, _ in outs],
        scratch_shapes=[pltpu.VMEM(shape, dtype) for shape, dtype in bufs] + [pltpu.SemaphoreType.DMA((COPIES,))],
        input_output_aliases=alias or {},
        compiler_params=pltpu.CompilerParams(vmem_limit_bytes=grant),
        cost_estimate=pl.CostEstimate(flops=1, bytes_accessed=1, transcendentals=0),
        name=name,
    )(*[placed(kind, array) for kind, array in ins])


def pack_first_body(y_ref, w_first, w_skip, b_col, w_row, extra, message, whole, sems):
    io = Copies(sems)
    depth, width = w_first.shape
    count = (message.shape[0] - EXTRA) // width
    tail = w_skip.shape[0] - depth
    copies = [
        io.start(w_row.at[0, :, pl.ds(pl.multiple_of((y_ref[0] * count + n) * width, width), width)], whole.at[EXTRA + n * width : EXTRA + (n + 1) * width])
        for n in range(count)
    ]
    copies.append(io.start(w_first, whole.at[0:depth]))
    copies.append(io.start(w_skip.at[tail : tail + depth], whole.at[depth : 2 * depth]))
    whole[2 * depth : EXTRA] = jnp.concatenate([b_col[...].astype(F32), jnp.zeros((EXTRA - 2 * depth - 4, width), F32)], 0).astype(BF)
    for copy in copies:
        copy.wait()
    copies = [io.start(whole, message), io.start(whole.at[0:EXTRA], extra)]
    for copy in copies:
        copy.wait()


def pack_rest_body(y_ref, w_row, w_col, w_skip, h1, h2, h3, b1, b2, b3, sems):
    io = Copies(sems)
    count, width = b1.shape[0], b1.shape[1]
    outs = ((b1, h1), (b2, h2), (b3, h3))

    def move(source):
        io.count = 0
        groups = [[io.start(source(k + 1, n), buf.at[n]) for n in range(count)] for k, (buf, _) in enumerate(outs)]
        last = []
        for group, (buf, out) in zip(groups, outs):
            for copy in group:
                copy.wait()
            last.append(io.start(buf, out))
        for copy in last:
            copy.wait()

    @pl.when(y_ref[0] == 0)
    def rows():
        move(lambda k, n: w_row.at[k, :, n * width : (n + 1) * width])

    @pl.when(y_ref[0] != 0)
    def columns():
        move(lambda k, n: (w_skip if k == 2 else w_col.at[k // 2]).at[n * width : (n + 1) * width])


class Weights:
    def __init__(self, io, k, y, refs, bufs, rows_first=False):
        own_row, sib_row, own_col, sib_col, hx, hy, cx, cy = refs
        row0, row1, col0, col1, far2, far3 = bufs
        self.bufs = bufs
        self.width = row0.shape[0]
        self.blocks = row0.shape[1] // self.width
        half = far2.shape[0] // 2
        at, other = pl.multiple_of(y * half, half), pl.multiple_of((1 - y) * half, half)
        col_of = (lambda ref: ref.at[0 : self.blocks * self.width]) if k == 2 else (lambda ref: ref.at[k // 2])
        pairs = {
            ("col", 0): [(col_of(own_col), col0)],
            ("col", 1): [(col_of(sib_col), col1)],
            ("far", 2): [(hx, far2.at[pl.ds(at, half)]), (hy, far2.at[pl.ds(other, half)])],
            ("far", 3): [(cx, far3.at[pl.ds(at, half)]), (cy, far3.at[pl.ds(other, half)])],
            ("row", 0): [(own_row.at[k], row0)],
            ("row", 1): [(sib_row.at[k], row1)],
        }
        near, late = (("row", "col") if rows_first else ("col", "row"))
        keys = [(near, 1), (near, 0), ("far", 3), ("far", 2), (late, 1), (late, 0)]
        self.waits = {key: [io.start(*pair) for pair in pairs[key]] for key in keys}

    def ready(self, *key):
        for copy in self.waits.pop(key, ()):
            copy.wait()

    def col(self, j):
        self.ready("col" if j < 2 else "far", j)
        if j < 2:
            return self.bufs[2 + j][...]
        return self.bufs[2 + j][self.blocks : 2 * self.blocks].reshape(self.blocks * self.width, self.width)

    def row(self, j, n):
        self.ready("row" if j < 2 else "far", j)
        if j < 2:
            return self.bufs[j][:, n * self.width : (n + 1) * self.width]
        return self.bufs[2 + j][n]


class FirstWeights:
    def __init__(self, io, y, refs, bufs):
        own_row, sib_row, hx, hy, cx, cy = refs
        self.bufs = bufs
        self.width = bufs[0].shape[0]
        half = bufs[2].shape[0] // 2
        at, other = pl.multiple_of(y * half, half), pl.multiple_of((1 - y) * half, half)
        rows = slice(EXTRA, EXTRA + half)
        self.waits = {
            1: [io.start(sib_row.at[0], bufs[1])],
            0: [io.start(own_row.at[0], bufs[0])],
            3: [io.start(cx.at[rows], bufs[3].at[pl.ds(at, half)]), io.start(cy.at[rows], bufs[3].at[pl.ds(other, half)])],
            2: [io.start(hx.at[rows], bufs[2].at[pl.ds(at, half)]), io.start(hy.at[rows], bufs[2].at[pl.ds(other, half)])],
        }

    def row(self, j, n):
        for copy in self.waits.pop(j, ()):
            copy.wait()
        cols = slice(n * self.width, (n + 1) * self.width)
        return self.bufs[j][:, cols] if j < 2 else self.bufs[j][cols]


def put_block(j, value, even, odd):
    (odd if j % 2 else even)[j // 2] = value


def get_block(j, even, odd):
    return (odd if j % 2 else even)[j // 2]


def first_body(pts, e0, e1, m2, m3, act02, act13, slope_ref, bias_ref, extras, acts, acts13, slopes, sems):
    io = Copies(sems)
    loads = [io.start(m2.at[0:EXTRA], extras.at[2]), io.start(m3.at[0:EXTRA], extras.at[3])]
    extras[0] = e0[...]
    extras[1] = e1[...]
    depth, width = pts.shape[0], e0.shape[1]
    for load in loads:
        load.wait()
    for j in range(4):
        bias_ref[:, j * width : (j + 1) * width] = extras[j, 2 * depth : 2 * depth + 4, :].astype(F32)
    outs = []
    for j in (1, 3, 0, 2):
        act, slope = silu_pair(dot_tn(pts[...], extras[j, 0:depth, :]) + bias_ref[0:1, j * width : (j + 1) * width])
        put_block(j, act, acts, acts13)
        slopes[j] = slope
        if j == 3:
            outs.append(io.start(acts13, act13))
    outs += [io.start(acts, act02), io.start(slopes, slope_ref)]
    for copy in outs:
        copy.wait()


def row_forward(weights, k, acts, acts13, b_row, up, slopes):
    width = acts.shape[1]
    for n in range(up.shape[1] // width):
        cols = slice(n * width, (n + 1) * width)
        pre = b_row[k : k + 1, cols].astype(F32)
        for j in (3, 2, 1, 0):
            pre = pre + dot(get_block(j, acts, acts13), weights.row(j, n))
        act, slope = silu_pair(pre)
        up[:, cols] = act
        slopes[:, cols] = slope


def row0_body(y_ref, b_row, act02, act13, own, sib, hx, hy, cx, cy, up_ref, slope_ref, acts, acts13, w0, w1, w2, w3, up, slopes, sems):
    io = Copies(sems)
    loads = [io.start(act02, acts), io.start(act13, acts13)]
    weights = FirstWeights(io, y_ref[0], (own, sib, hx, hy, cx, cy), (w0, w1, w2, w3))
    for load in loads:
        load.wait()
    row_forward(weights, 0, acts, acts13, b_row, up, slopes)
    outs = [io.start(up, up_ref), io.start(slopes, slope_ref)]
    for copy in outs:
        copy.wait()


def col_forward(weights, k, value, bias, pts, extras, acts, acts13, slopes):
    width = acts.shape[1]
    for j in (1, 0, 3, 2):
        pre = dot(value, weights.col(j)) + bias[k : k + 1, j * width : (j + 1) * width]
        if extras is not None:
            depth = pts.shape[0]
            pre = pre + dot_tn(pts[...], extras[j, depth : 2 * depth, :])
        act, slope = silu_pair(pre)
        put_block(j, act, acts, acts13)
        slopes[j] = slope


def pair_body(k, skip, y_ref, bias, b_row, *rest):
    rest = list(rest)
    pts = rest.pop(0) if skip else None
    extras = rest.pop(0) if skip else None
    u, own_row, sib_row, own_col, sib_col, hx, hy, cx, cy, act02, act13, slope_col, up_ref, slope_row, u_buf, w0, w1, w2, w3, w4, w5, acts, acts13, slopes_c, up, slopes_r, sems = rest
    io = Copies(sems)
    load = io.start(u, u_buf)
    weights = Weights(io, k, y_ref[0], (own_row, sib_row, own_col, sib_col, hx, hy, cx, cy), (w0, w1, w2, w3, w4, w5))
    load.wait()
    col_forward(weights, k, u_buf[...], bias, pts, extras, acts, acts13, slopes_c)
    outs = [io.start(acts13, act13), io.start(acts, act02), io.start(slopes_c, slope_col)]
    row_forward(weights, k, acts, acts13, b_row, up, slopes_r)
    outs += [io.start(up, up_ref), io.start(slopes_r, slope_row)]
    for copy in outs:
        copy.wait()


def chain_step(weights, gr, slope_col, slope_row, pts_depth, extras, gcs, gcs13, gru, gp):
    width = gcs.shape[1]
    blocks = gr.shape[1] // width
    for j in (1, 0, 3, 2):
        gca = dot_nt(gr[:, 0:width], weights.row(j, 0))
        for n in range(1, blocks):
            gca += dot_nt(gr[:, n * width : (n + 1) * width], weights.row(j, n))
        put_block(j, (gca * slope_col[j]).astype(BF), gcs, gcs13)
    if gru is not None:
        gu = None
        for j in (1, 0, 3, 2):
            step = dot_nt(get_block(j, gcs, gcs13), weights.col(j))
            gu = step if gu is None else gu + step
        gru[...] = (gu * slope_row[...]).astype(BF)
    if extras is not None:
        at = pts_depth if gru is not None else 0
        for j in (1, 0, 3, 2):
            gp = gp + dot_nt(extras[j, at : at + pts_depth, :], get_block(j, gcs, gcs13))
    return gp


def top_body(k, samples, n_heads, y_ref, counts, bias, b_row, *rest):
    rest = list(rest)
    heads_in = [rest.pop(0) for _ in range(n_heads)]
    u, slope_row, own_row, sib_row, own_col, sib_col, hx, hy, cx, cy, act02, act13, gr_ref, gc02, gc13, gr_low, colour_ref, gview_ref, weights_ref, gwb_ref, gwv_ref, small_ref, u_buf, sr_buf, w0, w1, w2, w3, w4, w5, acts, acts13, slopes_c, up, slopes_r, gr, gcs, gcs13, gru, sems = rest
    io = Copies(sems)
    load = io.start(u, u_buf)
    weights = Weights(io, k, y_ref[0], (own_row, sib_row, own_col, sib_col, hx, hy, cx, cy), (w0, w1, w2, w3, w4, w5))
    late = io.start(slope_row, sr_buf)
    load.wait()
    col_forward(weights, k, u_buf[...], bias, None, None, acts, acts13, slopes_c)
    outs = [io.start(acts13, act13), io.start(acts, act02)]
    row_forward(weights, k, acts, acts13, b_row, up, slopes_r)
    heads_body(samples, up, counts, *heads_in, slopes_r, colour_ref, gview_ref, gr, weights_ref, gwb_ref, gwv_ref, small_ref)
    outs.append(io.start(gr, gr_ref))
    late.wait()
    chain_step(weights, gr, slopes_c, sr_buf, 0, None, gcs, gcs13, gru, None)
    outs += [io.start(gcs13, gc13), io.start(gcs, gc02), io.start(gru, gr_low)]
    for copy in outs:
        copy.wait()


def chain_body(y_ref, extras, *rest):
    rest = list(rest)
    gr2_in = rest.pop(0)
    slopes_c = {k: rest.pop(0) for k in (2, 1, 0)}
    slopes_r = {k: rest.pop(0) for k in (1, 0)}
    refs = {k: [rest.pop(0) for _ in range(8)] for k in (2, 1)}
    refs[0] = [rest.pop(0) for _ in range(6)]
    gc02 = {k: rest.pop(0) for k in (2, 1, 0)}
    gc13 = {k: rest.pop(0) for k in (2, 1, 0)}
    gr_out = {k: rest.pop(0) for k in (1, 0)}
    gp_ref = rest.pop(0)
    gr = {k: rest.pop(0) for k in (2, 1, 0)}
    sc = {k: rest.pop(0) for k in (2, 1, 0)}
    sr = {k: rest.pop(0) for k in (1, 0)}
    bufs = {k: [rest.pop(0) for _ in range(6)] for k in (2, 1)}
    bufs[0] = [rest.pop(0) for _ in range(4)]
    gcs = {k: rest.pop(0) for k in (2, 1, 0)}
    gcs13 = {k: rest.pop(0) for k in (2, 1, 0)}
    (sems,) = rest
    io = Copies(sems)
    y = y_ref[0]
    weights, loads = {}, {}
    for k in (2, 1, 0):
        loads[k] = [io.start(slopes_c[k], sc[k])]
        if k == 2:
            loads[k].append(io.start(gr2_in, gr[2]))
        weights[k] = Weights(io, k, y, refs[k], bufs[k], rows_first=True) if k else FirstWeights(io, y, refs[k], bufs[k])
        if k:
            loads[k].append(io.start(slopes_r[k - 1], sr[k - 1]))
    depth = gp_ref.shape[0]
    gp = jnp.zeros(gp_ref.shape, F32)
    outs = []
    for k in (2, 1, 0):
        for load in loads[k]:
            load.wait()
        gp = chain_step(weights[k], gr[k], sc[k], sr.get(k - 1), depth, extras if k != 1 else None, gcs[k], gcs13[k], gr.get(k - 1), gp)
        outs += [io.start(gcs13[k], gc13[k]), io.start(gcs[k], gc02[k])]
        if k:
            outs.append(io.start(gr[k - 1], gr_out[k - 1]))
    gp_ref[...] = gp
    for copy in outs:
        copy.wait()


def row_sum(value):
    return jnp.sum(value.astype(F32), axis=0, keepdims=True)


def products_body(kind, folded, *rest):
    rest = list(rest)
    pair = kind != "low"
    i_ref = rest.pop(0) if folded else None
    x_ref = rest.pop(0) if kind == "low" else None
    points = kind != "plain"
    if points:
        pts, pts_s = rest.pop(0), rest.pop(0)
    if kind == "low":
        keep_h, came_h = rest.pop(0), rest.pop(0)
        bcs = [rest.pop(0) for _ in range(3)]
        dx2 = rest.pop(0)
        brs = [rest.pop(0) for _ in range(3)]
    act, act_s, gr, gr_s, gc, gc_s = [rest.pop(0) for _ in range(6)]
    if pair:
        u, u_s = rest.pop(0), rest.pop(0)
    away, home = rest.pop(0), rest.pop(0)
    if kind != "low":
        bc_ref, brow_ref = rest.pop(0), rest.pop(0)
    if kind == "points":
        dx_ref = rest.pop(0)
    act_b, act_sb, gr_b, gr_sb, gc_b, gc_sb = [rest.pop(0) for _ in range(6)]
    if pair:
        u_b, u_sb = rest.pop(0), rest.pop(0)
    if folded:
        away_b, home_b = rest.pop(0), rest.pop(0)
    (sems,) = rest
    io = Copies(sems)
    loads = [io.start(a, b) for a, b in ((act, act_b), (act_s, act_sb), (gr, gr_b), (gr_s, gr_sb), (gc, gc_b), (gc_s, gc_sb))]
    more = [io.start(u, u_b), io.start(u_s, u_sb)] if pair else []
    for load in loads:
        load.wait()
    width = act_b.shape[2]
    feat = gr_b.shape[1]
    blocks = feat // width
    outs = []
    dx = {}
    bc = {}
    if not folded:
        away_b, home_b = away, home
    for slot, out_b, out in ((1, away_b, away), (0, home_b, home)):
        for n in range(blocks):
            cols = slice(n * width, (n + 1) * width)
            out_b[n * width : (n + 1) * width] = (dot_tn(act_b[slot], gr_b[:, cols]) + dot_tn(act_sb[slot], gr_sb[:, cols])).astype(BF)
        for load in more:
            load.wait()
        more = []
        if pair:
            out_b[feat : 2 * feat] = (dot_tn(u_b[...], gc_b[slot]) + dot_tn(u_sb[...], gc_sb[slot])).astype(BF)
        bc[slot] = row_sum(gc_b[slot]) + row_sum(gc_sb[slot])
        if points:
            dx[slot] = dot(pts[...], gc_b[slot]) + dot(pts_s[...], gc_sb[slot])
        if kind == "low":
            half = keep_h.shape[0] // 2
            index = x_ref[0] if slot == 0 else 1 - x_ref[0]
            at = pl.ds(pl.multiple_of(index * half, half), half)
            out_b[feat : feat + half] = (keep_h[at, :].astype(F32) + came_h[at, :].astype(F32)).astype(BF)
            depth = pts.shape[0]
            parts = [dx[slot], dx2[slot], bc[slot]] + [b[slot : slot + 1, :] for b in bcs]
            parts.append(jnp.zeros((EXTRA - 2 * depth - 4, width), F32))
            brow = jnp.concatenate([row_sum(gr_b[:, n * width : (n + 1) * width]) + row_sum(gr_sb[:, n * width : (n + 1) * width]) for n in range(blocks)], 0)
            parts += [brow] + [br[...] for br in brs]
            tail = jnp.concatenate(parts, 0)
            pad = out_b.shape[0] - feat - half - tail.shape[0]
            out_b[feat + half :] = jnp.concatenate([tail, jnp.zeros((pad, width), F32)], 0).astype(BF)
        if not folded:
            continue
        half = out_b.shape[0] // 2
        at = pl.multiple_of(i_ref[0] * half, half)
        other = pl.multiple_of((1 - i_ref[0]) * half, half)
        rows = slice(0, half) if slot else slice(half, 2 * half)
        outs.append(io.start(out_b.at[pl.ds(other, half)], away.at[rows]))
        outs.append(io.start(out_b.at[pl.ds(at, half)], home.at[rows]))
    if kind != "low":
        for slot in range(2):
            bc_ref[slot : slot + 1, :] = bc[slot]
            if kind == "points":
                dx_ref[slot] = dx[slot]
        for n in range(blocks):
            cols = slice(n * width, (n + 1) * width)
            brow_ref[n : n + 1, :] = row_sum(gr_b[:, cols]) + row_sum(gr_sb[:, cols])
    for copy in outs:
        copy.wait()


def add_body(a, b, out):
    out[...] = (a[...].astype(F32) + b[...].astype(F32)).astype(BF)


def add_split_body(i_ref, a, b, keep, send):
    half = keep.shape[0]
    at = pl.ds(pl.multiple_of(i_ref[0] * half, half), half)
    other = pl.ds(pl.multiple_of((1 - i_ref[0]) * half, half), half)
    send[...] = (a[other, :].astype(F32) + b[other, :].astype(F32)).astype(BF)
    keep[...] = (a[at, :].astype(F32) + b[at, :].astype(F32)).astype(BF)


def merge_body(i_ref, a, b, out):
    half = a.shape[0]
    out[pl.ds(pl.multiple_of(i_ref[0] * half, half), half), :] = a[...]
    out[pl.ds(pl.multiple_of((1 - i_ref[0]) * half, half), half), :] = b[...]


def gather_pieces(y, z, pieces, whole):
    piece = pieces[0].shape[0]
    places = ((y, z), (y, 1 - z), (1 - y, z), (1 - y, 1 - z))
    for p, (a, b) in zip(pieces, places):
        whole[pl.ds(pl.multiple_of((2 * a + b) * piece, piece), piece), :] = p[...]


def write_row(io, whole, row_b, out, k):
    width = whole.shape[1]
    for n in range(row_b.shape[1] // width):
        row_b[:, n * width : (n + 1) * width] = whole[n * width : (n + 1) * width].astype(F32)
    return io.start(row_b, out.at[k])


def final_pair_body(k, n_alias, y_ref, z_ref, p0, p1, p2, p3, *rest):
    row_out, col_out, whole, row_b, col_b, sems = rest[n_alias:]
    io = Copies(sems)
    gather_pieces(y_ref[0], z_ref[0], (p0, p1, p2, p3), whole)
    copies = [write_row(io, whole, row_b, row_out, k)]
    feat = row_b.shape[1]
    col_b[...] = whole[feat : 2 * feat].astype(F32)
    copies.append(io.start(col_b, col_out.at[k // 2]))
    for copy in copies:
        copy.wait()


def final_skip_body(k, n_alias, y_ref, z_ref, p0, p1, p2, p3, *rest):
    row_out, skip_out, whole, row_b, col_b, sems = rest[n_alias:]
    io = Copies(sems)
    gather_pieces(y_ref[0], z_ref[0], (p0, p1, p2, p3), whole)
    copies = [write_row(io, whole, row_b, row_out, k)]
    feat = row_b.shape[1]
    col_b[...] = whole[feat : 2 * feat].astype(F32)
    copies.append(io.start(col_b, skip_out.at[0:feat]))
    for copy in copies:
        copy.wait()


def final_low_body(n_alias, y_ref, z_ref, p0, p1, p2, p3, *rest):
    row_out, skip_out, first, bcol, brow, share, whole, row_b, tail_b, sems = rest[n_alias:]
    io = Copies(sems)
    gather_pieces(y_ref[0], z_ref[0], (p0, p1, p2, p3), whole)
    copies = [write_row(io, whole, row_b, row_out, 0)]
    feat = row_b.shape[1]
    width = whole.shape[1]
    depth = first.shape[0]
    half = share.shape[0]
    share[...] = whole[feat : feat + half]
    tail_b[...] = whole[feat + half :].astype(F32)
    copies.append(io.start(tail_b.at[depth : 2 * depth], skip_out.at[feat : feat + depth]))
    first[...] = tail_b[0:depth]
    bcol[...] = tail_b[2 * depth : 2 * depth + 4]
    blocks = feat // width
    for j in range(4):
        for n in range(blocks):
            at = EXTRA + j * blocks + n
            brow[j : j + 1, n * width : (n + 1) * width] = tail_b[at : at + 1]
    for copy in copies:
        copy.wait()


def unpack_body(i_ref, a, b, g_density, g_bottle, gb_bottle, g_view, gb_view, g_rgb, gb_rgb, g_first, g_rest, gb_prop, g_wpd, packed, sems):
    merge_body(i_ref, a, b, packed)
    feat, width = g_bottle.shape
    vw = g_view.shape[1]
    g_bottle[...] = packed[0:feat].astype(F32)
    g_rest[...] = packed[feat : feat + 3 * width].reshape(3, width, width).astype(F32)
    first_at = feat + 3 * width
    view_at = first_at + g_first.shape[0]
    g_first[...] = packed[first_at:view_at].astype(F32)
    wide = packed[view_at : view_at + 144].astype(F32)
    g_view[0:144] = wide[:, 0:vw]
    g_view[144 : g_view.shape[0]] = wide[0 : g_view.shape[0] - 144, vw : 2 * vw]
    small = packed[view_at + 144 : view_at + 144 + SMALL].astype(F32)
    for n in range(feat // width):
        g_density[:, n * width : (n + 1) * width] = small[n : n + 1, :]
    gb_bottle[...] = small[4:5, :]
    gb_view[...] = small[5:6, 0:vw]
    gb_rgb[...] = small[5:6, vw : vw + 3]
    g_rgb[...] = small[6:9, 0:vw]
    gb_prop[...] = small[9:13, :]
    g_wpd[...] = small[13:14, :]


def ray_masks(count, samples):
    row = lax.broadcasted_iota(jnp.int32, (count, count), 0)
    col = lax.broadcasted_iota(jnp.int32, (count, count), 1)
    same = (row // samples) == (col // samples)
    return row, col, same


def exclusive_sum(depth, samples):
    row, col, same = ray_masks(depth.shape[1], samples)
    mask = jnp.where(same & (row < col), 1.0, 0.0)
    return dot_exact(depth, mask)


def later_sum(carried, samples):
    row, col, same = ray_masks(carried.shape[1], samples)
    mask = jnp.where(same & (row > col), 1.0, 0.0)
    return dot_exact(carried, mask)


def pad_rows(value, rows):
    return jnp.concatenate([value, jnp.zeros((rows - value.shape[0], value.shape[1]), value.dtype)], 0)


def row(ref):
    return ref[...].astype(F32)[None, :]


def spread(value, count):
    rays, samples = value.shape
    lane = lax.broadcasted_iota(jnp.int32, (samples, count), 1) % samples
    pick = jnp.where(lane == lax.broadcasted_iota(jnp.int32, (samples, count), 0), 1.0, 0.0)
    wide = dot_exact(value, pick)
    ray = lax.broadcasted_iota(jnp.int32, (rays, count), 1) // samples
    return jnp.sum(jnp.where(ray == lax.broadcasted_iota(jnp.int32, (rays, count), 0), wide, 0.0), axis=0, keepdims=True)


def heads_body(samples, top_ref, counts, w_density, w_bottle, b_bottle, w_view, b_view, w_rgb3, b_rgb, view_enc, deltas, d_ref, slope_row, colour_ref, gview_ref, gr_ref, weights_ref, gwb_ref, gwv_ref, small_ref):
    top = top_ref[...]
    count = top.shape[0]
    rays = count // samples
    venc = view_enc.shape[1]
    vw = w_view.shape[1]
    w_view_b = w_view.at[0 : w_bottle.shape[1]]
    w_view_v = w_view.at[w_bottle.shape[1] : w_view.shape[0]]
    w8 = pad_rows(row(w_density), 8).astype(BF)
    w_rgb = pad_rows(w_rgb3[...].astype(F32), 8).astype(BF)
    deltas = spread(deltas[...], count)
    raw = dot_nt(w8, top)[0:1]
    sigma = softplus(raw - 1.0)
    bottle = (dot(top, w_bottle[...]) + row(b_bottle)).astype(BF)
    view_rows = jnp.concatenate([jnp.broadcast_to(view_enc[r : r + 1, :].astype(F32), (samples, venc)) for r in range(rays)], 0).astype(BF)
    view_pre = dot(bottle, w_view_b[...]) + dot(view_rows, w_view_v[...]) + row(b_view)
    view_act, view_slope = silu_pair(view_pre)
    lane3 = lax.broadcasted_iota(jnp.int32, (3, 3), 0) == lax.broadcasted_iota(jnp.int32, (3, 3), 1)
    rgb_bias = jnp.sum(jnp.where(lane3, row(b_rgb), 0.0), axis=1, keepdims=True)
    rgb = jax.nn.sigmoid(dot_nt(w_rgb, view_act)[0:3] + rgb_bias)
    place = lax.broadcasted_iota(jnp.int32, (1, count), 1)
    limit = jnp.zeros((1, count), jnp.int32)
    for r in range(rays):
        limit = jnp.where(place // samples == r, counts[r], limit)
    live = place % samples < limit
    depth = jnp.where(live, sigma * deltas, 0.0)
    before = exclusive_sum(depth, samples)
    trans = jnp.exp(-before)
    weights = one_minus_exp(depth) * trans
    weights_ref[...] = weights
    pick = jnp.where(
        lax.broadcasted_iota(jnp.int32, (count, rays), 0) // samples == lax.broadcasted_iota(jnp.int32, (count, rays), 1), 1.0, 0.0
    )
    colour_ref[...] = dot_exact(weights * rgb, pick)
    d = dot_exact(d_ref[...], pick, (((1,), (1,)), ((), ())))
    grad_weights = jnp.sum(d * rgb, axis=0, keepdims=True)
    grad_rgb = (d * weights * rgb * (1.0 - rgb)).astype(BF)
    later = later_sum(grad_weights * weights, samples)
    grad_depth = grad_weights * jnp.exp(-depth) * trans - later
    grad_raw = (jnp.where(live, grad_depth * deltas, 0.0) * jax.nn.sigmoid(raw - 1.0)).astype(BF)
    grad_rgb8 = pad_rows(grad_rgb.astype(F32), 8).astype(BF)
    grad_raw8 = pad_rows(grad_raw.astype(F32), 8).astype(BF)
    grad_view_act = dot_tn(grad_rgb8, w_rgb)
    gvp = (grad_view_act * view_slope).astype(BF)
    g_bias_view = jnp.sum(gvp.astype(F32), axis=0, keepdims=True)
    grad_input = dot_nt(gvp, w_view_b[...])
    grad_bottle = grad_input.astype(BF)
    gview = dot_nt(gvp, w_view_v[...])
    gview_ref[...] = jnp.concatenate(
        [jnp.sum(gview[r * samples : (r + 1) * samples], axis=0, keepdims=True) for r in range(rays)], 0
    )
    gr_ref[...] = ((dot_nt(grad_bottle, w_bottle[...]) + dot_tn(grad_raw8, w8)) * slope_row[...]).astype(BF)
    gwb_ref[...] = dot_tn(top, grad_bottle).astype(BF)
    gwv = jnp.concatenate([dot_tn(bottle, gvp), pad_rows(dot_tn(view_rows, gvp), 32)], 0)
    half = gwv.shape[0] // 2
    gwv_ref[:, 0:vw] = gwv[0:half].astype(BF)
    gwv_ref[:, vw : 2 * vw] = gwv[half : 2 * half].astype(BF)
    width = small_ref.shape[1]
    small_ref[...] = jnp.zeros_like(small_ref)
    gwd = dot(grad_raw8, top)[0:1]
    for n in range(top.shape[1] // width):
        small_ref[n : n + 1, :] = gwd[:, n * width : (n + 1) * width]
    small_ref[4:5, :] = jnp.sum(grad_bottle.astype(F32), axis=0, keepdims=True)
    small_ref[5:6, 0:vw] = g_bias_view
    small_ref[6:9, 0:vw] = dot(grad_rgb8, view_act)[0:3]
    small_ref[5:6, vw : vw + 8] = dot_nt(jnp.ones((8, count), BF), grad_rgb8)[0:1]


def prop_forward_body(prop_in, wp_first, wp_rest, b_prop, wp_density, acts_ref, slopes_ref, raw_ref):
    current = prop_in[...]
    for j in range(4):
        weight = wp_first[...] if j == 0 else wp_rest[j - 1]
        pre = dot(current, weight) if j else dot_tn(current, weight)
        act, slope = silu_pair(pre + b_prop[j : j + 1, :].astype(F32))
        acts_ref[j] = act
        slopes_ref[j] = slope
        current = act
    raw_ref[...] = dot_nt(pad_rows(row(wp_density), 8).astype(BF), current)[0:1]


def prop_backward_body(samples, prop_in, acts, slopes, raw_ref, deltas, bounds, weights_ref, wp_first, wp_rest, wp_density, small_a, c_ref, g_bottle, g_view, gin_ref, keep, send, packed, small_ref, sems):
    io = Copies(sems)
    feat = g_bottle.shape[0]
    width = packed.shape[1]
    rest_at, first_at = feat, feat + 3 * width
    view_at = first_at + prop_in.shape[0]
    small_at = view_at + g_view.shape[0]
    packed[0:feat] = g_bottle[...]
    packed[view_at:small_at] = g_view[...]
    count = prop_in.shape[1]
    raw = raw_ref[...]
    deltas = spread(deltas[...], count)
    bounds = [spread(bounds[n].astype(F32), count) for n in range(2)]
    weights = weights_ref[...]
    depth = softplus(raw - 1.0) * deltas
    before = exclusive_sum(depth, samples)
    trans = jnp.exp(-before)
    pweights = one_minus_exp(depth) * trans
    at_row, _, same = ray_masks(count, samples)
    place = (at_row % samples).astype(F32)
    inside = jnp.where(same & (place >= bounds[0]) & (place < bounds[1]), 1.0, 0.0)
    bound = dot_exact(pweights, inside)
    excess = jnp.maximum(weights - bound, 0.0)
    grad_bound = -2.0 * excess / (weights + EPS)
    grad_pw = dot_exact(grad_bound, inside, (((1,), (1,)), ((), ())))
    later = later_sum(grad_pw * pweights, samples)
    grad_depth = grad_pw * jnp.exp(-depth) * trans - later
    grad_raw = (grad_depth * deltas * jax.nn.sigmoid(raw - 1.0)).astype(BF)
    raw8 = pad_rows(grad_raw.astype(F32), 8).astype(BF)
    wd8 = pad_rows(row(wp_density), 8).astype(BF)
    small_ref[...] = small_a[...]
    small_ref[13:14, :] = dot(raw8, acts[3])[0:1]
    grad = dot_tn(raw8, wd8)
    for j in (3, 2, 1, 0):
        gpre = (grad * slopes[j]).astype(BF)
        small_ref[9 + j : 10 + j, :] = jnp.sum(gpre.astype(F32), axis=0, keepdims=True)
        if j:
            packed[rest_at + (j - 1) * width : rest_at + j * width] = dot_tn(acts[j - 1], gpre).astype(BF)
            grad = dot_nt(gpre, wp_rest[j - 1])
        else:
            packed[first_at:view_at] = dot(prop_in[...], gpre).astype(BF)
            gin_ref[...] = dot_nt(wp_first[...], gpre)
    packed[small_at : small_at + SMALL] = small_ref[...].astype(BF)
    io.split(packed, c_ref[0], keep, send)


def swap(value, axis, bit):
    size = lax.axis_size(axis)
    return lax.ppermute(value, axis, [(i, i ^ bit) for i in range(size)])


class Order:
    def __init__(self):
        self.token = None

    def enter(self, *values):
        if self.token is None:
            return values
        return lax.optimization_barrier((*values, self.token))[:-1]

    def leave(self, value):
        self.token = value
        return value


def late_bits(start):
    bit = start
    while bit < lax.axis_size("dp"):
        yield bit
        bit *= 2


def add_here(order, mine, came, name):
    mine, came = order.enter(mine, came)
    [out] = kernel(lambda a, b, o, sems: add_body(a, b, o), name, [("w", mine), ("v", came)], [("w", mine.shape, BF)], spare=1)
    return order.leave(out)


def split_here(order, index, mine, came, name):
    mine, came = order.enter(mine, came)
    half = (mine.shape[0] // 2, *mine.shape[1:])
    keep, send = kernel(
        lambda i, a, b, k, s, sems: add_split_body(i, a, b, k, s),
        name,
        [("s", index), ("w", mine), ("v", came)],
        [("w", half, BF), ("v", half, BF)],
        spare=1,
    )
    order.leave(send)
    return keep, send


DIMS = {3: "xyz", 2: "yxz", 1: "xyz", 0: "zxy"}
PLAN = "Q P3 K P2 P1 3 P0 2 1 3 0 2 3 2 1 3 0 1 2 3 0 1 2 3 0 2 1 0 0 1 s s"
WIRES = {"x": ("mp", 2), "y": ("dp", 1), "z": ("dp", 2)}


def reduce_steps(order, name, dims, send, keep, index, finish):
    outer, inner = [d for d in dims if d != "x"]
    came = swap(send, *WIRES[dims[0]])
    yield
    if dims[0] == "x":
        keep, send = split_here(order, index[outer], keep, came, name + "_a")
        came = swap(send, *WIRES[outer])
    else:
        keep, send = split_here(order, index["second"], keep, came, name + "_a")
        came = swap(send, *WIRES["x"])
    yield
    keep, send = split_here(order, index[inner], keep, came, name + "_b")
    came = swap(send, *WIRES[inner])
    yield
    mine = add_here(order, keep, came, name + "_c")
    for bit in late_bits(4):
        came = swap(mine, "dp", bit)
        yield
        mine = add_here(order, mine, came, name + "_far")
    beside = swap(mine, *WIRES[inner])
    across = swap(mine, *WIRES[outer])
    yield
    (beside,) = order.enter(beside)
    corner = swap(beside, *WIRES[outer])
    yield
    finish((outer, inner), (mine, beside, across, corner))


def shared_steps(order, mine, x1, finish):
    came = swap(mine, "mp", 2)
    yield
    mine, came = order.enter(mine, came)
    [mine] = kernel(
        lambda i, a, b, o, sems: merge_body(i, a, b, o),
        "shared_merge",
        [("s", x1), ("v", mine), ("v", came)],
        [("v", (2 * mine.shape[0], mine.shape[1]), BF)],
        spare=1,
    )
    order.leave(mine)
    came = swap(mine, "mp", 1)
    yield
    finish(mine, came)


class Chain:
    def __init__(self, steps):
        self.steps = steps
        self.step()

    def step(self):
        next(self.steps, None)


def on_device(points_in, view_enc, deltas, counts, w_first, w_col, w_skip, w_row, b_col, b_row, w_density, w_bottle, b_bottle, w_view, b_view, w_rgb, b_rgb, prop_in, prop_deltas, bin_bounds, wp_first, wp_rest, b_prop, wp_density, d_colour):
    rows, ipe = points_in.shape
    rays, samples = deltas.shape
    feat = w_row.shape[2]
    width = w_row.shape[1]
    blocks = feat // width
    bottle = w_bottle.shape[1]
    vw = w_view.shape[1]
    venc = view_enc.shape[1]
    dp = lax.axis_index("dp")
    mp = lax.axis_index("mp")

    def scalar(value):
        return jnp.reshape(value, (1,)).astype(jnp.int32)

    one1 = jnp.ones((1,), jnp.int32)
    y1, z1, c1, x1 = scalar(dp % 2), scalar((dp // 2) % 2), scalar(mp % 2), scalar((mp // 2) % 2)
    order = Order()
    mat = (width, feat)
    tall = (feat, width)
    flat = (rows, feat)
    two = (2, rows, width)
    four = (4, rows, width)
    some = (blocks, width, width)
    many = (2 * blocks, width, width)

    message = (EXTRA + feat // 2, width)
    extra, first_half = kernel(
        pack_first_body,
        "pack_first",
        [("s", y1), ("a", w_first), ("a", w_skip), ("v", b_col), ("a", w_row)],
        [("a", (EXTRA, width), BF), ("a", message, BF)],
        [(message, BF)],
        spare=2,
    )
    order.leave(extra)
    hx = {0: swap(first_half, "mp", 2)}
    e1 = swap(extra, "mp", 1)
    pts = points_in.T
    (y1_k,) = order.enter(y1)
    hs = kernel(pack_rest_body, "pack_rest", [("s", y1_k), ("a", w_row), ("a", w_col), ("a", w_skip)], [("a", some, BF)] * 3, [(some, BF)] * 3, spare=2)
    order.leave(hs[0])
    for k in (1, 2, 3):
        hx[k] = swap(hs[k - 1], "mp", 2)
    row_s = swap(w_row, "mp", 1)
    col_s = swap(w_col, "mp", 1)
    skip_s = swap(w_skip, "mp", 1)
    pts_s = swap(pts, "mp", 1)
    own_cols = {1: w_col, 2: w_skip, 3: w_col}
    sib_cols = {1: col_s, 2: skip_s, 3: col_s}

    act02, act13, act_s, slope_col, slope_row, inputs, inputs_s, gathered = {}, {}, {}, {}, {}, {}, {}, {}

    crossed = {}

    def arrive(k):
        (hx[k],) = order.enter(hx[k])
        order.leave(hx[k])
        crossed[k] = swap(hx[k], "dp", 1), swap(hx[k], "mp", 1)

    def complete(k):
        hy, cx = crossed[k]
        (hy,) = order.enter(hy)
        order.leave(hy)
        gathered[k] = (hx[k], hy, cx, swap(hy, "mp", 1))

    arrive(0)
    args = order.enter(pts, extra, e1, hx[0], crossed[0][1])
    act02[0], act13[0], slope_col[0], bias, extras = kernel(
        first_body,
        "first_forward",
        [("v", a) for a in args[:3]] + [("a", a) for a in args[3:]],
        [("a", two, BF), ("a", two, BF), ("a", four, F32), ("v", (4, feat), F32), ("v", (4, EXTRA, width), BF)],
        [(two, BF), (two, BF), (four, F32)],
        spare=4,
    )
    order.leave(bias)
    act_s[0] = swap(act13[0], "mp", 1)
    arrive(1)

    prop_t, wp_first_k = order.enter(prop_in.T, wp_first)
    acts, slopes, prop_raw = kernel(
        lambda *refs: prop_forward_body(*refs[:-1]),
        "prop_forward",
        [("v", prop_t), ("v", wp_first_k), ("v", wp_rest), ("v", b_prop), ("v", wp_density)],
        [("v", (4, rows, bottle), BF), ("v", (4, rows, bottle), F32), ("v", (1, rows), F32)],
        spare=4,
    )
    order.leave(prop_raw)
    complete(0)
    arrive(2)
    b_row_k, a02, a13 = order.enter(b_row, act02[0], act13[0])
    up, slope_row[0] = kernel(
        row0_body,
        "row0_forward",
        [("s", y1), ("v", b_row_k), ("a", a02), ("a", a13), ("a", w_row), ("a", row_s)] + [("a", a) for a in gathered[0]],
        [("a", flat, BF), ("a", flat, F32)],
        [(two, BF), (two, BF), (mat, BF), (mat, BF), (tall, BF), (tall, BF), (flat, BF), (flat, F32)],
        spare=6,
    )
    order.leave(up)
    complete(1)
    arrive(3)
    complete(2)
    weight_bufs = [(mat, BF), (mat, BF), (tall, BF), (tall, BF), (many, BF), (many, BF)]

    def weights_of(k):
        return [("a", a) for a in (w_row, row_s, own_cols[k], sib_cols[k], *gathered[k])]

    for k in (1, 2):
        inputs[k] = up
        inputs_s[k] = swap(up, "mp", 1)
        (b_row_k,) = order.enter(b_row)
        more = [("v", pts), ("v", extras)] if k == 2 else []
        act02[k], act13[k], slope_col[k], up, slope_row[k] = kernel(
            functools.partial(pair_body, k, k == 2),
            f"pair{k}_forward",
            [("s", y1), ("v", bias), ("v", b_row_k)] + more + [("a", inputs[k])] + weights_of(k)[:4] + [("n", a) for a in gathered[k]],
            [("a", two, BF), ("a", two, BF), ("a", four, F32), ("a", flat, BF), ("a", flat, F32)],
            [(flat, BF), *weight_bufs, (two, BF), (two, BF), (four, F32), (flat, BF), (flat, F32)],
            spare=6,
        )
        order.leave(up)
        act_s[k] = swap(act13[k], "mp", 1)

    complete(3)
    inputs[3] = up
    inputs_s[3] = swap(up, "mp", 1)
    grs, gr_s, gc02, gc13, gc_s, bc, dx, brow = {}, {}, {}, {}, {}, {}, {}, {}
    heads_in = (w_density, w_bottle, b_bottle, w_view, b_view, w_rgb.T, b_rgb, view_enc, deltas, d_colour)
    (b_row_k,) = order.enter(b_row)
    got = kernel(
        functools.partial(top_body, 3, samples, len(heads_in)),
        "top",
        [("s", y1), ("s", counts), ("v", bias), ("v", b_row_k)] + [("v", a) for a in heads_in] + [("a", up), ("a", slope_row[2])] + weights_of(3)[:4] + [("n", a) for a in gathered[3]],
        [("a", two, BF), ("a", two, BF), ("a", flat, BF), ("a", two, BF), ("a", two, BF), ("a", flat, BF)]
        + [("v", (3, rays), F32), ("v", (rays, venc), F32), ("v", (1, rows), F32), ("v", (feat, bottle), BF), ("v", (144, 2 * vw), BF), ("v", (SMALL, width), F32)],
        [(flat, BF), (flat, F32), *weight_bufs, (two, BF), (two, BF), (four, F32), (flat, BF), (flat, F32), (flat, BF), (two, BF), (two, BF), (flat, BF)],
    )
    act02[3], act13[3], grs[3], gc02[3], gc13[3], grs[2], colour, grad_view, ray_weights, g_bottle, g_view, small_a = got
    order.leave(grs[2])
    act_s[3] = swap(act13[3], "mp", 1)
    gr_s[3] = swap(grs[3], "mp", 1)
    gc_s[3] = swap(gc13[3], "mp", 1)

    results, chains = {}, {}

    index = {"x": x1, "y": y1, "z": z1, "second": one1}

    def finish(k, halved, pieces):
        pieces = order.enter(*pieces)
        size = (4 * pieces[0].shape[0], width)
        ins = [("s", index[halved[0]]), ("s", index[halved[1]])] + [("v", p) for p in pieces]
        outs = [("a", (4, width, feat), F32)]
        bufs = [(size, BF), (mat, F32)]
        alias = {}

        def in_place(name, index):
            if name in results:
                alias[len(ins)] = index
                ins.append(("a", results[name]))

        in_place("row", 0)
        if k == 2:
            outs.append(("a", (feat + ipe, width), F32))
            bufs.append((tall, F32))
            in_place("skip", 1)
            got = kernel(functools.partial(final_skip_body, k, len(alias)), f"final{k}", ins, outs, bufs, alias, spare=4)
            results["skip"] = got[1]
        elif k:
            outs.append(("a", (2, feat, width), F32))
            bufs.append((tall, F32))
            in_place("col", 1)
            got = kernel(functools.partial(final_pair_body, k, len(alias)), f"final{k}", ins, outs, bufs, alias, spare=4)
            results["col"] = got[1]
        else:
            outs += [("a", (feat + ipe, width), F32), ("v", (ipe, width), F32), ("v", (4, width), F32), ("v", (4, feat), F32), ("v", (512, width), BF)]
            bufs.append(((size[0] - feat - 512, width), F32))
            in_place("skip", 1)
            got = kernel(functools.partial(final_low_body, len(alias)), f"final{k}", ins, outs, bufs, alias, spare=4)
            results["skip"] = got[1]
            results["tail"] = got[2:5]
            chains["s"] = Chain(shared_steps(order, got[5], x1, finish_shared))
        results["row"] = got[0]
        order.leave(got[0])

    def finish_shared(mine, came):
        mine, came = order.enter(mine, came)
        results["shared"] = kernel(
            unpack_body,
            "unpack",
            [("s", c1), ("v", mine), ("v", came)],
            [
                ("v", (1, feat), F32),
                ("v", (feat, bottle), F32),
                ("v", (1, bottle), F32),
                ("v", (bottle + venc, vw), F32),
                ("v", (1, vw), F32),
                ("v", (3, vw), F32),
                ("v", (1, 3), F32),
                ("v", (ipe, bottle), F32),
                ("v", (3, bottle, bottle), F32),
                ("v", (4, bottle), F32),
                ("v", (1, bottle), F32),
            ],
            [((2048, bottle), BF)],
            spare=4,
        )
        order.leave(results["shared"][0])

    def send_away(k):
        dims = DIMS[k]
        folded = dims[0] != "x"
        kind = {3: "plain", 2: "points", 1: "plain", 0: "low"}[k]
        args = [act02[k], act_s[k], grs[k], gr_s[k], gc02[k], gc_s[k]] + ([inputs[k], inputs_s[k]] if k else [])
        args = order.enter(*args)
        height = feat + 512 + 256 if kind == "low" else 2 * feat
        small = [("s", index[dims[0]])] if folded else []
        if kind == "low":
            small += [("s", x1)]
        if kind != "plain":
            small += [("v", pts), ("v", pts_s)]
        if kind == "low":
            small += [("v", keep_h), ("v", came_h)]
            small += [("v", bc[1]), ("v", bc[2]), ("v", bc[3]), ("v", dx[2]), ("v", brow[1]), ("v", brow[2]), ("v", brow[3])]
        outs = [("a" if folded else "v", (height, width), BF), ("w", (height, width), BF)]
        if kind != "low":
            outs += [("v", (2, width), F32), ("v", (blocks, width), F32)]
        if kind == "points":
            outs.append(("v", (2, ipe, width), F32))
        bufs = [(two, BF), (two, BF), (flat, BF), (flat, BF), (two, BF), (two, BF)] + ([(flat, BF), (flat, BF)] if k else [])
        out, home, *rest = kernel(
            functools.partial(products_body, kind, folded), f"products{k}", small + [("a", a) for a in args], outs, bufs + ([((height, width), BF)] * 2 if folded else []), spare=6
        )
        if rest:
            bc[k], brow[k] = rest[:2]
        if kind == "points":
            dx[k] = rest[2]
        order.leave(out)
        chains[str(k)] = Chain(reduce_steps(order, f"sum{k}", dims, out, home, index, functools.partial(finish, k)))

    def prop_backward():
        nonlocal grad_prop_in, keep_h, came_h
        prop_args = order.enter(prop_t, acts, slopes, prop_raw, prop_deltas, bin_bounds, ray_weights, wp_first, wp_rest, wp_density, small_a, c1, g_bottle, g_view)
        grad_prop_in, keep_h, send_h = kernel(
            functools.partial(prop_backward_body, samples),
            "prop_backward",
            [("s" if n == 11 else "v", a) for n, a in enumerate(prop_args)],
            [("v", (ipe, rows), F32), ("a", (1024, bottle), BF), ("a", (1024, bottle), BF)],
            [((2048, bottle), BF), ((SMALL, width), F32)],
            spare=6,
        )
        order.leave(send_h)
        came_h = swap(send_h, "mp", 1)

    def chain_backward():
        nonlocal grad_points
        args = order.enter(grs[2], slope_col[2], slope_col[1], slope_col[0], slope_row[1], slope_row[0])
        got = kernel(
            chain_body,
            "chain",
            [("s", y1), ("v", extras)]
            + [("a", a) for a in args]
            + weights_of(2)
            + weights_of(1)
            + [("a", a) for a in (w_row, row_s, *gathered[0])],
            [("a", two, BF)] * 6 + [("a", flat, BF)] * 2 + [("v", (ipe, rows), F32)],
            [(flat, BF)] * 3 + [(four, F32)] * 3 + [(flat, F32)] * 2 + weight_bufs + weight_bufs + [(mat, BF)] * 2 + [(tall, BF)] * 2 + [(two, BF)] * 6,
            spare=6,
        )
        gc02[2], gc02[1], gc02[0], gc13[2], gc13[1], gc13[0], grs[1], grs[0], grad_points = got
        order.leave(grad_points)
        for k in (2, 1, 0):
            gr_s[k] = swap(grs[k], "mp", 1)
            gc_s[k] = swap(gc13[k], "mp", 1)

    grad_prop_in = keep_h = came_h = grad_points = None
    for item in PLAN.split():
        if item == "Q":
            prop_backward()
        elif item == "K":
            chain_backward()
        elif item[0] == "P":
            send_away(int(item[1]))
        elif item in chains:
            chains[item].step()
    for item in ("3", "2", "1", "0", "s"):
        for _ in range(16):
            chains[item].step()

    g_density, g_bottle, gb_bottle, g_view, gb_view, g_rgb, gb_rgb, g_first, g_rest, gb_prop, g_wpd = results["shared"]
    first, bcol, brow_out = results["tail"]
    return (
        colour,
        grad_points.T,
        grad_view,
        grad_prop_in.T,
        first,
        results["col"],
        results["skip"],
        results["row"],
        bcol,
        brow_out,
        g_density.reshape(feat),
        g_bottle,
        gb_bottle.reshape(bottle),
        g_view,
        gb_view.reshape(vw),
        g_rgb.T,
        gb_rgb.reshape(3),
        g_first,
        g_rest,
        gb_prop,
        g_wpd.reshape(bottle),
    )


def solution(mesh):
    both = ("dp", "mp")
    placed = (
        P(both, None),
        P(both, None),
        P(both, None),
        P(both),
        P(None, "mp"),
        P(None, None, "mp"),
        P(None, "mp"),
        P(None, "mp", None),
        P(None, "mp"),
        *([P()] * 8),
        P(both, None),
        P(both, None),
        P(None, both, None),
        P(),
        P(),
        P(),
        P(),
        P(None, both),
    )
    return jax.shard_map(
        on_device,
        mesh=mesh,
        in_specs=placed,
        out_specs=(
            P(None, both),
            P(both, None),
            P(both, None),
            P(both, None),
            P(None, "mp"),
            P(None, None, "mp"),
            P(None, "mp"),
            P(None, "mp", None),
            P(None, "mp"),
            *([P()] * 12),
        ),
        check_vma=False,
    )
```
